32 devices in a mesh: dp: 8 (over z, x), fsdp: 4 (over y, core).
Axes of the slice: x: 2, y: 2, z: 4, core: 2. Of those that a mesh axis runs over, the one named last changes fastest.
Arguments:
- inputs: bfloat16 [32, 256, 2048], P(('dp', 'fsdp')), may hold values from -6 to 6
- lengths: int32 [32], P(('dp', 'fsdp')), may hold values from 1 to 256, 5120 in all
- weight_one: bfloat16 [2048, 6144], P(('dp', 'fsdp')), may hold values from -0.125 to 0.125
- forget_peep_one: bfloat16 [2048], P(('dp', 'fsdp')), may hold values from -1 to 1
- reset_peep_one: bfloat16 [2048], P(('dp', 'fsdp')), may hold values from -1 to 1
- forget_bias_one: bfloat16 [2048], P(('dp', 'fsdp')), may hold values from 0 to 3
- reset_bias_one: bfloat16 [2048], P(('dp', 'fsdp')), may hold values from -1 to 1
- norm_gain_one: bfloat16 [2048], P(('dp', 'fsdp')), may hold values from 0.099609375 to 1.8984375
- norm_bias_one: bfloat16 [2048], P(('dp', 'fsdp')), may hold values from -3 to 3
- weight_two: bfloat16 [2048, 6144], P(('dp', 'fsdp')), may hold values from -0.125 to 0.125
- forget_peep_two: bfloat16 [2048], P(('dp', 'fsdp')), may hold values from -1 to 1
- reset_peep_two: bfloat16 [2048], P(('dp', 'fsdp')), may hold values from -1 to 1
- forget_bias_two: bfloat16 [2048], P(('dp', 'fsdp')), may hold values from 0 to 3
- reset_bias_two: bfloat16 [2048], P(('dp', 'fsdp')), may hold values from -1 to 1
- norm_gain_two: bfloat16 [2048], P(('dp', 'fsdp')), may hold values from 0.099609375 to 1.8984375
- norm_bias_two: bfloat16 [2048], P(('dp', 'fsdp')), may hold values from -3 to 3
- cotangent: bfloat16 [32, 256, 2048], P(('dp', 'fsdp')), may hold values from -6 to 6
Outputs:
- hidden_out: bfloat16 [32, 256, 2048], P(('dp', 'fsdp'))
- input_grad: float32 [32, 256, 2048], P(('dp', 'fsdp'))
- grad_weight_one: float32 [2048, 6144], P(('dp', 'fsdp'))
- grad_forget_peep_one: float32 [2048], P(('dp', 'fsdp'))
- grad_reset_peep_one: float32 [2048], P(('dp', 'fsdp'))
- grad_forget_bias_one: float32 [2048], P(('dp', 'fsdp'))
- grad_reset_bias_one: float32 [2048], P(('dp', 'fsdp'))
- grad_norm_gain_one: float32 [2048], P(('dp', 'fsdp'))
- grad_norm_bias_one: float32 [2048], P(('dp', 'fsdp'))
- grad_weight_two: float32 [2048, 6144], P(('dp', 'fsdp'))
- grad_forget_peep_two: float32 [2048], P(('dp', 'fsdp'))
- grad_reset_peep_two: float32 [2048], P(('dp', 'fsdp'))
- grad_forget_bias_two: float32 [2048], P(('dp', 'fsdp'))
- grad_reset_bias_two: float32 [2048], P(('dp', 'fsdp'))
- grad_norm_gain_two: float32 [2048], P(('dp', 'fsdp'))
- grad_norm_bias_two: float32 [2048], P(('dp', 'fsdp'))
The draws below stay inside these ranges and needn't reach their ends.
Inputs may be any that keep to these rules, and one draw needn't show every extreme that they name: `lengths`: one length a sequence, summing to 5120; some sequence fills all its 256 positions.
All inputs are finite; a program needn't handle non-finite values. No bound on the sum of `lengths` on one device may be relied on, other than what follows from the above.
Results may differ from the reference program's by a relative error of at most 0.0067.
Values may be sent and summed in bfloat16 or wider, within the bound.
A program may use at most 256 MiB of HBM per device.

```python
import math
import jax
import jax.numpy as jnp
import numpy as np
from jax import lax

D = 2048
SLOT = 256
SEQS = 32


def raised(values, rng, source, target, parts, factor):
    def block_of(dim):
        return (jnp.arange(values.shape[dim]) // (values.shape[dim] // parts)).reshape((-1,) + (1,) * (values.ndim - 1 - dim))

    near = jax.random.permutation(rng, parts)[block_of(target)]
    far = (block_of(target) + parts // 2) % parts
    return jnp.where((block_of(source) == near) | (block_of(source) == far), factor * values, values)


def levels(key, dims, cuts, low, largest):
    level, own = 1.0, jax.random.fold_in(key, 6)
    for position, shards_of in cuts:
        draws = jnp.exp(jax.random.uniform(jax.random.fold_in(own, position), (shards_of,), jnp.float32, low / len(cuts), largest / len(cuts)))
        level = level * jnp.repeat(draws, dims[position] // shards_of).reshape([-1 if axis == position else 1 for axis in range(len(dims))])
    return level


def split_up(number_of, total, limit, lean):
    weights = [(1 << 20) // math.isqrt(standing ** lean) + 1 for standing in range(2, number_of + 1)]
    spare, counts = total - limit - (number_of - 1), [1] * (number_of - 1)
    while spare > 0:
        movable = [i for i in range(number_of - 1) if counts[i] < limit]
        mass, remaining = sum([weights[i] for i in movable]), spare
        for i in movable:
            extra = min(limit - counts[i], max(1, remaining * weights[i] // mass), spare)
            counts[i] = counts[i] + extra
            spare = spare - extra
    return np.array([limit] + counts)


def ragged(stream_key, amount, total, reach, slope):
    if amount == 2:
        one = jax.random.randint(stream_key, (), max(1, total - reach), min(reach, total - 1) + 1)
        return jnp.stack([one, total - one])
    sizes = jnp.asarray(split_up(amount, total, reach, slope), jnp.int32)
    couples = (amount - 1) // 2
    giver, receiver = sizes[1:1 + 2 * couples:2], sizes[2:2 + 2 * couples:2]
    margin = jnp.minimum(giver - 1, reach - receiver)
    moved = jax.random.randint(jax.random.fold_in(stream_key, 1), (couples,), 0, 1 << 20) % (margin + 1)
    sizes = sizes.at[1:1 + 2 * couples:2].set(giver - moved).at[2:2 + 2 * couples:2].set(receiver + moved)
    return sizes[jax.random.permutation(jax.random.fold_in(stream_key, 2), amount)]


def gaussian(stream_key, extent, width, reach, cuts=(), kind=jnp.bfloat16):
    values = jax.random.normal(stream_key, extent, jnp.float32) * width
    if len(cuts) > 0:
        values = levels(stream_key, extent, cuts, -0.22, 0.18) * values
    return jnp.clip(values, min=-reach, max=reach).astype(kind)


def heavy_noise(rng, shape, width, bound, cuts, heavy, kind=jnp.bfloat16):
    entries = width * jax.random.normal(rng, shape, jnp.float32)
    if cuts:
        entries = entries * levels(rng, shape, cuts, -0.22, 0.18)
    return jnp.clip(raised(entries, jax.random.fold_in(rng, 3), *heavy), -bound, bound).astype(kind)


def setup_inputs(seed: int = 0) -> dict:
    streams_of = jax.random.split(jax.random.key(seed), 18)
    return {
        "inputs": heavy_noise(streams_of[0], (SEQS, SLOT, D), 1.0, 6.0, ((0, 32),), (0, 2, 32, 2.75)),
        "lengths": ragged(streams_of[1], SEQS, SEQS * SLOT * 5 // 8, SLOT, 2).astype(jnp.int32),
        "weight_one": gaussian(streams_of[2], (D, 3 * D), D ** -0.5, 0.125, ((0, 32),)),
        "forget_peep_one": jnp.clip(jax.random.uniform(streams_of[3], (D,), jnp.float32, -1.0, 1.0) * levels(streams_of[3], (D,), ((0, 32),), -0.4, 0.0), -1.0, 1.0).astype(jnp.bfloat16),
        "reset_peep_one": jnp.clip(jax.random.uniform(streams_of[4], (D,), jnp.float32, -1.0, 1.0) * levels(streams_of[4], (D,), ((0, 32),), -0.4, 0.0), -1.0, 1.0).astype(jnp.bfloat16),
        "forget_bias_one": jnp.clip(3.0 * jax.random.uniform(streams_of[5], (D,), jnp.float32) ** levels(streams_of[5], (D,), ((0, 32),), -0.2, 0.2), 0.0, 3.0).astype(jnp.bfloat16),
        "reset_bias_one": jnp.clip(jax.random.uniform(streams_of[6], (D,), jnp.float32, -1.0, 1.0) * levels(streams_of[6], (D,), ((0, 32),), -0.4, 0.0), -1.0, 1.0).astype(jnp.bfloat16),
        "norm_gain_one": jnp.clip(1.0 + 0.18 * jax.random.normal(streams_of[7], (D,), jnp.float32), 0.099609375, 1.8984375).astype(jnp.bfloat16),
        "norm_bias_one": gaussian(streams_of[8], (D,), 0.5, 3.0, ((0, 32),)),
        "weight_two": gaussian(streams_of[9], (D, 3 * D), D ** -0.5, 0.125, ((0, 32),)),
        "forget_peep_two": jnp.clip(jax.random.uniform(streams_of[10], (D,), jnp.float32, -1.0, 1.0) * levels(streams_of[10], (D,), ((0, 32),), -0.4, 0.0), -1.0, 1.0).astype(jnp.bfloat16),
        "reset_peep_two": jnp.clip(jax.random.uniform(streams_of[11], (D,), jnp.float32, -1.0, 1.0) * levels(streams_of[11], (D,), ((0, 32),), -0.4, 0.0), -1.0, 1.0).astype(jnp.bfloat16),
        "forget_bias_two": jnp.clip(3.0 * jax.random.uniform(streams_of[12], (D,), jnp.float32) ** levels(streams_of[12], (D,), ((0, 32),), -0.2, 0.2), 0.0, 3.0).astype(jnp.bfloat16),
        "reset_bias_two": jnp.clip(jax.random.uniform(streams_of[13], (D,), jnp.float32, -1.0, 1.0) * levels(streams_of[13], (D,), ((0, 32),), -0.4, 0.0), -1.0, 1.0).astype(jnp.bfloat16),
        "norm_gain_two": jnp.clip(1.0 + 0.18 * jax.random.normal(streams_of[14], (D,), jnp.float32), 0.099609375, 1.8984375).astype(jnp.bfloat16),
        "norm_bias_two": gaussian(streams_of[15], (D,), 0.5, 3.0, ((0, 32),)),
        "cotangent": gaussian(streams_of[16], (SEQS, SLOT, D), 1.0, 6.0, ((0, 32),)),
    }


@jax.custom_vjp
def low(v):
    return lax.optimization_barrier(v.astype(jnp.bfloat16)).astype(jnp.float32)

@jax.custom_vjp
def low_back(v):
    return v

def low_keep(v):
    return (low(v), None)

def low_pass(kept, grad):
    return (grad,)

def back_keep(v):
    return (v, None)

def back_low(kept, grad):
    return (low(grad),)
low.defvjp(low_keep, low_pass)
low_back.defvjp(back_keep, back_low)
EPSILON = 1e-05

def norm_layer(residual, norm_gain, norm_shift):
    center = residual - lax.optimization_barrier(jnp.mean(residual, axis=-1, keepdims=True))
    variance = lax.optimization_barrier(jnp.mean(jnp.square(center), axis=-1, keepdims=True))
    return center * lax.rsqrt(variance + EPSILON) * norm_gain + norm_shift

def sru_layer(residual, live_mask, params):
    weight, peep_forget, peep_reset, bias_forget, bias_reset, norm_gain, norm_shift = params
    seq_count, step_count, feature_count = residual.shape
    lowered = low(norm_layer(residual, norm_gain, norm_shift))
    projected = jnp.dot(lowered.reshape(seq_count * step_count, feature_count), weight, precision=lax.Precision.HIGHEST, preferred_element_type=jnp.float32)
    projected = low_back(projected).reshape(seq_count, step_count, 3 * feature_count)

    def advance(carried, slices):
        proj_now, resid_now, mask_now = slices
        candidate = proj_now[:, :feature_count]
        forget_gate = jax.nn.sigmoid(proj_now[:, feature_count:2 * feature_count] + peep_forget * carried + bias_forget)
        reset_gate = jax.nn.sigmoid(proj_now[:, 2 * feature_count:] + peep_reset * carried + bias_reset)
        updated = forget_gate * carried + (1.0 - forget_gate) * candidate
        held_state = mask_now * updated + (1.0 - mask_now) * carried
        output = mask_now * (reset_gate * held_state + (1.0 - reset_gate) * resid_now)
        return (held_state, output)
    initial = jnp.zeros((seq_count, feature_count), jnp.float32)
    final_state, outputs = lax.scan(advance, initial, (jnp.swapaxes(projected, 0, 1), jnp.swapaxes(residual, 0, 1), jnp.swapaxes(live_mask, 0, 1)))
    return jnp.swapaxes(outputs, 0, 1)

def layer_pair(group_in, group_live, params_one, params_two):
    return sru_layer(sru_layer(group_in, group_live, params_one), group_live, params_two)

def reference(inputs, lengths, weight_one, forget_peep_one, reset_peep_one, forget_bias_one, reset_bias_one, norm_gain_one, norm_bias_one, weight_two, forget_peep_two, reset_peep_two, forget_bias_two, reset_bias_two, norm_gain_two, norm_bias_two, cotangent):
    params_one = tuple((tensor.astype(jnp.float32) for tensor in (weight_one, forget_peep_one, reset_peep_one, forget_bias_one, reset_bias_one, norm_gain_one, norm_bias_one)))
    params_two = tuple((tensor.astype(jnp.float32) for tensor in (weight_two, forget_peep_two, reset_peep_two, forget_bias_two, reset_bias_two, norm_gain_two, norm_bias_two)))
    positions = jnp.arange(SLOT, dtype=jnp.int32)
    live_mask = (positions[None, :] < lengths[:, None]).astype(jnp.float32)[:, :, None]
    group_size = math.gcd(SEQS, 8)
    group_count = SEQS // group_size
    checked = jax.checkpoint(layer_pair)

    def forward(residual, first, second):
        grouped = residual.reshape(group_count, group_size, SLOT, D)
        live_grouped = live_mask.reshape(group_count, group_size, SLOT, 1)
        outputs = lax.map(lambda pieces: checked(pieces[0], pieces[1], first, second), (grouped, live_grouped))
        return outputs.reshape(SEQS, SLOT, D)
    hidden, pullback = jax.vjp(forward, inputs.astype(jnp.float32), params_one, params_two)
    input_grad, grads_one, grads_two = pullback(cotangent.astype(jnp.float32))
    return (hidden.astype(jnp.bfloat16), input_grad, grads_one[0], grads_one[1], grads_one[2], grads_one[3], grads_one[4], grads_one[5], grads_one[6], grads_two[0], grads_two[1], grads_two[2], grads_two[3], grads_two[4], grads_two[5], grads_two[6])
```

```python
import functools
from collections import namedtuple

import jax
import jax.numpy as jnp
from jax import lax
from jax.experimental import pallas as pl
from jax.experimental.pallas import tpu as pltpu
from jax.sharding import PartitionSpec as P

MESH = pl.DeviceIdType.MESH
HBM = pl.BlockSpec(memory_space=pltpu.HBM)
VM = pl.BlockSpec(memory_space=pltpu.VMEM)
DMA = pltpu.SemaphoreType.DMA
BF = jnp.bfloat16
F32 = jnp.float32
EPSILON = 1e-05
PAD = 8
VMEM_CAP = 60 << 20

Cfg = namedtuple("Cfg", ("DP", "FS", "N", "A", "ZL", "X", "F", "C", "S", "T", "TP", "D", "FW", "L", "R", "M", "PER"))


def make_cfg(mesh, steps, width):
    dp, fs = mesh.shape["dp"], mesh.shape["fsdp"]
    zl = 2 if fs < 8 and dp % 4 == 0 else 1
    x = 2 if (dp // zl) % 2 == 0 else 1
    a = dp // (zl * x)
    f = zl * fs
    fw = width // f
    rows = width // (dp * fs)
    return Cfg(dp, fs, dp * fs, a, zl, x, f, f // 2, f, steps, steps + PAD, width, fw, fw // 128, rows, f * steps, 128 // rows)


def coords(cfg):
    dp, f = lax.axis_index("dp"), lax.axis_index("fsdp")
    b, zl, a = dp % cfg.X, (dp // cfg.X) % cfg.ZL, dp // (cfg.X * cfg.ZL)
    return a, zl, b, f


def device(cfg, a, zl, b, f):
    return ((a * cfg.ZL + zl) * cfg.X + b, f)


def flat(cfg, a, zl, b, f):
    return ((a * cfg.ZL + zl) * cfg.X + b) * cfg.FS + f


def member(cfg, a, b, s):
    return device(cfg, a, s // cfg.FS, b, s % cfg.FS)


def remote(src, dst, send, recv, where):
    return pltpu.make_async_remote_copy(src_ref=src, dst_ref=dst, send_sem=send, recv_sem=recv, device_id=where, device_id_type=MESH)


def greet(targets):
    barrier = pltpu.get_barrier_semaphore()
    for where in targets:
        pl.semaphore_signal(barrier, inc=1, device_id=where, device_id_type=MESH)
    pl.semaphore_wait(barrier, len(targets))


def greet_all(cfg, me):
    barrier = pltpu.get_barrier_semaphore()

    def one(k, _):
        m = (me + k) % cfg.N
        pl.semaphore_signal(barrier, inc=1, device_id=(m // cfg.FS, m % cfg.FS), device_id_type=MESH)
        return 0

    lax.fori_loop(1, cfg.N, one, 0)
    pl.semaphore_wait(barrier, cfg.N - 1)


def group_targets(cfg, a, b, s):
    return [member(cfg, a, b, (s + k) % cfg.F) for k in range(1, cfg.F)]


class Gather:
    def __init__(self, cfg, co, src, slot, send, recv, mate_send, mate_recv):
        self.cfg, self.co, self.src, self.slot = cfg, co, src, slot
        self.sems = send, recv, mate_send, mate_recv
        a, zl, b, f = co
        self.s = zl * cfg.FS + f
        self.cell, self.core = self.s // 2, self.s % 2

    def far(self, k):
        cfg, (a, zl, b, f) = self.cfg, self.co
        send, recv, _, _ = self.sems
        to = member(cfg, a, b, ((self.cell + k) % cfg.C) * 2 + self.core)
        return remote(self.src, self.slot(self.s), send.at[k], recv.at[k], to)

    def near(self, k):
        cfg, (a, zl, b, f) = self.cfg, self.co
        _, _, send, recv = self.sems
        origin = ((self.cell - k + cfg.C) % cfg.C) * 2 + self.core
        src = self.src if k == 0 else self.slot(origin)
        return remote(src, self.slot(origin), send.at[k], recv.at[k], member(cfg, a, b, self.cell * 2 + 1 - self.core))

    def start(self):
        for k in range(1, self.cfg.C):
            self.far(k).start()
        self.near(0).start()

    def finish(self):
        for k in range(1, self.cfg.C):
            self.far(k).wait_recv()
            self.near(k).start()
        for k in range(1, self.cfg.C):
            self.far(k).wait_send()
        for k in range(self.cfg.C):
            self.near(k).wait()


class Exchange:
    def __init__(self, cfg, co, src, dst, send, recv):
        self.cfg, self.co, self.src, self.dst, self.send, self.recv = cfg, co, src, dst, send, recv
        self.s = co[1] * cfg.FS + co[3]

    def copy(self, k):
        a, zl, b, f = self.co
        to = (self.s + k) % self.cfg.F
        return remote(self.src(to), self.dst(self.s), self.send.at[k], self.recv.at[k], member(self.cfg, a, b, to))

    def start(self):
        for k in range(1, self.cfg.F):
            self.copy(k).start()

    def finish(self):
        for k in range(1, self.cfg.F):
            self.copy(k).wait()


class WeightGather:
    def __init__(self, cfg, co, w, full, own, send, recv, asend, arecv, bsend, brecv):
        self.cfg, self.co, self.w, self.full = cfg, co, w, full
        self.own, self.send, self.recv = own, send, recv
        self.asend, self.arecv, self.bsend, self.brecv = asend, arecv, bsend, brecv
        self.s = co[1] * cfg.FS + co[3]

    def pieces(self, k):
        cfg, (a, zl, b, f) = self.cfg, self.co
        to = (self.s + k) % cfg.F
        me = flat(cfg, a, zl, b, f)
        for c in range(3):
            src = self.w.at[:, pl.ds(pl.multiple_of(c * cfg.D + to * cfg.FW, 128), cfg.FW)]
            dst = self.full.at[me, :, pl.ds(c * cfg.FW, cfg.FW)]
            if k == 0:
                yield pltpu.make_async_copy(src, dst, self.own.at[c])
            else:
                yield remote(src, dst, self.send.at[k, c], self.recv.at[k, c], member(cfg, a, b, to))

    def start(self):
        for k in range(self.cfg.F):
            for copy in self.pieces(k):
                copy.start()

    def middle(self):
        for k in range(self.cfg.F):
            for copy in self.pieces(k):
                copy.wait()

    def rows_of(self, a, zl, b):
        return self.full.at[pl.ds(flat(self.cfg, a, zl, b, 0), self.cfg.FS)]

    def to_a(self, k, zl):
        cfg, (a, _, b, f) = self.cfg, self.co
        rows = self.rows_of(a, zl, b)
        return remote(rows, rows, self.asend.at[k, zl], self.arecv.at[k, zl], device(cfg, (a + k) % cfg.A, self.co[1], b, f))

    def to_b(self, k, ka, zl):
        cfg, (a, _, b, f) = self.cfg, self.co
        rows = self.rows_of((a - ka + cfg.A) % cfg.A, zl, b)
        return remote(rows, rows, self.bsend.at[k, ka, zl], self.brecv.at[k, ka, zl], device(cfg, a, self.co[1], (b + k) % cfg.X, f))

    def start_out(self):
        cfg = self.cfg
        for zl in range(cfg.ZL):
            for k in range(1, cfg.A):
                self.to_a(k, zl).start()
            for k in range(1, cfg.X):
                self.to_b(k, 0, zl).start()

    def finish_out(self):
        cfg = self.cfg
        for zl in range(cfg.ZL):
            for ka in range(1, cfg.A):
                self.to_a(ka, zl).wait_recv()
                for k in range(1, cfg.X):
                    self.to_b(k, ka, zl).start()
        for zl in range(cfg.ZL):
            for ka in range(cfg.A):
                for k in range(1, cfg.X):
                    self.to_b(k, ka, zl).wait()
            for ka in range(1, cfg.A):
                self.to_a(ka, zl).wait_send()


def t_targets(cfg, co):
    a, zl, b, f = co
    out = [device(cfg, (a + k) % cfg.A, zl, b, f) for k in range(1, cfg.A)]
    return out + [device(cfg, a, zl, (b + k) % cfg.X, f) for k in range(1, cfg.X)]


def weight_sems(cfg):
    return [DMA((3,)), DMA((cfg.F, 3)), DMA((cfg.F, 3))] + [DMA((cfg.A, cfg.ZL))] * 2 + [DMA((cfg.X, cfg.A, cfg.ZL))] * 2


def start_kernel(cfg, x, cot, w1, w2, small, xg, cg, f1, f2, sg, own_sem, small_send, small_recv, gs, gr, gms, gmr, cs, cr, *wsems):
    co = coords(cfg)
    a, zl, b, f = co
    s, me = zl * cfg.FS + f, flat(cfg, *co)
    greet_all(cfg, me)
    weights = [WeightGather(cfg, co, w1, f1, *wsems[:7]), WeightGather(cfg, co, w2, f2, *wsems[7:])]
    weights[0].start()
    gather = Gather(cfg, co, x, lambda i: xg.at[i], gs, gr, gms, gmr)
    gather.start()

    def each(k, _):
        m = (me + k) % cfg.N
        remote(small, sg.at[me], small_send, small_recv, (m // cfg.FS, m % cfg.FS)).start()
        return 0

    lax.fori_loop(1, cfg.N, each, 0)
    weights[1].start()
    exchange = Exchange(cfg, co, lambda i: cot.at[:, pl.ds(pl.multiple_of(i * cfg.FW, 128), cfg.FW)], lambda i: cg.at[i], cs, cr)
    exchange.start()
    locals_ = [
        pltpu.make_async_copy(x, xg.at[s], own_sem.at[0]),
        pltpu.make_async_copy(cot.at[:, pl.ds(pl.multiple_of(s * cfg.FW, 128), cfg.FW)], cg.at[s], own_sem.at[1]),
        pltpu.make_async_copy(small, sg.at[me], own_sem.at[2]),
    ]
    for copy in locals_:
        copy.start()
    weights[0].middle()
    weights[0].start_out()
    weights[1].middle()
    gather.finish()
    weights[0].finish_out()
    weights[1].start_out()
    exchange.finish()
    weights[1].finish_out()
    everyone = sg.at[pl.ds(0, cfg.N - 1)]
    pltpu.make_async_copy(everyone, everyone, small_recv).wait()
    pltpu.make_async_copy(everyone, everyone, small_send).wait()
    for copy in locals_:
        copy.wait()


def start(cfg, x, cot, w1, w2, small):
    full = jax.ShapeDtypeStruct((cfg.N, cfg.R, 3 * cfg.FW), BF)
    return pl.pallas_call(
        functools.partial(start_kernel, cfg),
        name="start",
        out_shape=(
            jax.ShapeDtypeStruct((cfg.S, cfg.T, cfg.D), BF),
            jax.ShapeDtypeStruct((cfg.S, cfg.T, cfg.FW), BF),
            full,
            full,
            jax.ShapeDtypeStruct((cfg.N, 16, 128), BF),
        ),
        in_specs=[HBM] * 5,
        out_specs=[HBM] * 5,
        scratch_shapes=[DMA((3,)), DMA(()), DMA(())] + [DMA((cfg.C,))] * 4 + [DMA((cfg.F,))] * 2 + weight_sems(cfg) * 2,
        compiler_params=pltpu.CompilerParams(collective_id=0, has_side_effects=True),
    )(x, cot, w1, w2, small)


def rows(cfg, ref, t, first, count):
    return jnp.concatenate([ref[first + i, pl.ds(t, cfg.S, stride=cfg.TP), :] for i in range(count)], axis=1)


def put(cfg, ref, t, value, first=0):
    for i in range(value.shape[1] // 128):
        ref[first + i, pl.ds(t, cfg.S, stride=cfg.TP), :] = value[:, 128 * i : 128 * i + 128]


def wide(cfg, ref, row):
    return jnp.broadcast_to(ref[row : row + 1, :], (cfg.S, cfg.FW))


def scan_forward(cfg, proj, inp, vec, base, lens, hid, states, tf_ref, tr_ref):
    half_pf, half_pr = 0.5 * wide(cfg, vec, base), 0.5 * wide(cfg, vec, base + 1)
    half_bf, half_br = 0.5 * wide(cfg, vec, base + 2), 0.5 * wide(cfg, vec, base + 3)
    live = jnp.broadcast_to(lens[:, 0:1], (cfg.S, cfg.FW))

    def step(t, c):
        u, p, q = (rows(cfg, proj, t, i * cfg.L, cfg.L) for i in range(3))
        here = rows(cfg, inp, t, 0, cfg.L)
        p, q, hu, hc = 0.5 * p + half_bf, 0.5 * q + half_br, 0.5 * u, 0.5 * c
        tf = jnp.tanh(p + half_pf * c)
        tr = jnp.tanh(q + half_pr * c)
        new = (hc + hu) + tf * (hc - hu)
        out = jnp.where(t < live, 0.5 * (here + new) + 0.5 * tr * (new - here), 0.0)
        put(cfg, hid, t, out)
        put(cfg, states, t, new)
        put(cfg, tf_ref, t, tf)
        put(cfg, tr_ref, t, tr)
        return new

    lax.fori_loop(0, cfg.T, step, jnp.zeros((cfg.S, cfg.FW), F32), unroll=4)


def scan_backward(cfg, cand, inp, vec, base, lens, states, tf_ref, tr_ref, grad, grads, direct, sums):
    pf, pr = wide(cfg, vec, base), wide(cfg, vec, base + 1)
    live = jnp.broadcast_to(lens[:, 0:1], (cfg.S, cfg.FW))

    def step(i, carry):
        e, s0, s1, s2, s3 = carry
        t = cfg.T - 1 - i
        u, here, g = rows(cfg, cand, t, 0, cfg.L), rows(cfg, inp, t, 0, cfg.L), rows(cfg, grad, t, 0, cfg.L)
        f = 0.5 * rows(cfg, tf_ref, t, 0, cfg.L) + 0.5
        r = 0.5 * rows(cfg, tr_ref, t, 0, cfg.L) + 0.5
        new = rows(cfg, states, t, 0, cfg.L)
        c = jnp.where(t > 0, rows(cfg, states, jnp.maximum(t - 1, 0), 0, cfg.L), 0.0)
        k = jnp.where(t < live, g, 0.0)
        kr = k * r
        rest = 1.0 - f
        w = (c - u) * (f * rest)
        dq = (k - kr) * (new - here) * r
        s = e + kr
        dp = s * w
        put(cfg, grads, t, s * rest, 0)
        put(cfg, grads, t, dp, cfg.L)
        put(cfg, grads, t, dq, 2 * cfg.L)
        put(cfg, direct, t, k - kr)
        e = s * (f + w * pf) + dq * pr
        return e, s0 + dp * c, s1 + dq * c, s2 + dp, s3 + dq

    zero = jnp.zeros((cfg.S, cfg.FW), F32)
    out = lax.fori_loop(0, cfg.T, step, (zero,) * 5, unroll=2)
    for i in range(4):
        sums[i : i + 1, :] = jnp.sum(out[1 + i], axis=0, keepdims=True)


def normalize(x):
    center = x - jnp.mean(x, axis=-1, keepdims=True)
    inverse = lax.rsqrt(jnp.mean(center * center, axis=-1, keepdims=True) + EPSILON)
    return center * inverse, inverse


def project(cfg, z, gain, shift, w, low, proj, s):
    lowered = (z * gain + shift).astype(BF)
    low[0] = lowered
    out = jnp.dot(lowered, w[...], preferred_element_type=F32)
    base = pl.multiple_of(s * cfg.TP, 8)
    for i in range(3 * cfg.L):
        proj[i, pl.ds(base, cfg.T), :] = out[:, 128 * i : 128 * i + 128]


def seq_block(cfg, ref, i, s):
    return ref[i, pl.ds(pl.multiple_of(s * cfg.TP, 8), cfg.T), :]


def narrow(cfg, src, dst, count):
    for i in range(count):
        for s in range(cfg.S):
            dst[s * cfg.T : (s + 1) * cfg.T, 128 * i : 128 * i + 128] = src[i, s * cfg.TP : s * cfg.TP + cfg.T, :].astype(dst.dtype)


def first_kernel(cfg, x, w, vec, mine, lens, low, hid, hid_low, inp, cand, states, tf, tr, proj):
    s = pl.program_id(0)
    _, zl, _, f = coords(cfg)
    j = zl * cfg.FS + f
    data = x[0].astype(F32)
    z, _ = normalize(data)
    project(cfg, z, vec[4:5, :], vec[5:6, :], w, low, proj, s)
    own = x[0, :, pl.ds(pl.multiple_of(j * cfg.FW, 128), cfg.FW)].astype(F32)
    for i in range(cfg.L):
        inp[i, pl.ds(pl.multiple_of(s * cfg.TP, 8), cfg.T), :] = own[:, 128 * i : 128 * i + 128]

    @pl.when(s == cfg.S - 1)
    def _():
        scan_forward(cfg, proj, inp, mine, 0, lens, hid, states, tf, tr)
        narrow(cfg, hid, hid_low, cfg.L)
        for i in range(cfg.L):
            cand[i] = proj[i]


def keep(cfg, count):
    return jax.ShapeDtypeStruct((count, cfg.S * cfg.TP, 128), F32)


def const(shape):
    return pl.BlockSpec(shape, lambda i: (0,) * len(shape))


def first(cfg, x, w, vec, mine, lens):
    state = keep(cfg, cfg.L)
    spec = const(state.shape)
    return pl.pallas_call(
        functools.partial(first_kernel, cfg),
        name="first",
        grid=(cfg.S,),
        out_shape=(jax.ShapeDtypeStruct((cfg.S, cfg.T, cfg.D), BF), state, jax.ShapeDtypeStruct((cfg.M, cfg.FW), BF)) + (state,) * 5,
        in_specs=[pl.BlockSpec((1, cfg.T, cfg.D), lambda i: (i, 0, 0)), const(w.shape), const(vec.shape), const(mine.shape), const(lens.shape)],
        out_specs=[pl.BlockSpec((1, cfg.T, cfg.D), lambda i: (i, 0, 0)), spec, const((cfg.M, cfg.FW))] + [spec] * 5,
        scratch_shapes=[pltpu.VMEM((3 * cfg.L, cfg.S * cfg.TP, 128), F32)],
        compiler_params=pltpu.CompilerParams(vmem_limit_bytes=VMEM_CAP),
    )(x, w, vec, mine, lens)


def second_kernel(cfg, x, w, vec, mine, lens, inp, grad_in, low, hid_low, grads_low, part, z_own, inv, direct, sums, proj, hid, states, tf, tr, grad, grads):
    i = pl.program_id(0)
    _, zl, _, f = coords(cfg)
    j = zl * cfg.FS + f

    @pl.when(i < cfg.S)
    def _():
        z, inverse = normalize(x[0].astype(F32))
        project(cfg, z, vec[10:11, :], vec[11:12, :], w, low, proj, i)
        at = pl.ds(pl.multiple_of(i * cfg.T, 8), cfg.T)
        inv[at, :] = jnp.broadcast_to(inverse, (cfg.T, 128))
        raw = x[0, :, pl.ds(pl.multiple_of(j * cfg.FW, 128), cfg.FW)].astype(F32)
        mean = jnp.mean(x[0].astype(F32), axis=-1, keepdims=True)
        z_own[at, :] = (raw - mean) * inverse

    @pl.when(i == cfg.S - 1)
    def _():
        for s in range(cfg.S):
            g = grad_in[s].astype(F32)
            for l in range(cfg.L):
                grad[l, s * cfg.TP : s * cfg.TP + cfg.T, :] = g[:, 128 * l : 128 * l + 128]
        scan_forward(cfg, proj, inp, mine, 6, lens, hid, states, tf, tr)
        narrow(cfg, hid, hid_low, cfg.L)
        scan_backward(cfg, proj, inp, mine, 6, lens, states, tf, tr, grad, grads, direct, sums)
        narrow(cfg, grads, grads_low, 3 * cfg.L)

    @pl.when(i >= cfg.S)
    def _():
        k = i - cfg.S
        block = w[pl.ds(pl.multiple_of(k * cfg.FW, 8), cfg.FW), :]
        part[0] = lax.dot_general(grads_low[...], block, (((1,), (1,)), ((), ())), preferred_element_type=F32).astype(BF)


def second(cfg, x, w, vec, mine, lens, inp, grad_in):
    state = keep(cfg, cfg.L)
    spec = const(state.shape)
    big = pltpu.VMEM(state.shape, F32)
    last = cfg.S - 1
    one = pl.BlockSpec((1, cfg.T, cfg.D), lambda i: (jnp.minimum(i, last), 0, 0))
    return pl.pallas_call(
        functools.partial(second_kernel, cfg),
        name="second",
        grid=(cfg.S + cfg.F,),
        out_shape=(
            jax.ShapeDtypeStruct((cfg.S, cfg.T, cfg.D), BF),
            jax.ShapeDtypeStruct((cfg.M, cfg.FW), BF),
            jax.ShapeDtypeStruct((cfg.M, 3 * cfg.FW), BF),
            jax.ShapeDtypeStruct((cfg.F, cfg.M, cfg.FW), BF),
            jax.ShapeDtypeStruct((cfg.M, cfg.FW), F32),
            jax.ShapeDtypeStruct((cfg.M, 128), F32),
            state,
            jax.ShapeDtypeStruct((8, cfg.FW), F32),
        ),
        in_specs=[one, const(w.shape), const(vec.shape), const(mine.shape), const(lens.shape), spec, const(grad_in.shape)],
        out_specs=[
            one,
            const((cfg.M, cfg.FW)),
            const((cfg.M, 3 * cfg.FW)),
            pl.BlockSpec((1, cfg.M, cfg.FW), lambda i: (jnp.maximum(i - cfg.S, 0), 0, 0)),
            const((cfg.M, cfg.FW)),
            const((cfg.M, 128)),
            spec,
            const((8, cfg.FW)),
        ],
        scratch_shapes=[pltpu.VMEM((3 * cfg.L, cfg.S * cfg.TP, 128), F32)] + [big] * 5 + [pltpu.VMEM((3 * cfg.L, cfg.S * cfg.TP, 128), F32)],
        compiler_params=pltpu.CompilerParams(vmem_limit_bytes=VMEM_CAP),
    )(x, w, vec, mine, lens, inp, grad_in)


def third_kernel(cfg, w, mine, lens, inp, cand, states, tf, tr, grad, grads_low, part, direct_low, sums, grads, direct):
    s = pl.program_id(0)

    @pl.when(s == 0)
    def _():
        scan_backward(cfg, cand, inp, mine, 0, lens, states, tf, tr, grad, grads, direct, sums)
        narrow(cfg, grads, grads_low, 3 * cfg.L)
        narrow(cfg, direct, direct_low, cfg.L)

    at = pl.ds(pl.multiple_of(s * cfg.T, 8), cfg.T)
    part[0] = lax.dot_general(grads_low[at, :], w[...], (((1,), (1,)), ((), ())), preferred_element_type=F32).astype(BF)


def third(cfg, w, mine, lens, inp, cand, states, tf, tr, grad):
    state = keep(cfg, cfg.L)
    spec = const(state.shape)
    return pl.pallas_call(
        functools.partial(third_kernel, cfg),
        name="third",
        grid=(cfg.S,),
        out_shape=(
            jax.ShapeDtypeStruct((cfg.M, 3 * cfg.FW), BF),
            jax.ShapeDtypeStruct((cfg.S, cfg.T, cfg.D), BF),
            jax.ShapeDtypeStruct((cfg.M, cfg.FW), BF),
            jax.ShapeDtypeStruct((8, cfg.FW), F32),
        ),
        in_specs=[const(w.shape), const(mine.shape), const(lens.shape)] + [spec] * 6,
        out_specs=[const((cfg.M, 3 * cfg.FW)), pl.BlockSpec((1, cfg.T, cfg.D), lambda i: (i, 0, 0)), const((cfg.M, cfg.FW)), const((8, cfg.FW))],
        scratch_shapes=[pltpu.VMEM((3 * cfg.L, cfg.S * cfg.TP, 128), F32), pltpu.VMEM(state.shape, F32)],
        compiler_params=pltpu.CompilerParams(vmem_limit_bytes=VMEM_CAP),
    )(w, mine, lens, inp, cand, states, tf, tr, grad)


def gather_kernel(cfg, x, out, own, gs, gr, gms, gmr):
    co = coords(cfg)
    a, zl, b, f = co
    s = zl * cfg.FS + f
    cell, core = s // 2, s % 2
    greet([member(cfg, a, b, ((cell + k) % cfg.C) * 2 + core) for k in range(1, cfg.C)] + [member(cfg, a, b, cell * 2 + 1 - core)])
    slot = lambda i: out.at[:, pl.ds(pl.multiple_of(i * cfg.FW, 128), cfg.FW)]
    gather = Gather(cfg, co, x, slot, gs, gr, gms, gmr)
    gather.start()
    copy = pltpu.make_async_copy(x, slot(s), own)
    copy.start()
    gather.finish()
    copy.wait()


def gather_hidden(cfg, x):
    return pl.pallas_call(
        functools.partial(gather_kernel, cfg),
        name="gather_hidden",
        out_shape=jax.ShapeDtypeStruct((cfg.M, cfg.D), BF),
        in_specs=[HBM],
        out_specs=HBM,
        scratch_shapes=[DMA(())] + [DMA((cfg.C,))] * 4,
        compiler_params=pltpu.CompilerParams(collective_id=1, has_side_effects=True),
    )(x)


class Reduce:
    def __init__(self, cfg, co, part, own, mate, out, got, load, ms, mr, fs, fr):
        self.cfg, self.co, self.part, self.own, self.mate, self.out, self.got = cfg, co, part, own, mate, out, got
        self.load, self.ms, self.mr, self.fs, self.fr = load, ms, mr, fs, fr
        self.s = co[1] * cfg.FS + co[3]
        self.cell, self.core = self.s // 2, self.s % 2

    def target(self, k):
        return (self.cell + k) % self.cfg.C

    def to_mate(self, k):
        a, _, b, _ = self.co
        return remote(
            self.part.at[self.target(k) * 2 + 1 - self.core], self.mate.at[k], self.ms.at[k], self.mr.at[k],
            member(self.cfg, a, b, self.cell * 2 + 1 - self.core),
        )

    def fetch(self, k):
        return pltpu.make_async_copy(self.part.at[self.target(k) * 2 + self.core], self.own.at[k], self.load.at[k])

    def far(self, k):
        a, _, b, _ = self.co
        return remote(self.out.at[k - 1], self.got.at[k - 1], self.fs.at[k], self.fr.at[k], member(self.cfg, a, b, self.target(k) * 2 + self.core))

    def order(self):
        return list(range(1, self.cfg.C)) + [0]

    def start(self):
        for k in self.order():
            self.to_mate(k).start()
            self.fetch(k).start()

    def middle(self):
        rows_, _ = self.own.shape[1:]
        step = 256 if rows_ % 256 == 0 else rows_
        for k in self.order():
            self.to_mate(k).wait_recv()
            self.fetch(k).wait()
            if k:

                def add(i, _):
                    at = pl.ds(pl.multiple_of(i * step, 8), step)
                    self.out[k - 1, at, :] = (self.own[k, at, :].astype(F32) + self.mate[k, at, :].astype(F32)).astype(BF)
                    return 0

                lax.fori_loop(0, rows_ // step, add, 0)
                self.far(k).start()

    def finish(self):
        for k in range(1, self.cfg.C):
            self.far(k).wait()
        for k in range(self.cfg.C):
            self.to_mate(k).wait_send()

    def total(self, at):
        value = self.own[0, at, :].astype(F32) + self.mate[0, at, :].astype(F32)
        for k in range(1, self.cfg.C):
            value = value + self.got[k - 1, at, :].astype(F32)
        return value


def reduce_scratch(cfg, rows_, cols):
    return [pltpu.VMEM((cfg.C, rows_, cols), BF)] * 2 + [pltpu.VMEM((cfg.C - 1, rows_, cols), BF)] * 2 + [DMA((cfg.C,))] * 5


def middle_kernel(cfg, part, z_own, inv, direct, mine, grad, sums, ng, stats, mean, *sc):
    red_sc, (ss, sr) = sc[:9], sc[9:]
    co = coords(cfg)
    a, zl, b, f = co
    s = zl * cfg.FS + f
    greet(group_targets(cfg, a, b, s))
    red = Reduce(cfg, co, part, *red_sc)
    red.start()
    red.middle()
    red.finish()
    gain = mine[10:11, :]
    eye = (lax.broadcasted_iota(jnp.int32, (128, 128), 0) == lax.broadcasted_iota(jnp.int32, (128, 128), 1)).astype(F32)

    def first_pass(i, carry):
        s0, s1 = carry
        at = pl.ds(pl.multiple_of(i * 128, 8), 128)
        value = red.total(at)
        z = z_own[at, :]
        h = value * gain
        ng[at, :] = h
        for n, x in ((0, h), (1, h * z)):
            col = jnp.sum(x, axis=-1, keepdims=True)
            stats[s, n, pl.ds(i, 1), :] = jnp.sum(col * eye, axis=0, keepdims=True)
        return s0 + jnp.sum(value * z, axis=0, keepdims=True), s1 + jnp.sum(value, axis=0, keepdims=True)

    zero = jnp.zeros((1, cfg.FW), F32)
    s0, s1 = lax.fori_loop(0, cfg.M // 128, first_pass, (zero, zero))
    sums[0:1, :] = s0
    sums[1:2, :] = s1
    exchange = Exchange(cfg, co, lambda i: stats.at[s], lambda i: stats.at[i], ss, sr)
    exchange.start()
    exchange.finish()
    total = stats[0]
    for i in range(1, cfg.F):
        total = total + stats[i]
    mean[...] = total * (1.0 / cfg.D)

    def second_pass(i, _):
        at = pl.ds(pl.multiple_of(i * 128, 8), 128)
        m0 = jnp.sum(mean[0, pl.ds(i, 1), :] * eye, axis=-1, keepdims=True)
        m1 = jnp.sum(mean[1, pl.ds(i, 1), :] * eye, axis=-1, keepdims=True)
        value = (ng[at, :] - m0 - z_own[at, :] * m1) * inv[at, 0:1]
        per = cfg.T // 128
        to = pl.ds(pl.multiple_of((i // per) * cfg.TP + (i % per) * 128, 8), 128)
        for l in range(cfg.L):
            grad[l, to, :] = value[:, 128 * l : 128 * l + 128] + direct[l, to, :]
        return 0

    lax.fori_loop(0, cfg.M // 128, second_pass, 0)


def middle(cfg, part, z_own, inv, direct, mine):
    return pl.pallas_call(
        functools.partial(middle_kernel, cfg),
        name="middle",
        out_shape=(keep(cfg, cfg.L), jax.ShapeDtypeStruct((8, cfg.FW), F32)),
        in_specs=[HBM] + [VM] * 4,
        out_specs=[VM] * 2,
        scratch_shapes=[
            pltpu.VMEM((cfg.M, cfg.FW), F32),
            pltpu.VMEM((cfg.F, 2, cfg.M // 128, 128), F32),
            pltpu.VMEM((2, cfg.M // 128, 128), F32),
        ]
        + reduce_scratch(cfg, cfg.M, cfg.FW)
        + [DMA((cfg.F,))] * 2,
        compiler_params=pltpu.CompilerParams(collective_id=2, has_side_effects=True, vmem_limit_bytes=VMEM_CAP),
    )(part, z_own, inv, direct, mine)


def last_kernel(cfg, part, dir_low, hid_low, g1, g2, x, vec, grad, hid, b1, b2, sums, dgot, *sc):
    red_sc, sc = sc[:9], sc[9:]
    own, ds, dr, hs, hr = sc[:5]
    ts = sc[5:]
    co = coords(cfg)
    a, zl, b, f = co
    s = zl * cfg.FS + f
    barrier_to = group_targets(cfg, a, b, s)
    others = [(ka, kb) for ka in range(cfg.A) for kb in range(cfg.X) if ka or kb]
    far = lambda ka, kb: ((a + ka) % cfg.A, (b + kb) % cfg.X)
    for ka, kb in others:
        ta, tb = far(ka, kb)
        barrier_to.append(device(cfg, ta, zl, tb, f))
    greet(barrier_to)
    red = Reduce(cfg, co, part, *red_sc)
    red.start()

    def across(layer, o, z):
        src, dst = ((g1, b1), (g2, b2))[layer]
        ta, tb = far(*others[o])
        rows_ = src.at[pl.ds(flat(cfg, ta, z, tb, 0), cfg.FS)]
        return remote(rows_, dst.at[o, pl.ds(z * cfg.FS, cfg.FS)], ts[2 * layer].at[o, z], ts[2 * layer + 1].at[o, z], device(cfg, ta, zl, tb, f))

    for layer in (1, 0):
        for o in range(len(others)):
            for z in range(cfg.ZL):
                across(layer, o, z).start()
    ex_d = Exchange(cfg, co, lambda i: dir_low.at[pl.ds(i * cfg.T, cfg.T)], lambda i: dgot.at[:, pl.ds(pl.multiple_of(i * cfg.FW, 128), cfg.FW)], ds, dr)
    ex_h = Exchange(cfg, co, lambda i: hid_low.at[pl.ds(i * cfg.T, cfg.T)], lambda i: hid.at[:, pl.ds(pl.multiple_of(i * cfg.FW, 128), cfg.FW)], hs, hr)
    ex_d.start()
    ex_h.start()
    copies = [pltpu.make_async_copy(e.src(s), e.dst(s), own.at[i]) for i, e in enumerate((ex_d, ex_h))]
    for copy in copies:
        copy.start()
    red.middle()
    red.finish()
    ex_d.finish()
    for copy in copies:
        copy.wait()
    step = 64

    def body(i, carry):
        s0, s1 = carry
        at = pl.ds(pl.multiple_of(i * step, 8), step)
        value = red.total(at)
        z, inverse = normalize(x[at, :].astype(F32))
        h = value * vec[4:5, :]
        m0 = jnp.mean(h, axis=-1, keepdims=True)
        m1 = jnp.mean(h * z, axis=-1, keepdims=True)
        grad[at, :] = (h - m0 - z * m1) * inverse + dgot[at, :].astype(F32)
        return s0 + jnp.sum(value * z, axis=0, keepdims=True), s1 + jnp.sum(value, axis=0, keepdims=True)

    zero = jnp.zeros((1, cfg.D), F32)
    s0, s1 = lax.fori_loop(0, cfg.T // step, body, (zero, zero))
    sums[0:1, :] = s0
    sums[1:2, :] = s1
    ex_h.finish()
    for layer in (1, 0):
        for o in range(len(others)):
            for z in range(cfg.ZL):
                across(layer, o, z).wait()


def last(cfg, part, dir_low, hid_low, g1, g2, x, vec):
    n = cfg.A * cfg.X - 1
    got = jax.ShapeDtypeStruct((n, cfg.F, cfg.R, 3 * cfg.FW), BF)
    return pl.pallas_call(
        functools.partial(last_kernel, cfg),
        name="last",
        out_shape=(
            jax.ShapeDtypeStruct((cfg.T, cfg.D), F32),
            jax.ShapeDtypeStruct((cfg.T, cfg.D), BF),
            got,
            got,
            jax.ShapeDtypeStruct((8, cfg.D), F32),
        ),
        in_specs=[HBM] * 5 + [VM] * 2,
        out_specs=[VM, HBM, HBM, HBM, VM],
        scratch_shapes=[pltpu.VMEM((cfg.T, cfg.D), BF)]
        + reduce_scratch(cfg, cfg.T, cfg.D)
        + [DMA((2,))]
        + [DMA((cfg.F,))] * 4
        + [DMA((n, cfg.ZL))] * 4,
        compiler_params=pltpu.CompilerParams(collective_id=3, has_side_effects=True, vmem_limit_bytes=VMEM_CAP),
    )(part, dir_low, hid_low, g1, g2, x, vec)


def end_kernel(cfg, w1, w2, small, o1, o2, sg, own, small_send, small_recv, *sc):
    co = coords(cfg)
    a, zl, b, f = co
    s, me = zl * cfg.FS + f, flat(cfg, *co)
    greet_all(cfg, me)

    def pieces(layer, k):
        src, dst = ((w1, o1), (w2, o2))[layer]
        to = (s + k) % cfg.F
        for c in range(3):
            piece = src.at[to, :, pl.ds(c * cfg.FW, cfg.FW)]
            place = dst.at[:, pl.ds(pl.multiple_of(c * cfg.D + s * cfg.FW, 128), cfg.FW)]
            if k == 0:
                yield pltpu.make_async_copy(piece, place, own.at[layer, c])
            else:
                yield remote(piece, place, sc[2 * layer].at[k, c], sc[2 * layer + 1].at[k, c], member(cfg, a, b, to))

    every = [(layer, k) for layer in range(2) for k in range(cfg.F)]
    for layer, k in every:
        for copy in pieces(layer, k):
            copy.start()

    def each(k, _):
        m = (me + k) % cfg.N
        remote(small.at[m // cfg.PER], sg.at[me], small_send, small_recv, (m // cfg.FS, m % cfg.FS)).start()
        return 0

    lax.fori_loop(1, cfg.N, each, 0)
    mine = pltpu.make_async_copy(small.at[me // cfg.PER], sg.at[me], own.at[2, 0])
    mine.start()
    for layer, k in every:
        for copy in pieces(layer, k):
            copy.wait()
    mine.wait()
    everyone = sg.at[pl.ds(0, cfg.N - 1)]
    pltpu.make_async_copy(everyone, everyone, small_recv).wait()
    pltpu.make_async_copy(everyone, everyone, small_send).wait()


def end(cfg, w1, w2, small):
    out = jax.ShapeDtypeStruct((cfg.R, 3 * cfg.D), BF)
    return pl.pallas_call(
        functools.partial(end_kernel, cfg),
        name="end",
        out_shape=(out, out, jax.ShapeDtypeStruct((cfg.N,) + small.shape[1:], F32)),
        in_specs=[HBM] * 3,
        out_specs=[HBM] * 3,
        scratch_shapes=[DMA((3, 3)), DMA(()), DMA(())] + [DMA((cfg.F, 3))] * 4,
        compiler_params=pltpu.CompilerParams(collective_id=4, has_side_effects=True),
    )(w1, w2, small)


def wgrad(cfg, low, grads):
    out = lax.dot_general(low.reshape(cfg.M, cfg.D), grads, (((0,), (0,)), ((), ())), preferred_element_type=F32)
    return out.astype(BF).reshape(cfg.N, cfg.R, 3 * cfg.FW)


def own_sum(cfg, g, got, a, b):
    mine = lax.dynamic_index_in_dim(lax.dynamic_index_in_dim(g.reshape(cfg.A, cfg.ZL, cfg.X, cfg.FS, cfg.R, 3 * cfg.FW), a, 0, False), b, 1, False)
    mine = mine.reshape(cfg.F, cfg.R, 3 * cfg.FW)
    return (mine.astype(F32) + jnp.sum(got.astype(F32), axis=0)).astype(BF)


def shards(mesh, inputs, lengths, w1, pf1, pr1, bf1, br1, ng1, nb1, w2, pf2, pr2, bf2, br2, ng2, nb2, cotangent):
    _, steps, width = inputs.shape
    cfg = make_cfg(mesh, steps, width)
    a, zl, b, f = coords(cfg)
    j, me = zl * cfg.FS + f, flat(cfg, a, zl, b, f)
    vectors = [pf1, pr1, bf1, br1, ng1, nb1, pf2, pr2, bf2, br2, ng2, nb2, jnp.broadcast_to(lengths.astype(BF), (cfg.R,))]
    packed = jnp.tile(jnp.concatenate([jnp.stack(vectors), jnp.zeros((3, cfg.R), BF)]), (1, cfg.PER))
    lane = lax.broadcasted_iota(jnp.int32, (16, 128), 1)
    packed = jnp.where(lane // cfg.R == me % cfg.PER, packed, jnp.zeros_like(packed))

    xg, cg, full1, full2, smalls = start(cfg, inputs[0], cotangent[0], w1, w2, packed)
    full1, full2 = full1.reshape(cfg.D, 3 * cfg.FW), full2.reshape(cfg.D, 3 * cfg.FW)
    vec = jnp.sum(smalls.astype(F32).reshape(cfg.N // cfg.PER, cfg.PER, 16, 128), axis=1)
    vec = jnp.transpose(vec, (1, 0, 2)).reshape(16, cfg.D)
    mine = lax.dynamic_slice(vec, (0, j * cfg.FW), (16, cfg.FW))
    lens = vec[12].reshape(cfg.A, cfg.ZL, cfg.X, cfg.FS, cfg.R)[..., 0]
    lens = lax.dynamic_index_in_dim(lax.dynamic_index_in_dim(lens, a, 0, False), b, 1, False).reshape(cfg.S)
    lens = jnp.broadcast_to(lens.astype(jnp.int32)[:, None], (cfg.S, 128))

    low1, hid1, hid1_low, inp, cand, states, tf, tr = first(cfg, xg, full1, vec, mine, lens)
    hg = gather_hidden(cfg, hid1_low).reshape(cfg.S, cfg.T, cfg.D)
    low2, hid2_low, grads2, part2, z_own, inv, direct2, sums2 = second(cfg, hg, full2, vec, mine, lens, hid1, cg)
    grad1, norm2 = middle(cfg, part2, z_own, inv, direct2, mine)
    gw2 = wgrad(cfg, low2, grads2)
    grads1, part1, direct1, sums1 = third(cfg, full1, mine, lens, inp, cand, states, tf, tr, grad1)
    gw1 = wgrad(cfg, low1, grads1)
    input_grad, hidden, got1, got2, norm1 = last(cfg, part1, direct1, hid2_low, gw1, gw2, inputs[0], vec)
    s1, s2 = own_sum(cfg, gw1, got1, a, b), own_sum(cfg, gw2, got2, a, b)

    block = jnp.concatenate([sums1[:4], jnp.zeros((2, cfg.FW), F32), sums2[:4], norm2[:2], jnp.zeros((4, cfg.FW), F32)])
    small = lax.dynamic_update_slice(jnp.zeros((16, cfg.D), F32), block, (0, j * cfg.FW))
    small = lax.dynamic_update_slice(small, norm1[:2], (4, 0))
    small = jnp.transpose(small.reshape(16, cfg.N // cfg.PER, 128), (1, 0, 2))
    gw1, gw2, smalls = end(cfg, s1, s2, small)
    total = jnp.sum(smalls, axis=0)
    total = lax.dynamic_slice(total, (0, (me % cfg.PER) * cfg.R), (16, cfg.R))
    out = [hidden[None], input_grad[None], gw1.astype(F32)] + [total[i] for i in range(6)] + [gw2.astype(F32)] + [total[i] for i in range(6, 12)]
    return tuple(out)


def solution(mesh):
    both = ("dp", "fsdp")
    seq, mat, vec = P(both, None, None), P(both, None), P(both)
    return jax.shard_map(
        functools.partial(shards, mesh),
        mesh=mesh,
        in_specs=(seq, vec) + ((mat,) + (vec,) * 6) * 2 + (seq,),
        out_specs=(seq, seq) + ((mat,) + (vec,) * 6) * 2,
        check_vma=False,
    )
```

```python
import functools
from collections import namedtuple

import jax
import jax.numpy as jnp
from jax import lax
from jax.experimental import pallas as pl
from jax.experimental.pallas import tpu as pltpu
from jax.sharding import PartitionSpec as P

MESH = pl.DeviceIdType.MESH
HBM = pl.BlockSpec(memory_space=pltpu.HBM)
VM = pl.BlockSpec(memory_space=pltpu.VMEM)
DMA = pltpu.SemaphoreType.DMA
BF = jnp.bfloat16
F32 = jnp.float32
EPSILON = 1e-05
PAD = 8
VMEM_CAP = 62 << 20

Cfg = namedtuple("Cfg", ("DP", "FS", "N", "A", "ZL", "X", "F", "C", "S", "T", "TP", "D", "FW", "L", "R", "M", "PER"))


def make_cfg(mesh, steps, width):
    dp, fs = mesh.shape["dp"], mesh.shape["fsdp"]
    zl = 2 if fs < 8 and dp % 4 == 0 else 1
    x = 2 if zl == 1 and dp % 2 == 0 else 1
    a = dp // (zl * x)
    f = zl * fs
    fw = width // f
    rows = width // (dp * fs)
    return Cfg(dp, fs, dp * fs, a, zl, x, f, f // 2, f, steps, steps + PAD, width, fw, fw // 128, rows, f * steps, 128 // rows)


def coords(cfg):
    dp, f = lax.axis_index("dp"), lax.axis_index("fsdp")
    b, zl, a = dp % cfg.X, (dp // cfg.X) % cfg.ZL, dp // (cfg.X * cfg.ZL)
    return a, zl, b, f


def device(cfg, a, zl, b, f):
    return ((a * cfg.ZL + zl) * cfg.X + b, f)


def flat(cfg, a, zl, b, f):
    return ((a * cfg.ZL + zl) * cfg.X + b) * cfg.FS + f


def member(cfg, a, b, s):
    return device(cfg, a, s // cfg.FS, b, s % cfg.FS)


def remote(src, dst, send, recv, where):
    return pltpu.make_async_remote_copy(src_ref=src, dst_ref=dst, send_sem=send, recv_sem=recv, device_id=where, device_id_type=MESH)


def greet(targets):
    barrier = pltpu.get_barrier_semaphore()
    for where in targets:
        pl.semaphore_signal(barrier, inc=1, device_id=where, device_id_type=MESH)
    pl.semaphore_wait(barrier, len(targets))


def greet_all(cfg, me):
    barrier = pltpu.get_barrier_semaphore()

    def one(k, _):
        m = (me + k) % cfg.N
        pl.semaphore_signal(barrier, inc=1, device_id=(m // cfg.FS, m % cfg.FS), device_id_type=MESH)
        return 0

    lax.fori_loop(1, cfg.N, one, 0)
    pl.semaphore_wait(barrier, cfg.N - 1)


def group_targets(cfg, a, b, s):
    return [member(cfg, a, b, (s + k) % cfg.F) for k in range(1, cfg.F)]


class Gather:
    def __init__(self, cfg, co, src, slot, send, recv, mate_send, mate_recv):
        self.cfg, self.co, self.src, self.slot = cfg, co, src, slot
        self.sems = send, recv, mate_send, mate_recv
        a, zl, b, f = co
        self.s = zl * cfg.FS + f
        self.cell, self.core = self.s // 2, self.s % 2

    def far(self, k):
        cfg, (a, zl, b, f) = self.cfg, self.co
        send, recv, _, _ = self.sems
        to = member(cfg, a, b, ((self.cell + k) % cfg.C) * 2 + self.core)
        return remote(self.src, self.slot(self.s), send.at[k], recv.at[k], to)

    def near(self, k):
        cfg, (a, zl, b, f) = self.cfg, self.co
        _, _, send, recv = self.sems
        origin = ((self.cell - k + cfg.C) % cfg.C) * 2 + self.core
        src = self.src if k == 0 else self.slot(origin)
        return remote(src, self.slot(origin), send.at[k], recv.at[k], member(cfg, a, b, self.cell * 2 + 1 - self.core))

    def start(self):
        for k in range(1, self.cfg.C):
            self.far(k).start()
        self.near(0).start()

    def finish(self):
        for k in range(1, self.cfg.C):
            self.far(k).wait_recv()
            self.near(k).start()
        for k in range(1, self.cfg.C):
            self.far(k).wait_send()
        for k in range(self.cfg.C):
            self.near(k).wait()


class Exchange:
    def __init__(self, cfg, co, src, dst, send, recv):
        self.cfg, self.co, self.src, self.dst, self.send, self.recv = cfg, co, src, dst, send, recv
        self.s = co[1] * cfg.FS + co[3]

    def copy(self, k):
        a, zl, b, f = self.co
        to = (self.s + k) % self.cfg.F
        return remote(self.src(to), self.dst(self.s), self.send.at[k], self.recv.at[k], member(self.cfg, a, b, to))

    def start(self):
        for k in range(1, self.cfg.F):
            self.copy(k).start()

    def piece_sender(self, pieces):
        count = self.cfg.F // pieces

        def send(p):
            for h in range(count):
                to = p * count + h
                pl.when(to != self.s)(lambda to=to: self.copy((to - self.s + self.cfg.F) % self.cfg.F).start())

        return send

    def finish(self):
        for k in range(1, self.cfg.F):
            self.copy(k).wait()


class WeightGather:
    def __init__(self, cfg, co, w, full, own, send, recv, asend, arecv, bsend, brecv):
        self.cfg, self.co, self.w, self.full = cfg, co, w, full
        self.own, self.send, self.recv = own, send, recv
        self.asend, self.arecv, self.bsend, self.brecv = asend, arecv, bsend, brecv
        self.s = co[1] * cfg.FS + co[3]

    def pieces(self, k):
        cfg, (a, zl, b, f) = self.cfg, self.co
        to = (self.s + k) % cfg.F
        me = flat(cfg, a, zl, b, f)
        for c in range(3):
            src = self.w.at[:, pl.ds(pl.multiple_of(c * cfg.D + to * cfg.FW, 128), cfg.FW)]
            dst = self.full.at[me, :, pl.ds(c * cfg.FW, cfg.FW)]
            if k == 0:
                yield pltpu.make_async_copy(src, dst, self.own.at[c])
            else:
                yield remote(src, dst, self.send.at[k, c], self.recv.at[k, c], member(cfg, a, b, to))

    def start(self):
        for k in range(self.cfg.F):
            for copy in self.pieces(k):
                copy.start()

    def middle(self):
        for k in range(self.cfg.F):
            for copy in self.pieces(k):
                copy.wait()

    def rows_of(self, a, p, b):
        cfg = self.cfg
        count = cfg.FS // 2
        return self.full.at[pl.ds(flat(cfg, a, p // 2, b, 0) + (p % 2) * count, count)]

    def to_a(self, k, p):
        cfg, (a, zl, b, f) = self.cfg, self.co
        rows = self.rows_of(a, p, b)
        return remote(rows, rows, self.asend.at[k, p], self.arecv.at[k, p], device(cfg, (a + k) % cfg.A, zl, b, f))

    def to_b(self, k, ka, p):
        cfg, (a, zl, b, f) = self.cfg, self.co
        rows = self.rows_of((a - ka + cfg.A) % cfg.A, p, b)
        return remote(rows, rows, self.bsend.at[k, ka, p], self.brecv.at[k, ka, p], device(cfg, a, zl, (b + k) % cfg.X, f))

    def start_a(self):
        for p in range(2 * self.cfg.ZL):
            for k in range(1, self.cfg.A):
                self.to_a(k, p).start()

    def start_b(self):
        for p in range(2 * self.cfg.ZL):
            for k in range(1, self.cfg.X):
                self.to_b(k, 0, p).start()

    def start_out(self):
        self.start_a()
        self.start_b()

    def forward(self, p):
        for ka in range(1, self.cfg.A):
            self.to_a(ka, p).wait_recv()
            for k in range(1, self.cfg.X):
                self.to_b(k, ka, p).start()

    def finish(self):
        cfg = self.cfg
        for p in range(2 * cfg.ZL):
            for ka in range(cfg.A):
                for k in range(1, cfg.X):
                    self.to_b(k, ka, p).wait()
            for ka in range(1, cfg.A):
                self.to_a(ka, p).wait_send()

    def finish_out(self):
        for p in range(2 * self.cfg.ZL):
            self.forward(p)
        self.finish()


def t_targets(cfg, co):
    a, zl, b, f = co
    return [device(cfg, (a + way + cfg.A) % cfg.A, zl, b, f) for way in (1, -1)]


def weight_sems(cfg):
    return [DMA((3,)), DMA((cfg.F, 3)), DMA((cfg.F, 3))] + [DMA((cfg.A, 2 * cfg.ZL))] * 2 + [DMA((cfg.X, cfg.A, 2 * cfg.ZL))] * 2


def start_kernel(cfg, x, cot, w1, w2, small, xg, cg, f1, f2, sg, own_sem, small_send, small_recv, gs, gr, gms, gmr, cs, cr, *wsems):
    co = coords(cfg)
    a, zl, b, f = co
    s, me = zl * cfg.FS + f, flat(cfg, *co)
    greet_all(cfg, me)
    weights = [WeightGather(cfg, co, w1, f1, *wsems[:7]), WeightGather(cfg, co, w2, f2, *wsems[7:])]
    weights[0].start()
    gather = Gather(cfg, co, x, lambda i: xg.at[i], gs, gr, gms, gmr)
    gather.start()

    def each(k, _):
        m = (me + k) % cfg.N
        remote(small, sg.at[me], small_send, small_recv, (m // cfg.FS, m % cfg.FS)).start()
        return 0

    lax.fori_loop(1, cfg.N, each, 0)
    weights[1].start()
    exchange = Exchange(cfg, co, lambda i: cot.at[:, pl.ds(pl.multiple_of(i * cfg.FW, 128), cfg.FW)], lambda i: cg.at[i], cs, cr)
    exchange.start()
    locals_ = [
        pltpu.make_async_copy(x, xg.at[s], own_sem.at[0]),
        pltpu.make_async_copy(cot.at[:, pl.ds(pl.multiple_of(s * cfg.FW, 128), cfg.FW)], cg.at[s], own_sem.at[1]),
        pltpu.make_async_copy(small, sg.at[me], own_sem.at[2]),
    ]
    for copy in locals_:
        copy.start()
    weights[0].middle()
    weights[0].start_out()
    weights[1].middle()
    gather.finish()
    weights[0].finish_out()
    weights[1].start_out()
    exchange.finish()
    weights[1].finish_out()
    everyone = sg.at[pl.ds(0, cfg.N - 1)]
    pltpu.make_async_copy(everyone, everyone, small_recv).wait()
    pltpu.make_async_copy(everyone, everyone, small_send).wait()
    for copy in locals_:
        copy.wait()


def start(cfg, x, cot, w1, w2, small):
    full = jax.ShapeDtypeStruct((cfg.N, cfg.R, 3 * cfg.FW), BF)
    return pl.pallas_call(
        functools.partial(start_kernel, cfg),
        name="start",
        out_shape=(
            jax.ShapeDtypeStruct((cfg.S, cfg.T, cfg.D), BF),
            jax.ShapeDtypeStruct((cfg.S, cfg.T, cfg.FW), BF),
            full,
            full,
            jax.ShapeDtypeStruct((cfg.N, 16, 128), BF),
        ),
        in_specs=[HBM] * 5,
        out_specs=[HBM] * 5,
        scratch_shapes=[DMA((3,)), DMA(()), DMA(())] + [DMA((cfg.C,))] * 4 + [DMA((cfg.F,))] * 2 + weight_sems(cfg) * 2,
        compiler_params=pltpu.CompilerParams(collective_id=0, has_side_effects=True),
    )(x, cot, w1, w2, small)


def rows(cfg, ref, t, first, count):
    return jnp.concatenate([ref[first + i, pl.ds(t, cfg.S, stride=cfg.TP), :] for i in range(count)], axis=1)


def put(cfg, ref, t, value, first=0):
    for i in range(value.shape[1] // 128):
        ref[first + i, pl.ds(t, cfg.S, stride=cfg.TP), :] = value[:, 128 * i : 128 * i + 128]


def wide(cfg, ref, row):
    return jnp.broadcast_to(ref[row : row + 1, :], (cfg.S, cfg.FW))


def scan_forward(cfg, proj, inp, vec, base, lens, hid, states, tf_ref, tr_ref):
    half_pf, half_pr = 0.5 * wide(cfg, vec, base), 0.5 * wide(cfg, vec, base + 1)
    half_bf, half_br = 0.5 * wide(cfg, vec, base + 2), 0.5 * wide(cfg, vec, base + 3)
    live = jnp.broadcast_to(lens[:, 0:1], (cfg.S, cfg.FW))

    def step(t, c):
        u, p, q = (rows(cfg, proj, t, i * cfg.L, cfg.L) for i in range(3))
        here = rows(cfg, inp, t, 0, cfg.L)
        p, q, hu, hc = 0.5 * p + half_bf, 0.5 * q + half_br, 0.5 * u, 0.5 * c
        tf = jnp.tanh(p + half_pf * c)
        tr = jnp.tanh(q + half_pr * c)
        new = (hc + hu) + tf * (hc - hu)
        out = jnp.where(t < live, 0.5 * (here + new) + 0.5 * tr * (new - here), 0.0)
        put(cfg, hid, t, out)
        put(cfg, states, t, new)
        put(cfg, tf_ref, t, tf)
        put(cfg, tr_ref, t, tr)
        return new

    lax.fori_loop(0, cfg.T, step, jnp.zeros((cfg.S, cfg.FW), F32), unroll=4)


def scan_backward(cfg, cand, inp, vec, base, lens, states, tf_ref, tr_ref, grad, grads, direct, sums):
    pf, pr = wide(cfg, vec, base), wide(cfg, vec, base + 1)
    live = jnp.broadcast_to(lens[:, 0:1], (cfg.S, cfg.FW))

    def step(i, carry):
        e, new, s0, s1, s2, s3 = carry
        t = cfg.T - 1 - i
        u, here, g = rows(cfg, cand, t, 0, cfg.L), rows(cfg, inp, t, 0, cfg.L), rows(cfg, grad, t, 0, cfg.L)
        f = 0.5 * rows(cfg, tf_ref, t, 0, cfg.L) + 0.5
        r = 0.5 * rows(cfg, tr_ref, t, 0, cfg.L) + 0.5
        c = jnp.where(t > 0, rows(cfg, states, jnp.maximum(t - 1, 0), 0, cfg.L), 0.0)
        k = jnp.where(t < live, g, 0.0)
        kr = k * r
        rest = 1.0 - f
        w = (c - u) * (f * rest)
        dq = (k - kr) * (new - here) * r
        s = e + kr
        dp = s * w
        put(cfg, grads, t, s * rest, 0)
        put(cfg, grads, t, dp, cfg.L)
        put(cfg, grads, t, dq, 2 * cfg.L)
        put(cfg, direct, t, k - kr)
        e = s * (f + w * pf) + dq * pr
        return e, c, s0 + dp * c, s1 + dq * c, s2 + dp, s3 + dq

    zero = jnp.zeros((cfg.S, cfg.FW), F32)
    out = lax.fori_loop(0, cfg.T, step, (zero, rows(cfg, states, cfg.T - 1, 0, cfg.L)) + (zero,) * 4, unroll=4)
    for i in range(4):
        sums[i : i + 1, :] = jnp.sum(out[2 + i], axis=0, keepdims=True)


def normalize(x):
    center = x - jnp.mean(x, axis=-1, keepdims=True)
    inverse = lax.rsqrt(jnp.mean(center * center, axis=-1, keepdims=True) + EPSILON)
    return center * inverse, inverse


def project(cfg, z, gain, shift, w, low, proj, s):
    lowered = (z * gain + shift).astype(BF)
    low[0] = lowered
    out = jnp.dot(lowered, w[...], preferred_element_type=F32)
    base = pl.multiple_of(s * cfg.TP, 8)
    for i in range(3 * cfg.L):
        proj[i, pl.ds(base, cfg.T), :] = out[:, 128 * i : 128 * i + 128]


def seq_block(cfg, ref, i, s):
    return ref[i, pl.ds(pl.multiple_of(s * cfg.TP, 8), cfg.T), :]


def narrow(cfg, src, dst, count):
    for i in range(count):
        for s in range(cfg.S):
            dst[s * cfg.T : (s + 1) * cfg.T, 128 * i : 128 * i + 128] = src[i, s * cfg.TP : s * cfg.TP + cfg.T, :].astype(dst.dtype)


def first_kernel(cfg, x, w, vec, mine, lens, low, hid, hid_low, inp, cand, states, tf, tr, proj):
    s = pl.program_id(0)
    _, zl, _, f = coords(cfg)
    j = zl * cfg.FS + f
    data = x[0].astype(F32)
    z, _ = normalize(data)
    project(cfg, z, vec[4:5, :], vec[5:6, :], w, low, proj, s)
    own = x[0, :, pl.ds(pl.multiple_of(j * cfg.FW, 128), cfg.FW)].astype(F32)
    for i in range(cfg.L):
        inp[i, pl.ds(pl.multiple_of(s * cfg.TP, 8), cfg.T), :] = own[:, 128 * i : 128 * i + 128]

    @pl.when(s == cfg.S - 1)
    def _():
        scan_forward(cfg, proj, inp, mine, 0, lens, hid, states, tf, tr)
        narrow(cfg, hid, hid_low, cfg.L)
        for i in range(cfg.L):
            cand[i] = proj[i]


def keep(cfg, count):
    return jax.ShapeDtypeStruct((count, cfg.S * cfg.TP, 128), F32)


def const(shape):
    return pl.BlockSpec(shape, lambda i: (0,) * len(shape))


def first(cfg, x, w, vec, mine, lens):
    state = keep(cfg, cfg.L)
    spec = const(state.shape)
    return pl.pallas_call(
        functools.partial(first_kernel, cfg),
        name="first",
        grid=(cfg.S,),
        out_shape=(jax.ShapeDtypeStruct((cfg.S, cfg.T, cfg.D), BF), state, jax.ShapeDtypeStruct((cfg.M, cfg.FW), BF)) + (state,) * 5,
        in_specs=[pl.BlockSpec((1, cfg.T, cfg.D), lambda i: (i, 0, 0)), const(w.shape), const(vec.shape), const(mine.shape), const(lens.shape)],
        out_specs=[pl.BlockSpec((1, cfg.T, cfg.D), lambda i: (i, 0, 0)), spec, const((cfg.M, cfg.FW))] + [spec] * 5,
        scratch_shapes=[pltpu.VMEM((3 * cfg.L, cfg.S * cfg.TP, 128), F32)],
        compiler_params=pltpu.CompilerParams(vmem_limit_bytes=VMEM_CAP),
    )(x, w, vec, mine, lens)


def second_kernel(cfg, x, w, vec, mine, lens, inp, grad_in, low, hid_low, grads_low, part, z_own, inv, direct, sums, proj, hid, states, tf, tr, grad, grads):
    i = pl.program_id(0)
    _, zl, _, f = coords(cfg)
    j = zl * cfg.FS + f

    @pl.when(i < cfg.S)
    def _():
        z, inverse = normalize(x[0].astype(F32))
        project(cfg, z, vec[10:11, :], vec[11:12, :], w, low, proj, i)
        at = pl.ds(pl.multiple_of(i * cfg.T, 8), cfg.T)
        inv[at, :] = jnp.broadcast_to(inverse, (cfg.T, 128))
        raw = x[0, :, pl.ds(pl.multiple_of(j * cfg.FW, 128), cfg.FW)].astype(F32)
        mean = jnp.mean(x[0].astype(F32), axis=-1, keepdims=True)
        z_own[at, :] = (raw - mean) * inverse

    @pl.when(i == cfg.S - 1)
    def _():
        for s in range(cfg.S):
            g = grad_in[s].astype(F32)
            for l in range(cfg.L):
                grad[l, s * cfg.TP : s * cfg.TP + cfg.T, :] = g[:, 128 * l : 128 * l + 128]
        scan_forward(cfg, proj, inp, mine, 6, lens, hid, states, tf, tr)
        narrow(cfg, hid, hid_low, cfg.L)
        scan_backward(cfg, proj, inp, mine, 6, lens, states, tf, tr, grad, grads, direct, sums)
        narrow(cfg, grads, grads_low, 3 * cfg.L)

    @pl.when(i >= cfg.S)
    def _():
        k = i - cfg.S
        block = w[pl.ds(pl.multiple_of(k * cfg.FW, 8), cfg.FW), :]
        part[0] = lax.dot_general(grads_low[...], block, (((1,), (1,)), ((), ())), preferred_element_type=F32).astype(BF)


def second(cfg, x, w, vec, mine, lens, inp, grad_in):
    state = keep(cfg, cfg.L)
    spec = const(state.shape)
    big = pltpu.VMEM(state.shape, F32)
    last = cfg.S - 1
    one = pl.BlockSpec((1, cfg.T, cfg.D), lambda i: (jnp.minimum(i, last), 0, 0))
    return pl.pallas_call(
        functools.partial(second_kernel, cfg),
        name="second",
        grid=(cfg.S + cfg.F,),
        out_shape=(
            jax.ShapeDtypeStruct((cfg.S, cfg.T, cfg.D), BF),
            jax.ShapeDtypeStruct((cfg.M, cfg.FW), BF),
            jax.ShapeDtypeStruct((cfg.M, 3 * cfg.FW), BF),
            jax.ShapeDtypeStruct((cfg.F, cfg.M, cfg.FW), BF),
            jax.ShapeDtypeStruct((cfg.M, cfg.FW), F32),
            jax.ShapeDtypeStruct((cfg.M, 128), F32),
            state,
            jax.ShapeDtypeStruct((8, cfg.FW), F32),
        ),
        in_specs=[one, const(w.shape), const(vec.shape), const(mine.shape), const(lens.shape), spec, const(grad_in.shape)],
        out_specs=[
            one,
            const((cfg.M, cfg.FW)),
            const((cfg.M, 3 * cfg.FW)),
            pl.BlockSpec((1, cfg.M, cfg.FW), lambda i: (jnp.maximum(i - cfg.S, 0), 0, 0)),
            const((cfg.M, cfg.FW)),
            const((cfg.M, 128)),
            spec,
            const((8, cfg.FW)),
        ],
        scratch_shapes=[pltpu.VMEM((3 * cfg.L, cfg.S * cfg.TP, 128), F32)] + [big] * 5 + [pltpu.VMEM((3 * cfg.L, cfg.S * cfg.TP, 128), F32)],
        compiler_params=pltpu.CompilerParams(vmem_limit_bytes=VMEM_CAP),
    )(x, w, vec, mine, lens, inp, grad_in)


def third_kernel(cfg, w, mine, lens, inp, cand, states, tf, tr, grad, grads_low, part, direct_low, sums, grads, direct):
    s = pl.program_id(0)

    @pl.when(s == 0)
    def _():
        scan_backward(cfg, cand, inp, mine, 0, lens, states, tf, tr, grad, grads, direct, sums)
        narrow(cfg, grads, grads_low, 3 * cfg.L)
        narrow(cfg, direct, direct_low, cfg.L)

    at = pl.ds(pl.multiple_of(s * cfg.T, 8), cfg.T)
    part[0] = lax.dot_general(grads_low[at, :], w[...], (((1,), (1,)), ((), ())), preferred_element_type=F32).astype(BF)


def third(cfg, w, mine, lens, inp, cand, states, tf, tr, grad):
    state = keep(cfg, cfg.L)
    spec = const(state.shape)
    return pl.pallas_call(
        functools.partial(third_kernel, cfg),
        name="third",
        grid=(cfg.S,),
        out_shape=(
            jax.ShapeDtypeStruct((cfg.M, 3 * cfg.FW), BF),
            jax.ShapeDtypeStruct((cfg.S, cfg.T, cfg.D), BF),
            jax.ShapeDtypeStruct((cfg.M, cfg.FW), BF),
            jax.ShapeDtypeStruct((8, cfg.FW), F32),
        ),
        in_specs=[const(w.shape), const(mine.shape), const(lens.shape)] + [spec] * 6,
        out_specs=[const((cfg.M, 3 * cfg.FW)), pl.BlockSpec((1, cfg.T, cfg.D), lambda i: (i, 0, 0)), const((cfg.M, cfg.FW)), const((8, cfg.FW))],
        scratch_shapes=[pltpu.VMEM((3 * cfg.L, cfg.S * cfg.TP, 128), F32), pltpu.VMEM(state.shape, F32)],
        compiler_params=pltpu.CompilerParams(vmem_limit_bytes=VMEM_CAP),
    )(w, mine, lens, inp, cand, states, tf, tr, grad)


def gather_kernel(cfg, x, out, own, gs, gr, gms, gmr):
    co = coords(cfg)
    a, zl, b, f = co
    s = zl * cfg.FS + f
    cell, core = s // 2, s % 2
    greet([member(cfg, a, b, ((cell + k) % cfg.C) * 2 + core) for k in range(1, cfg.C)] + [member(cfg, a, b, cell * 2 + 1 - core)])
    slot = lambda i: out.at[:, pl.ds(pl.multiple_of(i * cfg.FW, 128), cfg.FW)]
    gather = Gather(cfg, co, x, slot, gs, gr, gms, gmr)
    gather.start()
    copy = pltpu.make_async_copy(x, slot(s), own)
    copy.start()
    gather.finish()
    copy.wait()


def gather_hidden(cfg, x):
    return pl.pallas_call(
        functools.partial(gather_kernel, cfg),
        name="gather_hidden",
        out_shape=jax.ShapeDtypeStruct((cfg.M, cfg.D), BF),
        in_specs=[HBM],
        out_specs=HBM,
        scratch_shapes=[DMA(())] + [DMA((cfg.C,))] * 4,
        compiler_params=pltpu.CompilerParams(collective_id=1, has_side_effects=True),
    )(x)


class Reduce:
    def __init__(self, cfg, co, part, own, mate, out, got, load, ms, mr, fs, fr):
        self.cfg, self.co, self.part, self.own, self.mate, self.out, self.got = cfg, co, part, own, mate, out, got
        self.load, self.ms, self.mr, self.fs, self.fr = load, ms, mr, fs, fr
        self.s = co[1] * cfg.FS + co[3]
        self.cell, self.core = self.s // 2, self.s % 2

    def target(self, k):
        return (self.cell + k) % self.cfg.C

    def to_mate(self, k):
        a, _, b, _ = self.co
        return remote(
            self.part.at[self.target(k) * 2 + 1 - self.core], self.mate.at[k], self.ms.at[k], self.mr.at[k],
            member(self.cfg, a, b, self.cell * 2 + 1 - self.core),
        )

    def fetch(self, k):
        return pltpu.make_async_copy(self.part.at[self.target(k) * 2 + self.core], self.own.at[k], self.load.at[k])

    def far(self, k):
        a, _, b, _ = self.co
        return remote(self.out.at[k - 1], self.got.at[k - 1], self.fs.at[k], self.fr.at[k], member(self.cfg, a, b, self.target(k) * 2 + self.core))

    def order(self):
        return list(range(1, self.cfg.C)) + [0]

    def start(self):
        for k in self.order():
            self.to_mate(k).start()
            self.fetch(k).start()

    def middle(self):
        rows_, _ = self.own.shape[1:]
        step = 256 if rows_ % 256 == 0 else rows_
        for k in self.order():
            self.to_mate(k).wait_recv()
            self.fetch(k).wait()
            if k:

                def add(i, _):
                    at = pl.ds(pl.multiple_of(i * step, 8), step)
                    self.out[k - 1, at, :] = (self.own[k, at, :].astype(F32) + self.mate[k, at, :].astype(F32)).astype(BF)
                    return 0

                lax.fori_loop(0, rows_ // step, add, 0)
                self.far(k).start()

    def finish(self):
        for k in range(1, self.cfg.C):
            self.far(k).wait()
        for k in range(self.cfg.C):
            self.to_mate(k).wait_send()

    def total(self, at):
        value = self.own[0, at, :].astype(F32) + self.mate[0, at, :].astype(F32)
        for k in range(1, self.cfg.C):
            value = value + self.got[k - 1, at, :].astype(F32)
        return value


def reduce_scratch(cfg, rows_, cols):
    return [pltpu.VMEM((cfg.C, rows_, cols), BF)] * 2 + [pltpu.VMEM((cfg.C - 1, rows_, cols), BF)] * 2 + [DMA((cfg.C,))] * 5


def middle_kernel(cfg, part, z_own, inv, direct, mine, grad, sums, ng, stats, mean, *sc):
    red_sc, (ss, sr) = sc[:9], sc[9:]
    co = coords(cfg)
    a, zl, b, f = co
    s = zl * cfg.FS + f
    greet(group_targets(cfg, a, b, s))
    red = Reduce(cfg, co, part, *red_sc)
    red.start()
    red.middle()
    red.finish()
    gain = mine[10:11, :]
    eye = (lax.broadcasted_iota(jnp.int32, (128, 128), 0) == lax.broadcasted_iota(jnp.int32, (128, 128), 1)).astype(F32)

    def first_pass(i, carry):
        s0, s1 = carry
        at = pl.ds(pl.multiple_of(i * 128, 8), 128)
        value = red.total(at)
        z = z_own[at, :]
        h = value * gain
        ng[at, :] = h
        for n, x in ((0, h), (1, h * z)):
            col = jnp.sum(x, axis=-1, keepdims=True)
            stats[s, n, pl.ds(i, 1), :] = jnp.sum(col * eye, axis=0, keepdims=True)
        return s0 + jnp.sum(value * z, axis=0, keepdims=True), s1 + jnp.sum(value, axis=0, keepdims=True)

    zero = jnp.zeros((1, cfg.FW), F32)
    s0, s1 = lax.fori_loop(0, cfg.M // 128, first_pass, (zero, zero))
    sums[0:1, :] = s0
    sums[1:2, :] = s1
    exchange = Exchange(cfg, co, lambda i: stats.at[s], lambda i: stats.at[i], ss, sr)
    exchange.start()
    exchange.finish()
    total = stats[0]
    for i in range(1, cfg.F):
        total = total + stats[i]
    mean[...] = total * (1.0 / cfg.D)

    def second_pass(i, _):
        at = pl.ds(pl.multiple_of(i * 128, 8), 128)
        m0 = jnp.sum(mean[0, pl.ds(i, 1), :] * eye, axis=-1, keepdims=True)
        m1 = jnp.sum(mean[1, pl.ds(i, 1), :] * eye, axis=-1, keepdims=True)
        value = (ng[at, :] - m0 - z_own[at, :] * m1) * inv[at, 0:1]
        per = cfg.T // 128
        to = pl.ds(pl.multiple_of((i // per) * cfg.TP + (i % per) * 128, 8), 128)
        for l in range(cfg.L):
            grad[l, to, :] = value[:, 128 * l : 128 * l + 128] + direct[l, to, :]
        return 0

    lax.fori_loop(0, cfg.M // 128, second_pass, 0)


def middle(cfg, part, z_own, inv, direct, mine):
    return pl.pallas_call(
        functools.partial(middle_kernel, cfg),
        name="middle",
        out_shape=(keep(cfg, cfg.L), jax.ShapeDtypeStruct((8, cfg.FW), F32)),
        in_specs=[HBM] + [VM] * 4,
        out_specs=[VM] * 2,
        scratch_shapes=[
            pltpu.VMEM((cfg.M, cfg.FW), F32),
            pltpu.VMEM((cfg.F, 2, cfg.M // 128, 128), F32),
            pltpu.VMEM((2, cfg.M // 128, 128), F32),
        ]
        + reduce_scratch(cfg, cfg.M, cfg.FW)
        + [DMA((cfg.F,))] * 2,
        compiler_params=pltpu.CompilerParams(collective_id=2, has_side_effects=True, vmem_limit_bytes=VMEM_CAP),
    )(part, z_own, inv, direct, mine)


def last_kernel(cfg, part, dir_low, hid_low, g1, g2, x, vec, grad, hid, b1, b2, sums, dgot, *sc):
    red_sc, sc = sc[:9], sc[9:]
    own, ds, dr, hs, hr = sc[:5]
    ts = sc[5:]
    co = coords(cfg)
    a, zl, b, f = co
    s = zl * cfg.FS + f
    barrier_to = group_targets(cfg, a, b, s)
    others = [(ka, kb) for ka in range(cfg.A) for kb in range(cfg.X) if ka or kb]
    far = lambda ka, kb: ((a + ka) % cfg.A, (b + kb) % cfg.X)
    for ka, kb in others:
        ta, tb = far(ka, kb)
        barrier_to.append(device(cfg, ta, zl, tb, f))
    greet(barrier_to)
    red = Reduce(cfg, co, part, *red_sc)
    red.start()

    def across(layer, o, z):
        src, dst = ((g1, b1), (g2, b2))[layer]
        ta, tb = far(*others[o])
        rows_ = src.at[pl.ds(flat(cfg, ta, z, tb, 0), cfg.FS)]
        return remote(rows_, dst.at[o, pl.ds(z * cfg.FS, cfg.FS)], ts[2 * layer].at[o, z], ts[2 * layer + 1].at[o, z], device(cfg, ta, zl, tb, f))

    for layer in (1, 0):
        for o in range(len(others)):
            for z in range(cfg.ZL):
                across(layer, o, z).start()
    ex_d = Exchange(cfg, co, lambda i: dir_low.at[pl.ds(i * cfg.T, cfg.T)], lambda i: dgot.at[:, pl.ds(pl.multiple_of(i * cfg.FW, 128), cfg.FW)], ds, dr)
    ex_h = Exchange(cfg, co, lambda i: hid_low.at[pl.ds(i * cfg.T, cfg.T)], lambda i: hid.at[:, pl.ds(pl.multiple_of(i * cfg.FW, 128), cfg.FW)], hs, hr)
    ex_d.start()
    ex_h.start()
    copies = [pltpu.make_async_copy(e.src(s), e.dst(s), own.at[i]) for i, e in enumerate((ex_d, ex_h))]
    for copy in copies:
        copy.start()
    red.middle()
    red.finish()
    ex_d.finish()
    for copy in copies:
        copy.wait()
    step = 64

    def body(i, carry):
        s0, s1 = carry
        at = pl.ds(pl.multiple_of(i * step, 8), step)
        value = red.total(at)
        z, inverse = normalize(x[at, :].astype(F32))
        h = value * vec[4:5, :]
        m0 = jnp.mean(h, axis=-1, keepdims=True)
        m1 = jnp.mean(h * z, axis=-1, keepdims=True)
        grad[at, :] = (h - m0 - z * m1) * inverse + dgot[at, :].astype(F32)
        return s0 + jnp.sum(value * z, axis=0, keepdims=True), s1 + jnp.sum(value, axis=0, keepdims=True)

    zero = jnp.zeros((1, cfg.D), F32)
    s0, s1 = lax.fori_loop(0, cfg.T // step, body, (zero, zero))
    sums[0:1, :] = s0
    sums[1:2, :] = s1
    ex_h.finish()
    for layer in (1, 0):
        for o in range(len(others)):
            for z in range(cfg.ZL):
                across(layer, o, z).wait()


def last(cfg, part, dir_low, hid_low, g1, g2, x, vec):
    n = cfg.A * cfg.X - 1
    got = jax.ShapeDtypeStruct((n, cfg.F, cfg.R, 3 * cfg.FW), BF)
    return pl.pallas_call(
        functools.partial(last_kernel, cfg),
        name="last",
        out_shape=(
            jax.ShapeDtypeStruct((cfg.T, cfg.D), F32),
            jax.ShapeDtypeStruct((cfg.T, cfg.D), BF),
            got,
            got,
            jax.ShapeDtypeStruct((8, cfg.D), F32),
        ),
        in_specs=[HBM] * 5 + [VM] * 2,
        out_specs=[VM, HBM, HBM, HBM, VM],
        scratch_shapes=[pltpu.VMEM((cfg.T, cfg.D), BF)]
        + reduce_scratch(cfg, cfg.T, cfg.D)
        + [DMA((2,))]
        + [DMA((cfg.F,))] * 4
        + [DMA((n, cfg.ZL))] * 4,
        compiler_params=pltpu.CompilerParams(collective_id=3, has_side_effects=True, vmem_limit_bytes=VMEM_CAP),
    )(part, dir_low, hid_low, g1, g2, x, vec)


def end_kernel(cfg, w1, w2, small, o1, o2, sg, own, small_send, small_recv, *sc):
    co = coords(cfg)
    a, zl, b, f = co
    s, me = zl * cfg.FS + f, flat(cfg, *co)
    greet_all(cfg, me)

    def pieces(layer, k):
        src, dst = ((w1, o1), (w2, o2))[layer]
        to = (s + k) % cfg.F
        for c in range(3):
            piece = src.at[to, :, pl.ds(c * cfg.FW, cfg.FW)]
            place = dst.at[:, pl.ds(pl.multiple_of(c * cfg.D + s * cfg.FW, 128), cfg.FW)]
            if k == 0:
                yield pltpu.make_async_copy(piece, place, own.at[layer, c])
            else:
                yield remote(piece, place, sc[2 * layer].at[k, c], sc[2 * layer + 1].at[k, c], member(cfg, a, b, to))

    every = [(layer, k) for layer in range(2) for k in range(cfg.F)]
    for layer, k in every:
        for copy in pieces(layer, k):
            copy.start()

    def each(k, _):
        m = (me + k) % cfg.N
        remote(small.at[m // cfg.PER], sg.at[me], small_send, small_recv, (m // cfg.FS, m % cfg.FS)).start()
        return 0

    lax.fori_loop(1, cfg.N, each, 0)
    mine = pltpu.make_async_copy(small.at[me // cfg.PER], sg.at[me], own.at[2, 0])
    mine.start()
    for layer, k in every:
        for copy in pieces(layer, k):
            copy.wait()
    mine.wait()
    everyone = sg.at[pl.ds(0, cfg.N - 1)]
    pltpu.make_async_copy(everyone, everyone, small_recv).wait()
    pltpu.make_async_copy(everyone, everyone, small_send).wait()


def end(cfg, w1, w2, small):
    out = jax.ShapeDtypeStruct((cfg.R, 3 * cfg.D), BF)
    return pl.pallas_call(
        functools.partial(end_kernel, cfg),
        name="end",
        out_shape=(out, out, jax.ShapeDtypeStruct((cfg.N,) + small.shape[1:], F32)),
        in_specs=[HBM] * 3,
        out_specs=[HBM] * 3,
        scratch_shapes=[DMA((3, 3)), DMA(()), DMA(())] + [DMA((cfg.F, 3))] * 4,
        compiler_params=pltpu.CompilerParams(collective_id=4, has_side_effects=True),
    )(w1, w2, small)


def wgrad(cfg, low, grads):
    out = lax.dot_general(low.reshape(cfg.M, cfg.D), grads, (((0,), (0,)), ((), ())), preferred_element_type=F32)
    return out.astype(BF).reshape(cfg.N, cfg.R, 3 * cfg.FW)


def own_sum(cfg, g, got, a, b):
    mine = lax.dynamic_index_in_dim(lax.dynamic_index_in_dim(g.reshape(cfg.A, cfg.ZL, cfg.X, cfg.FS, cfg.R, 3 * cfg.FW), a, 0, False), b, 1, False)
    mine = mine.reshape(cfg.F, cfg.R, 3 * cfg.FW)
    return (mine.astype(F32) + jnp.sum(got.astype(F32), axis=0)).astype(BF)


CHUNKS = 4


class Square:
    def __init__(self, cfg, co):
        self.cfg, self.co = cfg, co
        a, zl, b, f = co
        y, self.core = f // 2, f % 2
        self.cells = [(zl, y), (zl, 1 - y), (1 - zl, y), (1 - zl, 1 - y)]
        self.s = zl * cfg.FS + f

    def index(self, k, mate=False):
        zl, y = self.cells[k]
        return zl * self.cfg.FS + y * 2 + ((1 - self.core) if mate else self.core)

    def place(self, k, mate=False):
        a, _, b, _ = self.co
        zl, y = self.cells[k]
        return device(self.cfg, a, zl, b, y * 2 + ((1 - self.core) if mate else self.core))


class SquareGather:
    def __init__(self, sq, slot, by_y, sems, src=None):
        self.sq, self.slot, self.by_y = sq, slot, by_y
        self.src = src or (lambda c: slot(sq.s, c))
        self.ns, self.nr, self.fs, self.fr, self.ms, self.mr = sems

    def side(self, k, c):
        sq = self.sq
        return remote(self.src(c), self.slot(sq.s, c), self.ns.at[k, c], self.nr.at[k, c], sq.place(k))

    def across(self, c):
        sq = self.sq
        cfg, (a, zl, b, f) = sq.cfg, sq.co
        y, v = f // 2, self.by_y(c)
        via = (zl + (1 - v) * (1 - 2 * zl)) * cfg.FS + (y + v * (1 - 2 * y)) * 2 + sq.core
        to = device(cfg, a, zl + v * (1 - 2 * zl), b, (y + (1 - v) * (1 - 2 * y)) * 2 + sq.core)
        block = self.slot(via, c)
        return remote(block, block, self.fs.at[c], self.fr.at[c], to)

    def near(self, k, c):
        sq = self.sq
        block = self.slot(sq.index(k), c)
        return remote(self.src(c) if k == 0 else block, block, self.ms.at[k, c], self.mr.at[k, c], sq.place(0, True))

    def push(self, c):
        self.side(1, c).start()
        self.side(2, c).start()
        self.near(0, c).start()

    def arrive(self, c):
        self.side(1, c).wait_recv()
        self.side(2, c).wait_recv()
        self.across(c).start()
        self.near(1, c).start()
        self.near(2, c).start()

    def complete(self, c):
        self.across(c).wait_recv()
        self.near(3, c).start()
        for k in range(4):
            self.near(k, c).wait_recv()

    def drain(self):
        def one(c, _):
            self.side(1, c).wait_send()
            self.side(2, c).wait_send()
            self.across(c).wait_send()
            for k in range(4):
                self.near(k, c).wait_send()
            return 0

        lax.fori_loop(0, CHUNKS, one, 0)


def gather_sems():
    return [DMA((3, CHUNKS))] * 2 + [DMA((CHUNKS,))] * 2 + [DMA((4, CHUNKS))] * 2


class SquareReduce:
    def __init__(self, sq, to_mate, own, mate, landed, gy, gz, sems):
        self.sq, self.to_mate, self.own, self.mate = sq, to_mate, own, mate
        self.landed, self.got = landed, (None, gy, gz)
        self.ms, self.mr, self.ds, self.dr, self.gs, self.gr = sems
        self.rows = own.shape[1] // CHUNKS

    def at(self, c):
        return pl.ds(c * self.rows, self.rows)

    def near(self, k, c):
        return remote(self.to_mate.at[k, self.at(c)], self.mate.at[k, self.at(c)], self.ms.at[k, c], self.mr.at[k, c], self.sq.place(0, True))

    def far(self, c):
        return remote(self.own.at[3, self.at(c)], self.landed.at[self.at(c)], self.ds.at[c], self.dr.at[c], self.sq.place(1 + c % 2))

    def side(self, k, c):
        return remote(self.own.at[k, self.at(c)], self.got[k].at[self.at(c)], self.gs.at[k, c], self.gr.at[k, c], self.sq.place(k))

    def add(self, k, c, other):
        step = 64 if self.own.shape[2] > 512 else 256

        def body(i, _):
            at = pl.ds(pl.multiple_of(c * self.rows + i * step, 8), step)
            value = other[k, at, :] if len(other.shape) == 3 else other[at, :]
            self.own[k, at, :] = (self.own[k, at, :].astype(F32) + value.astype(F32)).astype(BF)
            return 0

        lax.fori_loop(0, self.rows // step, body, 0)

    def run(self, product):
        order = (3, 1, 2, 0)

        def settle(k):
            for c in range(CHUNKS):
                self.near(k, c).wait_recv()
                if k:
                    self.add(k, c, self.mate)
                if k == 3:
                    self.far(c).start()
                elif k and c % 2 == k - 1:
                    self.side(k, c).start()

        for n, k in enumerate(order):
            product(self.sq.index(k, True), self.to_mate.at[k])
            for c in range(CHUNKS):
                self.near(k, c).start()
            product(self.sq.index(k), self.own.at[k])
            settle(k)

    def pass_on(self):
        for c in range(CHUNKS):
            k = 2 - c % 2
            self.far(c).wait_recv()
            self.add(k, c, self.landed)
            self.side(k, c).start()

    def receive(self, c):
        self.side(1, c).wait_recv()
        self.side(2, c).wait_recv()

    def total(self, at):
        value = self.own[0, at, :].astype(F32) + self.mate[0, at, :].astype(F32)
        return value + self.got[1][at, :].astype(F32) + self.got[2][at, :].astype(F32)

    def drain(self):
        for c in range(CHUNKS):
            for k in range(4):
                self.near(k, c).wait_send()
            self.far(c).wait_send()
            self.side(1, c).wait_send()
            self.side(2, c).wait_send()


def reduce_parts(rows_, cols):
    return [pltpu.VMEM((4, rows_, cols), BF)] * 3 + [pltpu.VMEM((rows_, cols), BF)] * 3


def reduce_sems():
    return [DMA((4, CHUNKS))] * 2 + [DMA((CHUNKS,))] * 2 + [DMA((3, CHUNKS))] * 2


PIECES = 4


class LineGather(WeightGather):
    def __init__(self, cfg, co, w, full, own, send, recv, rs, rr, ls, lr):
        super().__init__(cfg, co, w, full, own, send, recv, None, None, None, None)
        self.rs, self.rr, self.ls, self.lr = rs, rr, ls, lr
        self.a = co[0]

    def unit(self, a, p):
        count = self.cfg.F // PIECES
        return self.full.at[pl.ds(a * self.cfg.F + p * count, count)]

    def move(self, way, i, p):
        cfg, (a, zl, b, f) = self.cfg, self.co
        block = self.unit((a - way * i + cfg.A) % cfg.A, p)
        send, recv = (self.rs, self.rr) if way == 1 else (self.ls, self.lr)
        return remote(block, block, send.at[i, p], recv.at[i, p], device(cfg, (a + way + cfg.A) % cfg.A, zl, b, f))

    def landing(self, way, i, p):
        cfg, (a, zl, b, f) = self.cfg, self.co
        block = self.unit((a - way * (i + 1) + cfg.A) % cfg.A, p)
        send, recv = (self.rs, self.rr) if way == 1 else (self.ls, self.lr)
        return remote(block, block, send.at[i, p], recv.at[i, p], device(cfg, (a + way + cfg.A) % cfg.A, zl, b, f))

    def behind(self, way):
        return self.a if way == 1 else self.cfg.A - 1 - self.a

    def start_line(self):
        for p in range(PIECES):
            for way in (1, -1):
                pl.when(self.behind(-way) > 0)(lambda way=way, p=p: self.move(way, 0, p).start())

    def forward(self, i, p):
        for way in (1, -1):

            @pl.when(self.behind(way) >= i)
            def _():
                self.landing(way, i - 1, p).wait_recv()
                if i < self.cfg.A - 1:
                    pl.when(self.behind(-way) > 0)(lambda: self.move(way, i, p).start())

    def finish(self):
        for i in range(self.cfg.A - 1):
            for p in range(PIECES):
                for way in (1, -1):
                    there = (self.behind(way) >= i) & (self.behind(-way) > 0)
                    pl.when(there)(lambda way=way, i=i, p=p: self.move(way, i, p).wait_send())


def line_sems(cfg):
    return [DMA((3,)), DMA((cfg.F, 3)), DMA((cfg.F, 3))] + [DMA((cfg.A - 1, PIECES))] * 4


class LineSum:
    def __init__(self, cfg, co, gw, land, rs, rr, ls, lr):
        self.cfg, self.co, self.gw, self.land = cfg, co, gw, land
        self.rs, self.rr, self.ls, self.lr = rs, rr, ls, lr
        self.a = co[0]
        self.count = cfg.F // PIECES

    def behind(self, way):
        return self.a if way == 1 else self.cfg.A - 1 - self.a

    def slots(self, t, p):
        return pl.ds(t * self.cfg.F + p * self.count, self.count)

    def move(self, way, t, p):
        cfg, (a, zl, b, f) = self.cfg, self.co
        send, recv, at = (self.rs, self.rr, t + 1) if way == 1 else (self.ls, self.lr, t)
        to = device(cfg, (a + way + cfg.A) % cfg.A, zl, b, f)
        return remote(self.gw.at[self.slots(t, p)], self.land.at[at, pl.ds(p * self.count, self.count)], send.at[t, p], recv.at[t, p], to)

    def landed(self, way, t, p):
        return self.land[t + 1 if way == 1 else t, pl.ds(p * self.count, self.count)]

    def each(self, todo, distances):
        for d in distances:
            for way in (1, -1):
                pl.when(self.behind(-way) >= d)(lambda d=d, way=way: todo(way, self.a + way * d))

    def produce(self, block, begin, end):
        cfg = self.cfg

        def make(t):
            def body(h, _):
                block(t * cfg.F + h * cfg.FS)
                return 0

            lax.fori_loop(0, cfg.ZL, body, 0)

        far = cfg.A - 1

        def one(n, _):
            d = far - n // 2
            way = 1 - 2 * (n % 2)
            t = self.a + way * d

            @pl.when((t >= 0) & (t < cfg.A) & (n < 2 * far))
            def _():
                make(t)
                for w in (1, -1):

                    @pl.when((self.behind(w) == 0) & (way == w))
                    def _():
                        for p in range(PIECES):
                            self.move(w, t, p).start()

            pl.when(n == 2 * far)(lambda: make(self.a))
            return 0

        lax.fori_loop(begin, end, one, 0)

    def pump(self, distances):
        def todo(way, t):
            @pl.when(self.behind(way) > 0)
            def _():
                def body(p, _):
                    self.move(way, t, p).wait_recv()
                    at = self.slots(t, p)
                    self.gw[at] = (self.gw[at].astype(F32) + self.landed(way, t, p).astype(F32)).astype(BF)
                    self.move(way, t, p).start()
                    return 0

                lax.fori_loop(0, PIECES, body, 0)

        self.each(todo, distances)

    def settle(self, out, then=lambda p: None):
        def body(p, _):
            mine = self.gw[self.slots(self.a, p)].astype(F32)
            to = pl.ds(p * self.count, self.count)
            for way in (1, -1):
                pl.when(self.behind(way) > 0)(lambda way=way: self.move(way, self.a, p).wait_recv())
            for low, high in ((0, 1), (1, 0), (1, 1)):

                @pl.when(((self.behind(1) > 0) == (low == 1)) & ((self.behind(-1) > 0) == (high == 1)))
                def _():
                    value = mine
                    if low:
                        value = value + self.landed(1, self.a, p).astype(F32)
                    if high:
                        value = value + self.landed(-1, self.a, p).astype(F32)
                    out[to] = value.astype(BF)

            then(p)
            return 0

        lax.fori_loop(0, PIECES, body, 0)

    def drain(self):
        def todo(way, t):
            for p in range(PIECES):
                self.move(way, t, p).wait_send()

        self.each(todo, range(1, self.cfg.A))


def line_parts(cfg):
    cols = 3 * cfg.FW
    return [pltpu.VMEM((cfg.N, cfg.R, cols), BF), pltpu.VMEM((cfg.A + 1, cfg.F, cfg.R, cols), BF)]


def line_sum_sems(cfg):
    return [DMA((cfg.A, PIECES))] * 4


def weight_rows(cfg, w, first, count):
    return w[pl.ds(first, count)].reshape(count * cfg.R, 3 * cfg.FW)


def grad_block(cfg, low, grads, gw):
    def block(first):
        slots = pl.ds(first, cfg.FS)
        columns = pl.ds(pl.multiple_of(first * cfg.R, 128), cfg.FS * cfg.R)
        data = low[:, :, columns].reshape(cfg.M, cfg.FS * cfg.R)
        out = lax.dot_general(data, grads[...], (((0,), (0,)), ((), ())), preferred_element_type=F32)
        gw[slots] = out.astype(BF).reshape(cfg.FS, cfg.R, 3 * cfg.FW)

    return block


def multiply_chunk(cfg, low, w, proj, c):
    n = cfg.T // CHUNKS
    data = low[:, pl.ds(pl.multiple_of(c * n, 16), n), :].reshape(cfg.S * n, cfg.D)
    out = jnp.dot(data, w[...].reshape(cfg.D, 3 * cfg.FW), preferred_element_type=F32)
    for i in range(cfg.S):
        to = pl.ds(pl.multiple_of(i * cfg.TP + c * n, 8), n)
        for l in range(3 * cfg.L):
            proj[l, to, :] = out[i * n : (i + 1) * n, 128 * l : 128 * l + 128]


def multiply_units(cfg, low, w, proj, c, first, count, more):
    n, k = cfg.T // CHUNKS, cfg.F * cfg.R
    depth = pl.ds(pl.multiple_of(first * k, 128), count * k)
    data = low[:, pl.ds(pl.multiple_of(c * n, 16), n), depth].reshape(cfg.S * n, count * k)
    out = jnp.dot(data, weight_rows(cfg, w, first * cfg.F, count * cfg.F), preferred_element_type=F32)
    for i in range(cfg.S):
        to = pl.ds(pl.multiple_of(i * cfg.TP + c * n, 8), n)
        for l in range(3 * cfg.L):
            value = out[i * n : (i + 1) * n, 128 * l : 128 * l + 128]
            proj[l, to, :] = proj[l, to, :] + value if more else value


def scan_chunk(cfg, proj, inp, vec, base, lens, hid, states, tf_ref, tr_ref, carry, c):
    half_pf, half_pr = 0.5 * wide(cfg, vec, base), 0.5 * wide(cfg, vec, base + 1)
    half_bf, half_br = 0.5 * wide(cfg, vec, base + 2), 0.5 * wide(cfg, vec, base + 3)
    live = jnp.broadcast_to(lens[:, 0:1], (cfg.S, cfg.FW))
    n = cfg.T // CHUNKS

    def step(i, state):
        t = c * n + i
        u, p, q = (rows(cfg, proj, t, j * cfg.L, cfg.L) for j in range(3))
        here = rows(cfg, inp, t, 0, cfg.L)
        p, q, hu, hc = 0.5 * p + half_bf, 0.5 * q + half_br, 0.5 * u, 0.5 * state
        tf = jnp.tanh(p + half_pf * state)
        tr = jnp.tanh(q + half_pr * state)
        new = (hc + hu) + tf * (hc - hu)
        out = jnp.where(t < live, 0.5 * (here + new) + 0.5 * tr * (new - here), 0.0)
        put(cfg, hid, t, out)
        put(cfg, states, t, new)
        put(cfg, tf_ref, t, tf)
        put(cfg, tr_ref, t, tr)
        return new

    carry[...] = lax.fori_loop(0, n, step, carry[...], unroll=4)


def forward_kernel(cfg, *refs):
    refs = list(refs)

    def take(n):
        out = refs[:n]
        del refs[:n]
        return out

    x, cot, w1, w2, small = take(5)
    low1_out, low2_out, f1_out, f2_out, saved, vec, mine, lens, zo_out, inv_out, hid_out, p_out, dir_out, sums = take(14)
    xg, hg, low, f1, f2, sg, cg, proj, inp, states, tf, tr, hid, direct, hid_low, p_low, z_own, inv, carry = take(19)
    own_sem, small_send, small_recv, cs, cr, flush = take(6)
    xsems, hsems, w1sems, w2sems = take(6), take(6), take(7), take(7)
    co = coords(cfg)
    a, zl, b, f = co
    sq = Square(cfg, co)
    s, me = sq.s, flat(cfg, *co)
    rows_c = cfg.T // CHUNKS
    cols = lambda i: pl.ds(pl.multiple_of(i * cfg.FW, 128), cfg.FW)
    greet_all(cfg, me)
    one = LineGather(cfg, co, w1, f1, *w1sems)
    two = LineGather(cfg, co, w2, f2, *w2sems)
    one.start()

    def each(k, _):
        m = (me + k) % cfg.N
        remote(small, sg.at[me], small_send, small_recv, (m // cfg.FS, m % cfg.FS)).start()
        return 0

    lax.fori_loop(1, cfg.N, each, 0)
    part = lambda c: pl.ds(pl.multiple_of(c * rows_c, 16), rows_c)
    xgather = SquareGather(sq, lambda i, c: xg.at[i, part(c)], lambda c: 1 - c % 2, xsems, lambda c: x.at[part(c)])
    hgather = SquareGather(sq, lambda i, c: hg.at[:, part(c), cols(i)], lambda c: 1 - c % 2, hsems)
    two.start()
    for c in range(CHUNKS):
        xgather.push(c)
    exchange = Exchange(cfg, co, lambda i: cot.at[:, cols(i)], lambda i: cg.at[i], cs, cr)
    local = [
        pltpu.make_async_copy(x, xg.at[s], own_sem.at[0]),
        pltpu.make_async_copy(cot.at[:, cols(s)], cg.at[s], own_sem.at[1]),
        pltpu.make_async_copy(small, sg.at[me], own_sem.at[2]),
    ]
    for copy in local:
        copy.start()

    everyone = sg.at[pl.ds(0, cfg.N - 1)]
    def norm_one(c):
        def body(i, _):
            two_of = pl.ds(2 * i, 2)
            z, _ = normalize(xg[two_of, part(c), :].reshape(2 * rows_c, cfg.D).astype(F32))
            low[two_of, part(c), :] = (z * vec[4:5, :] + vec[5:6, :]).astype(BF).reshape(2, rows_c, cfg.D)
            for h in range(2):
                own = xg[2 * i + h, part(c), cols(s)].astype(F32)
                to = pl.ds(pl.multiple_of((2 * i + h) * cfg.TP + c * rows_c, 8), rows_c)
                for l in range(cfg.L):
                    inp[l, to, :] = own[:, 128 * l : 128 * l + 128]
            return 0

        lax.fori_loop(0, cfg.S // 2, body, 0)

    def norm_two(c):
        def body(i, _):
            two_of = pl.ds(2 * i, 2)
            data = hg[two_of, part(c), :].reshape(2 * rows_c, cfg.D).astype(F32)
            mean = jnp.mean(data, axis=-1, keepdims=True)
            center = data - mean
            inverse = lax.rsqrt(jnp.mean(center * center, axis=-1, keepdims=True) + EPSILON)
            low[two_of, part(c), :] = (center * inverse * vec[10:11, :] + vec[11:12, :]).astype(BF).reshape(2, rows_c, cfg.D)
            own = (hg[two_of, part(c), cols(s)].reshape(2 * rows_c, cfg.FW).astype(F32) - mean) * inverse
            for h in range(2):
                at = pl.ds(pl.multiple_of((2 * i + h) * cfg.T + c * rows_c, 8), rows_c)
                inv[at, :] = jnp.broadcast_to(inverse[h * rows_c : (h + 1) * rows_c], (rows_c, 128))
                z_own[at, :] = own[h * rows_c : (h + 1) * rows_c]
            return 0

        lax.fori_loop(0, cfg.S // 2, body, 0)

    def hidden_chunk(c):
        for i in range(cfg.S):
            to = pl.ds(pl.multiple_of(i * cfg.TP + c * rows_c, 8), rows_c)
            for l in range(cfg.L):
                hg[i, part(c), pl.ds(pl.multiple_of(s * cfg.FW + 128 * l, 128), 128)] = hid[l, to, :].astype(BF)

    keep_low1 = pltpu.make_async_copy(low, low1_out, flush.at[0])
    keep_f1 = pltpu.make_async_copy(f1, f1_out, flush.at[1])
    keeps = [
        pltpu.make_async_copy(ref if n != 1 else proj.at[pl.ds(0, cfg.L)], saved.at[pl.ds(n * cfg.L, cfg.L)], flush.at[2 + n])
        for n, ref in enumerate((inp, None, states, tf, tr))
    ]
    carry[...] = jnp.zeros_like(carry)
    one.middle()
    one.start_line()
    pltpu.make_async_copy(everyone, everyone, small_recv).wait()
    for copy in local:
        copy.wait()
    for i in range(cfg.N // cfg.PER):
        total = sg[i * cfg.PER].astype(F32)
        for p in range(1, cfg.PER):
            total = total + sg[i * cfg.PER + p].astype(F32)
        vec[:, 128 * i : 128 * i + 128] = total
    mine[...] = vec[:, cols(s)]
    for i in range(cfg.S):
        n = flat(cfg, a, i // cfg.FS, b, i % cfg.FS)
        length = jnp.max(sg[n].astype(F32)[12:13, :], axis=-1, keepdims=True)
        lens[i : i + 1, :] = jnp.broadcast_to(length, (1, 128)).astype(jnp.int32)

    xgather.arrive(0)
    one.forward(1, 0)
    one.forward(1, 1)
    xgather.arrive(1)
    one.forward(1, 2)
    one.forward(1, 3)
    xgather.arrive(2)
    one.forward(2, 0)
    xgather.arrive(3)
    one.forward(2, 1)
    one.forward(2, 2)
    one.forward(2, 3)
    two.middle()
    two.start_line()
    exchange.start()

    def layer_one(k, _):
        @pl.when(k < CHUNKS)
        def _():
            xgather.complete(k)
            norm_one(k)

            @pl.when(k == 3)
            def _():
                keep_low1.start()
                for p in range(PIECES):
                    one.forward(3, p)
                keep_f1.start()

        @pl.when(k >= CHUNKS - 1)
        def _():
            c = k - (CHUNKS - 1)
            multiply_chunk(cfg, low, f1, proj, c)
            scan_chunk(cfg, proj, inp, mine, 0, lens, hid, states, tf, tr, carry, c)
            hidden_chunk(c)
            hgather.push(c)
            pl.when(c > 0)(lambda: hgather.arrive(c - 1))
            two.forward(1, c)

        return 0

    lax.fori_loop(0, 2 * CHUNKS - 1, layer_one, 0)
    for copy in keeps:
        copy.start()
    carry[...] = jnp.zeros_like(carry)
    hgather.arrive(CHUNKS - 1)
    two.forward(2, 0)
    two.forward(2, 1)
    keep_low1.wait()

    for copy in keeps:
        copy.wait()
    end_unit = a // (cfg.A - 1)
    at_end = (a == 0) | (a == cfg.A - 1)

    def layer_two(k, _):
        hgather.complete(k)
        norm_two(k)

        @pl.when(k == 0)
        def _():
            two.forward(2, 2)
            two.forward(2, 3)

        @pl.when(at_end)
        def _():
            multiply_units(cfg, low, f2, proj, k, end_unit, cfg.A - 1, False)

        @pl.when(jnp.logical_not(at_end))
        def _():
            multiply_units(cfg, low, f2, proj, k, 0, cfg.A, False)

        return 0

    lax.fori_loop(0, CHUNKS, layer_two, 0)
    for p in range(PIECES):
        two.forward(3, p)

    def layer_two_scan(k, _):
        @pl.when(at_end)
        def _():
            multiply_units(cfg, low, f2, proj, k, (cfg.A - 1) * (1 - end_unit), 1, True)

        scan_chunk(cfg, proj, hid, mine, 6, lens, inp, states, tf, tr, carry, k)
        return 0

    lax.fori_loop(0, CHUNKS, layer_two_scan, 0)
    outs = [
        pltpu.make_async_copy(low, low2_out, flush.at[0]),
        pltpu.make_async_copy(z_own, zo_out, flush.at[7]),
        pltpu.make_async_copy(inv, inv_out, flush.at[8]),
        pltpu.make_async_copy(f2, f2_out, flush.at[9]),
    ]
    for copy in outs:
        copy.start()
    hgather.drain()
    one.finish()
    two.finish()
    narrow(cfg, inp, hid_low, cfg.L)
    outs.append(pltpu.make_async_copy(hid_low, hid_out, flush.at[10]))
    outs[-1].start()
    exchange.finish()
    for i in range(cfg.S):
        g = cg[i].astype(F32)
        for l in range(cfg.L):
            inp[l, i * cfg.TP : i * cfg.TP + cfg.T, :] = g[:, 128 * l : 128 * l + 128]
    scan_backward(cfg, proj, hid, mine, 6, lens, states, tf, tr, inp, proj, direct, sums)
    narrow(cfg, proj, p_low, 3 * cfg.L)
    outs.append(pltpu.make_async_copy(p_low, p_out, flush.at[11]))
    outs.append(pltpu.make_async_copy(direct, dir_out, flush.at[12]))
    for copy in outs[-2:]:
        copy.start()
    xgather.drain()
    pltpu.make_async_copy(everyone, everyone, small_send).wait()
    keep_f1.wait()
    for copy in outs:
        copy.wait()


def forward(cfg, x, cot, w1, w2, small):
    low = jax.ShapeDtypeStruct((cfg.S, cfg.T, cfg.D), BF)
    full = jax.ShapeDtypeStruct((cfg.N, cfg.R, 3 * cfg.FW), BF)
    state = keep(cfg, cfg.L)
    vm = lambda t: pltpu.VMEM(t.shape, t.dtype)
    shape = jax.ShapeDtypeStruct
    outs = [
        (low, HBM), (low, HBM), (full, HBM), (full, HBM), (keep(cfg, 5 * cfg.L), HBM),
        (shape((16, cfg.D), F32), VM), (shape((16, cfg.FW), F32), VM), (shape((cfg.S, 128), jnp.int32), VM),
        (shape((cfg.M, cfg.FW), F32), HBM), (shape((cfg.M, 128), F32), HBM), (shape((cfg.M, cfg.FW), BF), HBM),
        (shape((cfg.M, 3 * cfg.FW), BF), HBM), (state, HBM), (shape((8, cfg.FW), F32), VM),
    ]
    return pl.pallas_call(
        functools.partial(forward_kernel, cfg),
        name="forward",
        out_shape=[o for o, _ in outs],
        in_specs=[HBM] * 5,
        out_specs=[p for _, p in outs],
        scratch_shapes=[
            vm(low), vm(low), vm(low), vm(full), vm(full), pltpu.VMEM((cfg.N, 16, 128), BF), pltpu.VMEM((cfg.S, cfg.T, cfg.FW), BF),
            vm(keep(cfg, 3 * cfg.L)),
        ]
        + [vm(state)] * 6
        + [pltpu.VMEM((cfg.M, cfg.FW), BF), pltpu.VMEM((cfg.M, 3 * cfg.FW), BF), pltpu.VMEM((cfg.M, cfg.FW), F32), pltpu.VMEM((cfg.M, 128), F32), pltpu.VMEM((cfg.S, cfg.FW), F32)]
        + [DMA((4,)), DMA(()), DMA(()), DMA((cfg.F,)), DMA((cfg.F,)), DMA((13,))]
        + gather_sems() * 2
        + line_sems(cfg) * 2,
        compiler_params=pltpu.CompilerParams(collective_id=5, has_side_effects=True, vmem_limit_bytes=VMEM_CAP),
    )(x, cot, w1, w2, small)


def inner_kernel(cfg, *refs):
    refs = list(refs)

    def take(n):
        out = refs[:n]
        del refs[:n]
        return out

    p_in, f2_in, low_in, zo_in, inv_in, dir_in, saved, hid_low, mine, lens = take(10)
    p_out, dlow_out, land, hid, norms, sums = take(6)
    p, w, low, z_own, inv, direct, inp, states, tf, tr, proj, grad, ng, stats, mean, group_sum = take(16)
    red_parts, t_parts = take(6), take(2)
    load, ss, sr, hs, hr, s2, r2 = take(7)
    red_sems, t_sems = take(6), take(4)
    co = coords(cfg)
    a, zl, b, f = co
    sq = Square(cfg, co)
    s = sq.s
    cols = lambda i: pl.ds(pl.multiple_of(i * cfg.FW, 128), cfg.FW)
    loads = [pltpu.make_async_copy(src, dst, load.at[n]) for n, (src, dst) in enumerate((
        (p_in, p), (low_in, low), (f2_in, w), (zo_in, z_own), (inv_in, inv), (dir_in, direct),
        (saved.at[pl.ds(0, cfg.L)], inp), (saved.at[pl.ds(cfg.L, cfg.L)], proj.at[pl.ds(0, cfg.L)]),
        (saved.at[pl.ds(2 * cfg.L, cfg.L)], states), (saved.at[pl.ds(3 * cfg.L, cfg.L)], tf), (saved.at[pl.ds(4 * cfg.L, cfg.L)], tr),
    ))]
    for copy in loads:
        copy.start()
    greet(group_targets(cfg, a, b, s) + t_targets(cfg, co))
    red = SquareReduce(sq, *red_parts, red_sems)
    tsum = LineSum(cfg, co, *t_parts, *t_sems)
    loads[0].wait()
    loads[1].wait()

    def product(i, out):
        block = weight_rows(cfg, w, i * (cfg.FW // cfg.R), cfg.FW // cfg.R)

        def body(n, _):
            at = pl.ds(pl.multiple_of(n * 512, 8), 512)
            out[at, :] = lax.dot_general(p[at, :], block, (((1,), (1,)), ((), ())), preferred_element_type=F32).astype(BF)
            return 0

        lax.fori_loop(0, cfg.M // 512, body, 0)

    block_of = grad_block(cfg, low, p, t_parts[0])
    tsum.produce(block_of, 0, 4)
    loads[2].wait()
    red.run(product)
    tsum.produce(block_of, 4, 7)
    tsum.pump((2,))
    red.pass_on()
    ex_h = Exchange(cfg, co, lambda i: hid_low.at[pl.ds(i * cfg.T, cfg.T)], lambda i: hid.at[:, cols(i)], hs, hr)
    ex_h.start()
    own_hid = pltpu.make_async_copy(ex_h.src(s), ex_h.dst(s), load.at[11])
    own_hid.start()
    tsum.pump((1,))
    for copy in loads[3:]:
        copy.wait()
    gain = mine[10:11, :]
    eye = (lax.broadcasted_iota(jnp.int32, (128, 128), 0) == lax.broadcasted_iota(jnp.int32, (128, 128), 1)).astype(F32)

    def first_pass(i, carry):
        s0, s1 = carry
        at = pl.ds(pl.multiple_of(i * 128, 8), 128)
        value = red.total(at)
        z = z_own[at, :]
        h = value * gain
        ng[at, :] = h
        for n, x in ((0, h), (1, h * z)):
            col = jnp.sum(x, axis=-1, keepdims=True)
            stats[s, n, pl.ds(i, 1), :] = jnp.sum(col * eye, axis=0, keepdims=True)
        return s0 + jnp.sum(value * z, axis=0, keepdims=True), s1 + jnp.sum(value, axis=0, keepdims=True)

    zero = jnp.zeros((1, cfg.FW), F32)
    carry = (zero, zero)
    per = cfg.M // 128 // CHUNKS
    for c in range(CHUNKS):
        red.receive(c)
        carry = lax.fori_loop(c * per, (c + 1) * per, first_pass, carry)
    norms[0:1, :] = carry[0]
    norms[1:2, :] = carry[1]
    exchange = Exchange(cfg, co, lambda i: stats.at[s], lambda i: stats.at[i], ss, sr)
    exchange.start()
    exchange.finish()
    total = stats[0]
    for i in range(1, cfg.F):
        total = total + stats[i]
    mean[...] = total * (1.0 / cfg.D)

    def second_pass(i, _):
        at = pl.ds(pl.multiple_of(i * 128, 8), 128)
        m0 = jnp.sum(mean[0, pl.ds(i, 1), :] * eye, axis=-1, keepdims=True)
        m1 = jnp.sum(mean[1, pl.ds(i, 1), :] * eye, axis=-1, keepdims=True)
        value = (ng[at, :] - m0 - z_own[at, :] * m1) * inv[at, 0:1]
        each = cfg.T // 128
        to = pl.ds(pl.multiple_of((i // each) * cfg.TP + (i % each) * 128, 8), 128)
        for l in range(cfg.L):
            grad[l, to, :] = value[:, 128 * l : 128 * l + 128] + direct[l, to, :]
        return 0

    lax.fori_loop(0, cfg.M // 128, second_pass, 0)
    ex_2 = Exchange(cfg, co, lambda i: group_sum.at[i], lambda i: land.at[i], s2, r2)
    tsum.settle(group_sum, ex_2.piece_sender(PIECES))
    own_sum = pltpu.make_async_copy(group_sum.at[s], land.at[s], load.at[2])
    own_sum.start()
    scan_backward(cfg, proj, inp, mine, 0, lens, states, tf, tr, grad, proj, direct, sums)
    narrow(cfg, proj, p, 3 * cfg.L)
    outs = [pltpu.make_async_copy(p, p_out, load.at[0])]
    outs[0].start()
    red.drain()
    dlow = red_parts[0].at[0]
    narrow(cfg, direct, dlow, cfg.L)
    outs.append(pltpu.make_async_copy(dlow, dlow_out, load.at[1]))
    outs[1].start()
    ex_2.finish()
    own_sum.wait()
    ex_h.finish()
    own_hid.wait()
    tsum.drain()
    for copy in outs:
        copy.wait()


def inner(cfg, p, f2, low, zo, inv, direct, saved, hid_low, mine, lens):
    shape = jax.ShapeDtypeStruct
    state = keep(cfg, cfg.L)
    vm = lambda t: pltpu.VMEM(t.shape, t.dtype)
    part = shape((cfg.F, cfg.R, 3 * cfg.FW), BF)
    return pl.pallas_call(
        functools.partial(inner_kernel, cfg),
        name="inner",
        out_shape=[shape((cfg.M, 3 * cfg.FW), BF), shape((cfg.M, cfg.FW), BF), part, shape((cfg.T, cfg.D), BF), shape((8, cfg.FW), F32), shape((8, cfg.FW), F32)],
        in_specs=[HBM] * 8 + [VM] * 2,
        out_specs=[HBM] * 4 + [VM] * 2,
        scratch_shapes=[vm(p), vm(f2), vm(low), vm(zo), vm(inv)]
        + [vm(state)] * 5
        + [vm(keep(cfg, 3 * cfg.L)), vm(state), pltpu.VMEM((cfg.M, cfg.FW), F32)]
        + [pltpu.VMEM((cfg.F, 2, cfg.M // 128, 128), F32), pltpu.VMEM((2, cfg.M // 128, 128), F32), vm(part)]
        + reduce_parts(cfg.M, cfg.FW)
        + line_parts(cfg)
        + [DMA((12,))] + [DMA((cfg.F,))] * 6
        + reduce_sems()
        + line_sum_sems(cfg),
        compiler_params=pltpu.CompilerParams(collective_id=6, has_side_effects=True, vmem_limit_bytes=VMEM_CAP),
    )(p, f2, low, zo, inv, direct, saved, hid_low, mine, lens)


def final_kernel(cfg, *refs):
    refs = list(refs)

    def take(n):
        out = refs[:n]
        del refs[:n]
        return out

    p_in, f1_in, low_in, dlow, sum2, x, vec, sums1, sums2, norm2 = take(10)
    grad, o1, o2, total = take(4)
    p, w, low, dgot, land1, land2, group_sum, small, sg = take(9)
    red_parts, t_parts = take(6), take(2)
    load, small_send, small_recv, ds, dr, s1, r1 = take(7)
    red_sems, t_sems = take(6), take(4)
    co = coords(cfg)
    a, zl, b, f = co
    sq = Square(cfg, co)
    s, me = sq.s, flat(cfg, *co)
    cols = lambda i: pl.ds(pl.multiple_of(i * cfg.FW, 128), cfg.FW)
    loads = [pltpu.make_async_copy(src, dst, load.at[n]) for n, (src, dst) in enumerate(((p_in, p), (low_in, low), (f1_in, w)))]
    for copy in loads:
        copy.start()
    greet_all(cfg, me)
    red = SquareReduce(sq, *red_parts, red_sems)
    ex_d = Exchange(cfg, co, lambda i: dlow.at[pl.ds(i * cfg.T, cfg.T)], lambda i: dgot.at[:, cols(i)], ds, dr)
    ex_d.start()
    copies = [pltpu.make_async_copy(ex_d.src(s), ex_d.dst(s), load.at[3]), pltpu.make_async_copy(sum2, land2, load.at[4])]
    for copy in copies:
        copy.start()
    tsum = LineSum(cfg, co, *t_parts, *t_sems)
    loads[0].wait()
    loads[1].wait()

    def product(i, out):
        data = p[pl.ds(pl.multiple_of(i * cfg.T, 8), cfg.T), :]

        def body(n, _):
            wide_ = cfg.D // 4
            block_ = weight_rows(cfg, w, n * (wide_ // cfg.R), wide_ // cfg.R)
            value = lax.dot_general(data, block_, (((1,), (1,)), ((), ())), preferred_element_type=F32)
            out[:, pl.ds(pl.multiple_of(n * wide_, 128), wide_)] = value.astype(BF)
            return 0

        lax.fori_loop(0, 4, body, 0)

    block_of = grad_block(cfg, low, p, t_parts[0])
    tsum.produce(block_of, 0, 4)
    loads[2].wait()
    red.run(product)
    tsum.produce(block_of, 4, 7)
    tsum.pump((2,))
    ex_1 = Exchange(cfg, co, lambda i: group_sum.at[i], lambda i: land1.at[i], s1, r1)
    red.pass_on()
    tsum.pump((1,))
    ex_d.finish()
    for copy in copies:
        copy.wait()
    step = 64

    def body(i, carry):
        s0, s1_ = carry
        at = pl.ds(pl.multiple_of(i * step, 8), step)
        value = red.total(at)
        z, inverse = normalize(x[at, :].astype(F32))
        h = value * vec[4:5, :]
        m0 = jnp.mean(h, axis=-1, keepdims=True)
        m1 = jnp.mean(h * z, axis=-1, keepdims=True)
        grad[at, :] = (h - m0 - z * m1) * inverse + dgot[at, :].astype(F32)
        return s0 + jnp.sum(value * z, axis=0, keepdims=True), s1_ + jnp.sum(value, axis=0, keepdims=True)

    zero = jnp.zeros((1, cfg.D), F32)
    carry = (zero, zero)
    per = cfg.T // step // CHUNKS
    for c in range(CHUNKS):
        red.receive(c)
        carry = lax.fori_loop(c * per, (c + 1) * per, body, carry)
    many = cfg.N // cfg.PER
    small[...] = jnp.zeros_like(small)
    for i in range(cfg.L):
        lanes = slice(128 * i, 128 * i + 128)
        small[s * cfg.L + i, 0:4, :] = sums1[0:4, lanes]
        small[s * cfg.L + i, 6:10, :] = sums2[0:4, lanes]
        small[s * cfg.L + i, 10:12, :] = norm2[0:2, lanes]
    for i in range(many):
        small[i, 4:5, :] = carry[0][:, 128 * i : 128 * i + 128]
        small[i, 5:6, :] = carry[1][:, 128 * i : 128 * i + 128]

    def each(k, _):
        m = (me + k) % cfg.N
        remote(small.at[m // cfg.PER], sg.at[me], small_send, small_recv, (m // cfg.FS, m % cfg.FS)).start()
        return 0

    lax.fori_loop(1, cfg.N, each, 0)
    sg[me] = small[me // cfg.PER]
    tsum.settle(group_sum, ex_1.piece_sender(PIECES))
    land1[s] = group_sum[s]

    def spread(land, out):
        for i in range(cfg.F):
            for c in range(3):
                at = c * cfg.D + i * cfg.FW
                out[:, at : at + cfg.FW] = land[i, :, c * cfg.FW : (c + 1) * cfg.FW].astype(F32)

    spread(land2, o2)
    everyone = sg.at[pl.ds(0, cfg.N - 1)]
    pltpu.make_async_copy(everyone, everyone, small_recv).wait()
    value = sg[0]
    for i in range(1, cfg.N):
        value = value + sg[i]
    total[...] = value
    ex_1.finish()
    spread(land1, o1)
    red.drain()
    tsum.drain()
    pltpu.make_async_copy(everyone, everyone, small_send).wait()


def final(cfg, p, f1, low, dlow, sum2, x, vec, sums1, sums2, norm2):
    shape = jax.ShapeDtypeStruct
    vm = lambda t: pltpu.VMEM(t.shape, t.dtype)
    part = pltpu.VMEM((cfg.F, cfg.R, 3 * cfg.FW), BF)
    out = shape((cfg.R, 3 * cfg.D), F32)
    return pl.pallas_call(
        functools.partial(final_kernel, cfg),
        name="final",
        out_shape=[shape((cfg.T, cfg.D), F32), out, out, shape((16, 128), F32)],
        in_specs=[HBM] * 5 + [VM] * 5,
        out_specs=[VM] * 4,
        scratch_shapes=[vm(p), vm(f1), vm(low), pltpu.VMEM((cfg.T, cfg.D), BF), part, part, part]
        + [pltpu.VMEM((cfg.N // cfg.PER, 16, 128), F32), pltpu.VMEM((cfg.N, 16, 128), F32)]
        + reduce_parts(cfg.T, cfg.D)
        + line_parts(cfg)
        + [DMA((5,)), DMA(()), DMA(())]
        + [DMA((cfg.F,))] * 4
        + reduce_sems()
        + line_sum_sems(cfg),
        compiler_params=pltpu.CompilerParams(collective_id=7, has_side_effects=True, vmem_limit_bytes=VMEM_CAP),
    )(p, f1, low, dlow, sum2, x, vec, sums1, sums2, norm2)


def shards_square(cfg, inputs, cotangent, w1, w2, packed, me):
    low1, low2, full1, full2, saved, vec, mine, lens, z_own, inv, hid2, p2, direct2, sums2 = forward(cfg, inputs[0], cotangent[0], w1, w2, packed)
    p1, direct1, part2, hidden, norm2, sums1 = inner(cfg, p2, full2, low2, z_own, inv, direct2, saved, hid2, mine, lens)
    grad, gw1, gw2, total = final(cfg, p1, full1, low1, direct1, part2, inputs[0], vec, sums1, sums2, norm2)
    total = lax.dynamic_slice(total, (0, (me % cfg.PER) * cfg.R), (16, cfg.R))
    out = [hidden[None], grad[None], gw1] + [total[i] for i in range(6)] + [gw2] + [total[i] for i in range(6, 12)]
    return tuple(out)


def shards(mesh, inputs, lengths, w1, pf1, pr1, bf1, br1, ng1, nb1, w2, pf2, pr2, bf2, br2, ng2, nb2, cotangent):
    _, steps, width = inputs.shape
    cfg = make_cfg(mesh, steps, width)
    a, zl, b, f = coords(cfg)
    j, me = zl * cfg.FS + f, flat(cfg, a, zl, b, f)
    vectors = [pf1, pr1, bf1, br1, ng1, nb1, pf2, pr2, bf2, br2, ng2, nb2, jnp.broadcast_to(lengths.astype(BF), (cfg.R,))]
    packed = jnp.tile(jnp.concatenate([jnp.stack(vectors), jnp.zeros((3, cfg.R), BF)]), (1, cfg.PER))
    lane = lax.broadcasted_iota(jnp.int32, (16, 128), 1)
    packed = jnp.where(lane // cfg.R == me % cfg.PER, packed, jnp.zeros_like(packed))

    square = cfg.ZL == 2 and cfg.FS == 4 and cfg.A == 4 and cfg.X == 1 and cfg.R % 16 == 0 and cfg.FW % 128 == 0
    if square:
        return shards_square(cfg, inputs, cotangent, w1, w2, packed, me)
    xg, cg, full1, full2, smalls = start(cfg, inputs[0], cotangent[0], w1, w2, packed)
    full1, full2 = full1.reshape(cfg.D, 3 * cfg.FW), full2.reshape(cfg.D, 3 * cfg.FW)
    vec = jnp.sum(smalls.astype(F32).reshape(cfg.N // cfg.PER, cfg.PER, 16, 128), axis=1)
    vec = jnp.transpose(vec, (1, 0, 2)).reshape(16, cfg.D)
    mine = lax.dynamic_slice(vec, (0, j * cfg.FW), (16, cfg.FW))
    lens = vec[12].reshape(cfg.A, cfg.ZL, cfg.X, cfg.FS, cfg.R)[..., 0]
    lens = lax.dynamic_index_in_dim(lax.dynamic_index_in_dim(lens, a, 0, False), b, 1, False).reshape(cfg.S)
    lens = jnp.broadcast_to(lens.astype(jnp.int32)[:, None], (cfg.S, 128))

    low1, hid1, hid1_low, inp, cand, states, tf, tr = first(cfg, xg, full1, vec, mine, lens)
    hg = gather_hidden(cfg, hid1_low).reshape(cfg.S, cfg.T, cfg.D)
    low2, hid2_low, grads2, part2, z_own, inv, direct2, sums2 = second(cfg, hg, full2, vec, mine, lens, hid1, cg)
    grad1, norm2 = middle(cfg, part2, z_own, inv, direct2, mine)
    gw2 = wgrad(cfg, low2, grads2)
    grads1, part1, direct1, sums1 = third(cfg, full1, mine, lens, inp, cand, states, tf, tr, grad1)
    gw1 = wgrad(cfg, low1, grads1)
    input_grad, hidden, got1, got2, norm1 = last(cfg, part1, direct1, hid2_low, gw1, gw2, inputs[0], vec)
    s1, s2 = own_sum(cfg, gw1, got1, a, b), own_sum(cfg, gw2, got2, a, b)

    block = jnp.concatenate([sums1[:4], jnp.zeros((2, cfg.FW), F32), sums2[:4], norm2[:2], jnp.zeros((4, cfg.FW), F32)])
    small = lax.dynamic_update_slice(jnp.zeros((16, cfg.D), F32), block, (0, j * cfg.FW))
    small = lax.dynamic_update_slice(small, norm1[:2], (4, 0))
    small = jnp.transpose(small.reshape(16, cfg.N // cfg.PER, 128), (1, 0, 2))
    gw1, gw2, smalls = end(cfg, s1, s2, small)
    total = jnp.sum(smalls, axis=0)
    total = lax.dynamic_slice(total, (0, (me % cfg.PER) * cfg.R), (16, cfg.R))
    out = [hidden[None], input_grad[None], gw1.astype(F32)] + [total[i] for i in range(6)] + [gw2.astype(F32)] + [total[i] for i in range(6, 12)]
    return tuple(out)


def solution(mesh):
    both = ("dp", "fsdp")
    seq, mat, vec = P(both, None, None), P(both, None), P(both)
    return jax.shard_map(
        functools.partial(shards, mesh),
        mesh=mesh,
        in_specs=(seq, vec) + ((mat,) + (vec,) * 6) * 2 + (seq,),
        out_specs=(seq, seq) + ((mat,) + (vec,) * 6) * 2,
        check_vma=False,
    )
```

```python
import functools
from collections import namedtuple

import jax
import jax.numpy as jnp
from jax import lax
from jax.experimental import pallas as pl
from jax.experimental.pallas import tpu as pltpu
from jax.sharding import PartitionSpec as P

MESH = pl.DeviceIdType.MESH
HBM = pl.BlockSpec(memory_space=pltpu.HBM)
VM = pl.BlockSpec(memory_space=pltpu.VMEM)
DMA = pltpu.SemaphoreType.DMA
BF = jnp.bfloat16
F32 = jnp.float32
EPSILON = 1e-05
PAD = 8
VMEM_CAP = 62 << 20

Cfg = namedtuple("Cfg", ("DP", "FS", "N", "A", "ZL", "X", "F", "C", "S", "T", "TP", "D", "FW", "L", "R", "M", "PER"))


def make_cfg(mesh, steps, width):
    dp, fs = mesh.shape["dp"], mesh.shape["fsdp"]
    zl = 2 if fs < 8 and dp % 4 == 0 else 1
    x = 2 if zl == 1 and dp % 2 == 0 else 1
    a = dp // (zl * x)
    f = zl * fs
    fw = width // f
    rows = width // (dp * fs)
    return Cfg(dp, fs, dp * fs, a, zl, x, f, f // 2, f, steps, steps + PAD, width, fw, fw // 128, rows, f * steps, 128 // rows)


def coords(cfg):
    dp, f = lax.axis_index("dp"), lax.axis_index("fsdp")
    b, zl, a = dp % cfg.X, (dp // cfg.X) % cfg.ZL, dp // (cfg.X * cfg.ZL)
    return a, zl, b, f


def device(cfg, a, zl, b, f):
    return ((a * cfg.ZL + zl) * cfg.X + b, f)


def flat(cfg, a, zl, b, f):
    return ((a * cfg.ZL + zl) * cfg.X + b) * cfg.FS + f


def member(cfg, a, b, s):
    return device(cfg, a, s // cfg.FS, b, s % cfg.FS)


def remote(src, dst, send, recv, where):
    return pltpu.make_async_remote_copy(src_ref=src, dst_ref=dst, send_sem=send, recv_sem=recv, device_id=where, device_id_type=MESH)


def greet(targets):
    barrier = pltpu.get_barrier_semaphore()
    for where in targets:
        pl.semaphore_signal(barrier, inc=1, device_id=where, device_id_type=MESH)
    pl.semaphore_wait(barrier, len(targets))


def greet_all(cfg, me):
    barrier = pltpu.get_barrier_semaphore()

    def one(k, _):
        m = (me + k) % cfg.N
        pl.semaphore_signal(barrier, inc=1, device_id=(m // cfg.FS, m % cfg.FS), device_id_type=MESH)
        return 0

    lax.fori_loop(1, cfg.N, one, 0)
    pl.semaphore_wait(barrier, cfg.N - 1)


def group_targets(cfg, a, b, s):
    return [member(cfg, a, b, (s + k) % cfg.F) for k in range(1, cfg.F)]


class Gather:
    def __init__(self, cfg, co, src, slot, send, recv, mate_send, mate_recv):
        self.cfg, self.co, self.src, self.slot = cfg, co, src, slot
        self.sems = send, recv, mate_send, mate_recv
        a, zl, b, f = co
        self.s = zl * cfg.FS + f
        self.cell, self.core = self.s // 2, self.s % 2

    def far(self, k):
        cfg, (a, zl, b, f) = self.cfg, self.co
        send, recv, _, _ = self.sems
        to = member(cfg, a, b, ((self.cell + k) % cfg.C) * 2 + self.core)
        return remote(self.src, self.slot(self.s), send.at[k], recv.at[k], to)

    def near(self, k):
        cfg, (a, zl, b, f) = self.cfg, self.co
        _, _, send, recv = self.sems
        origin = ((self.cell - k + cfg.C) % cfg.C) * 2 + self.core
        src = self.src if k == 0 else self.slot(origin)
        return remote(src, self.slot(origin), send.at[k], recv.at[k], member(cfg, a, b, self.cell * 2 + 1 - self.core))

    def start(self):
        for k in range(1, self.cfg.C):
            self.far(k).start()
        self.near(0).start()

    def finish(self):
        for k in range(1, self.cfg.C):
            self.far(k).wait_recv()
            self.near(k).start()
        for k in range(1, self.cfg.C):
            self.far(k).wait_send()
        for k in range(self.cfg.C):
            self.near(k).wait()


class Exchange:
    def __init__(self, cfg, co, src, dst, send, recv):
        self.cfg, self.co, self.src, self.dst, self.send, self.recv = cfg, co, src, dst, send, recv
        self.s = co[1] * cfg.FS + co[3]

    def copy(self, k):
        a, zl, b, f = self.co
        to = (self.s + k) % self.cfg.F
        return remote(self.src(to), self.dst(self.s), self.send.at[k], self.recv.at[k], member(self.cfg, a, b, to))

    def start(self, begin=1, end=None):
        for k in range(begin, end or self.cfg.F):
            self.copy(k).start()

    def piece_sender(self, pieces):
        count = self.cfg.F // pieces

        def send(p):
            for h in range(count):
                to = p * count + h
                pl.when(to != self.s)(lambda to=to: self.copy((to - self.s + self.cfg.F) % self.cfg.F).start())

        return send

    def finish(self):
        for k in range(1, self.cfg.F):
            self.copy(k).wait()


class WeightGather:
    def __init__(self, cfg, co, w, full, own, send, recv, asend, arecv, bsend, brecv):
        self.cfg, self.co, self.w, self.full = cfg, co, w, full
        self.own, self.send, self.recv = own, send, recv
        self.asend, self.arecv, self.bsend, self.brecv = asend, arecv, bsend, brecv
        self.s = co[1] * cfg.FS + co[3]

    def pieces(self, k):
        cfg, (a, zl, b, f) = self.cfg, self.co
        to = (self.s + k) % cfg.F
        me = flat(cfg, a, zl, b, f)
        for c in range(3):
            src = self.w.at[:, pl.ds(pl.multiple_of(c * cfg.D + to * cfg.FW, 128), cfg.FW)]
            dst = self.full.at[me, :, pl.ds(c * cfg.FW, cfg.FW)]
            if k == 0:
                yield pltpu.make_async_copy(src, dst, self.own.at[c])
            else:
                yield remote(src, dst, self.send.at[k, c], self.recv.at[k, c], member(cfg, a, b, to))

    def start(self):
        for k in range(self.cfg.F):
            for copy in self.pieces(k):
                copy.start()

    def middle(self):
        for k in range(self.cfg.F):
            for copy in self.pieces(k):
                copy.wait()

    def rows_of(self, a, p, b):
        cfg = self.cfg
        count = cfg.FS // 2
        return self.full.at[pl.ds(flat(cfg, a, p // 2, b, 0) + (p % 2) * count, count)]

    def to_a(self, k, p):
        cfg, (a, zl, b, f) = self.cfg, self.co
        rows = self.rows_of(a, p, b)
        return remote(rows, rows, self.asend.at[k, p], self.arecv.at[k, p], device(cfg, (a + k) % cfg.A, zl, b, f))

    def to_b(self, k, ka, p):
        cfg, (a, zl, b, f) = self.cfg, self.co
        rows = self.rows_of((a - ka + cfg.A) % cfg.A, p, b)
        return remote(rows, rows, self.bsend.at[k, ka, p], self.brecv.at[k, ka, p], device(cfg, a, zl, (b + k) % cfg.X, f))

    def start_a(self):
        for p in range(2 * self.cfg.ZL):
            for k in range(1, self.cfg.A):
                self.to_a(k, p).start()

    def start_b(self):
        for p in range(2 * self.cfg.ZL):
            for k in range(1, self.cfg.X):
                self.to_b(k, 0, p).start()

    def start_out(self):
        self.start_a()
        self.start_b()

    def forward(self, p):
        for ka in range(1, self.cfg.A):
            self.to_a(ka, p).wait_recv()
            for k in range(1, self.cfg.X):
                self.to_b(k, ka, p).start()

    def finish(self):
        cfg = self.cfg
        for p in range(2 * cfg.ZL):
            for ka in range(cfg.A):
                for k in range(1, cfg.X):
                    self.to_b(k, ka, p).wait()
            for ka in range(1, cfg.A):
                self.to_a(ka, p).wait_send()

    def finish_out(self):
        for p in range(2 * self.cfg.ZL):
            self.forward(p)
        self.finish()


def t_targets(cfg, co):
    a, zl, b, f = co
    return [device(cfg, (a + way + cfg.A) % cfg.A, zl, b, f) for way in (1, -1)]


def weight_sems(cfg):
    return [DMA((3,)), DMA((cfg.F, 3)), DMA((cfg.F, 3))] + [DMA((cfg.A, 2 * cfg.ZL))] * 2 + [DMA((cfg.X, cfg.A, 2 * cfg.ZL))] * 2


def start_kernel(cfg, x, cot, w1, w2, small, xg, cg, f1, f2, sg, own_sem, small_send, small_recv, gs, gr, gms, gmr, cs, cr, *wsems):
    co = coords(cfg)
    a, zl, b, f = co
    s, me = zl * cfg.FS + f, flat(cfg, *co)
    greet_all(cfg, me)
    weights = [WeightGather(cfg, co, w1, f1, *wsems[:7]), WeightGather(cfg, co, w2, f2, *wsems[7:])]
    weights[0].start()
    gather = Gather(cfg, co, x, lambda i: xg.at[i], gs, gr, gms, gmr)
    gather.start()

    def each(k, _):
        m = (me + k) % cfg.N
        remote(small, sg.at[me], small_send, small_recv, (m // cfg.FS, m % cfg.FS)).start()
        return 0

    lax.fori_loop(1, cfg.N, each, 0)
    weights[1].start()
    exchange = Exchange(cfg, co, lambda i: cot.at[:, pl.ds(pl.multiple_of(i * cfg.FW, 128), cfg.FW)], lambda i: cg.at[i], cs, cr)
    exchange.start()
    locals_ = [
        pltpu.make_async_copy(x, xg.at[s], own_sem.at[0]),
        pltpu.make_async_copy(cot.at[:, pl.ds(pl.multiple_of(s * cfg.FW, 128), cfg.FW)], cg.at[s], own_sem.at[1]),
        pltpu.make_async_copy(small, sg.at[me], own_sem.at[2]),
    ]
    for copy in locals_:
        copy.start()
    weights[0].middle()
    weights[0].start_out()
    weights[1].middle()
    gather.finish()
    weights[0].finish_out()
    weights[1].start_out()
    exchange.finish()
    weights[1].finish_out()
    everyone = sg.at[pl.ds(0, cfg.N - 1)]
    pltpu.make_async_copy(everyone, everyone, small_recv).wait()
    pltpu.make_async_copy(everyone, everyone, small_send).wait()
    for copy in locals_:
        copy.wait()


def start(cfg, x, cot, w1, w2, small):
    full = jax.ShapeDtypeStruct((cfg.N, cfg.R, 3 * cfg.FW), BF)
    return pl.pallas_call(
        functools.partial(start_kernel, cfg),
        name="start",
        out_shape=(
            jax.ShapeDtypeStruct((cfg.S, cfg.T, cfg.D), BF),
            jax.ShapeDtypeStruct((cfg.S, cfg.T, cfg.FW), BF),
            full,
            full,
            jax.ShapeDtypeStruct((cfg.N, 16, 128), BF),
        ),
        in_specs=[HBM] * 5,
        out_specs=[HBM] * 5,
        scratch_shapes=[DMA((3,)), DMA(()), DMA(())] + [DMA((cfg.C,))] * 4 + [DMA((cfg.F,))] * 2 + weight_sems(cfg) * 2,
        compiler_params=pltpu.CompilerParams(collective_id=0, has_side_effects=True),
    )(x, cot, w1, w2, small)


def rows(cfg, ref, t, first, count):
    return jnp.concatenate([ref[first + i, pl.ds(t, cfg.S, stride=cfg.TP), :] for i in range(count)], axis=1)


def put(cfg, ref, t, value, first=0):
    for i in range(value.shape[1] // 128):
        ref[first + i, pl.ds(t, cfg.S, stride=cfg.TP), :] = value[:, 128 * i : 128 * i + 128]


def wide(cfg, ref, row):
    return jnp.broadcast_to(ref[row : row + 1, :], (cfg.S, cfg.FW))


def scan_forward(cfg, proj, inp, vec, base, lens, hid, states, tf_ref, tr_ref):
    half_pf, half_pr = 0.5 * wide(cfg, vec, base), 0.5 * wide(cfg, vec, base + 1)
    half_bf, half_br = 0.5 * wide(cfg, vec, base + 2), 0.5 * wide(cfg, vec, base + 3)
    live = jnp.broadcast_to(lens[:, 0:1], (cfg.S, cfg.FW))

    def step(t, c):
        u, p, q = (rows(cfg, proj, t, i * cfg.L, cfg.L) for i in range(3))
        here = rows(cfg, inp, t, 0, cfg.L)
        p, q, hu, hc = 0.5 * p + half_bf, 0.5 * q + half_br, 0.5 * u, 0.5 * c
        tf = jnp.tanh(p + half_pf * c)
        tr = jnp.tanh(q + half_pr * c)
        new = (hc + hu) + tf * (hc - hu)
        out = jnp.where(t < live, 0.5 * (here + new) + 0.5 * tr * (new - here), 0.0)
        put(cfg, hid, t, out)
        put(cfg, states, t, new)
        put(cfg, tf_ref, t, tf)
        put(cfg, tr_ref, t, tr)
        return new

    lax.fori_loop(0, cfg.T, step, jnp.zeros((cfg.S, cfg.FW), F32), unroll=4)


def scan_backward(cfg, cand, inp, vec, base, lens, states, tf_ref, tr_ref, grad, grads, direct, sums):
    pf, pr = wide(cfg, vec, base), wide(cfg, vec, base + 1)
    live = jnp.broadcast_to(lens[:, 0:1], (cfg.S, cfg.FW))

    def step(i, carry):
        e, new, s0, s1, s2, s3 = carry
        t = cfg.T - 1 - i
        u, here, g = rows(cfg, cand, t, 0, cfg.L), rows(cfg, inp, t, 0, cfg.L), rows(cfg, grad, t, 0, cfg.L)
        f = 0.5 * rows(cfg, tf_ref, t, 0, cfg.L) + 0.5
        r = 0.5 * rows(cfg, tr_ref, t, 0, cfg.L) + 0.5
        c = jnp.where(t > 0, rows(cfg, states, jnp.maximum(t - 1, 0), 0, cfg.L), 0.0)
        k = jnp.where(t < live, g, 0.0)
        kr = k * r
        rest = 1.0 - f
        w = (c - u) * (f * rest)
        dq = (k - kr) * (new - here) * r
        s = e + kr
        dp = s * w
        put(cfg, grads, t, s * rest, 0)
        put(cfg, grads, t, dp, cfg.L)
        put(cfg, grads, t, dq, 2 * cfg.L)
        put(cfg, direct, t, k - kr)
        e = s * (f + w * pf) + dq * pr
        return e, c, s0 + dp * c, s1 + dq * c, s2 + dp, s3 + dq

    zero = jnp.zeros((cfg.S, cfg.FW), F32)
    out = lax.fori_loop(0, cfg.T, step, (zero, rows(cfg, states, cfg.T - 1, 0, cfg.L)) + (zero,) * 4, unroll=4)
    for i in range(4):
        sums[i : i + 1, :] = jnp.sum(out[2 + i], axis=0, keepdims=True)


def normalize(x):
    center = x - jnp.mean(x, axis=-1, keepdims=True)
    inverse = lax.rsqrt(jnp.mean(center * center, axis=-1, keepdims=True) + EPSILON)
    return center * inverse, inverse


def project(cfg, z, gain, shift, w, low, proj, s):
    lowered = (z * gain + shift).astype(BF)
    low[0] = lowered
    out = jnp.dot(lowered, w[...], preferred_element_type=F32)
    base = pl.multiple_of(s * cfg.TP, 8)
    for i in range(3 * cfg.L):
        proj[i, pl.ds(base, cfg.T), :] = out[:, 128 * i : 128 * i + 128]


def seq_block(cfg, ref, i, s):
    return ref[i, pl.ds(pl.multiple_of(s * cfg.TP, 8), cfg.T), :]


def narrow(cfg, src, dst, count):
    for i in range(count):
        for s in range(cfg.S):
            dst[s * cfg.T : (s + 1) * cfg.T, 128 * i : 128 * i + 128] = src[i, s * cfg.TP : s * cfg.TP + cfg.T, :].astype(dst.dtype)


def first_kernel(cfg, x, w, vec, mine, lens, low, hid, hid_low, inp, cand, states, tf, tr, proj):
    s = pl.program_id(0)
    _, zl, _, f = coords(cfg)
    j = zl * cfg.FS + f
    data = x[0].astype(F32)
    z, _ = normalize(data)
    project(cfg, z, vec[4:5, :], vec[5:6, :], w, low, proj, s)
    own = x[0, :, pl.ds(pl.multiple_of(j * cfg.FW, 128), cfg.FW)].astype(F32)
    for i in range(cfg.L):
        inp[i, pl.ds(pl.multiple_of(s * cfg.TP, 8), cfg.T), :] = own[:, 128 * i : 128 * i + 128]

    @pl.when(s == cfg.S - 1)
    def _():
        scan_forward(cfg, proj, inp, mine, 0, lens, hid, states, tf, tr)
        narrow(cfg, hid, hid_low, cfg.L)
        for i in range(cfg.L):
            cand[i] = proj[i]


def keep(cfg, count):
    return jax.ShapeDtypeStruct((count, cfg.S * cfg.TP, 128), F32)


def const(shape):
    return pl.BlockSpec(shape, lambda i: (0,) * len(shape))


def first(cfg, x, w, vec, mine, lens):
    state = keep(cfg, cfg.L)
    spec = const(state.shape)
    return pl.pallas_call(
        functools.partial(first_kernel, cfg),
        name="first",
        grid=(cfg.S,),
        out_shape=(jax.ShapeDtypeStruct((cfg.S, cfg.T, cfg.D), BF), state, jax.ShapeDtypeStruct((cfg.M, cfg.FW), BF)) + (state,) * 5,
        in_specs=[pl.BlockSpec((1, cfg.T, cfg.D), lambda i: (i, 0, 0)), const(w.shape), const(vec.shape), const(mine.shape), const(lens.shape)],
        out_specs=[pl.BlockSpec((1, cfg.T, cfg.D), lambda i: (i, 0, 0)), spec, const((cfg.M, cfg.FW))] + [spec] * 5,
        scratch_shapes=[pltpu.VMEM((3 * cfg.L, cfg.S * cfg.TP, 128), F32)],
        compiler_params=pltpu.CompilerParams(vmem_limit_bytes=VMEM_CAP),
    )(x, w, vec, mine, lens)


def second_kernel(cfg, x, w, vec, mine, lens, inp, grad_in, low, hid_low, grads_low, part, z_own, inv, direct, sums, proj, hid, states, tf, tr, grad, grads):
    i = pl.program_id(0)
    _, zl, _, f = coords(cfg)
    j = zl * cfg.FS + f

    @pl.when(i < cfg.S)
    def _():
        z, inverse = normalize(x[0].astype(F32))
        project(cfg, z, vec[10:11, :], vec[11:12, :], w, low, proj, i)
        at = pl.ds(pl.multiple_of(i * cfg.T, 8), cfg.T)
        inv[at, :] = jnp.broadcast_to(inverse, (cfg.T, 128))
        raw = x[0, :, pl.ds(pl.multiple_of(j * cfg.FW, 128), cfg.FW)].astype(F32)
        mean = jnp.mean(x[0].astype(F32), axis=-1, keepdims=True)
        z_own[at, :] = (raw - mean) * inverse

    @pl.when(i == cfg.S - 1)
    def _():
        for s in range(cfg.S):
            g = grad_in[s].astype(F32)
            for l in range(cfg.L):
                grad[l, s * cfg.TP : s * cfg.TP + cfg.T, :] = g[:, 128 * l : 128 * l + 128]
        scan_forward(cfg, proj, inp, mine, 6, lens, hid, states, tf, tr)
        narrow(cfg, hid, hid_low, cfg.L)
        scan_backward(cfg, proj, inp, mine, 6, lens, states, tf, tr, grad, grads, direct, sums)
        narrow(cfg, grads, grads_low, 3 * cfg.L)

    @pl.when(i >= cfg.S)
    def _():
        k = i - cfg.S
        block = w[pl.ds(pl.multiple_of(k * cfg.FW, 8), cfg.FW), :]
        part[0] = lax.dot_general(grads_low[...], block, (((1,), (1,)), ((), ())), preferred_element_type=F32).astype(BF)


def second(cfg, x, w, vec, mine, lens, inp, grad_in):
    state = keep(cfg, cfg.L)
    spec = const(state.shape)
    big = pltpu.VMEM(state.shape, F32)
    last = cfg.S - 1
    one = pl.BlockSpec((1, cfg.T, cfg.D), lambda i: (jnp.minimum(i, last), 0, 0))
    return pl.pallas_call(
        functools.partial(second_kernel, cfg),
        name="second",
        grid=(cfg.S + cfg.F,),
        out_shape=(
            jax.ShapeDtypeStruct((cfg.S, cfg.T, cfg.D), BF),
            jax.ShapeDtypeStruct((cfg.M, cfg.FW), BF),
            jax.ShapeDtypeStruct((cfg.M, 3 * cfg.FW), BF),
            jax.ShapeDtypeStruct((cfg.F, cfg.M, cfg.FW), BF),
            jax.ShapeDtypeStruct((cfg.M, cfg.FW), F32),
            jax.ShapeDtypeStruct((cfg.M, 128), F32),
            state,
            jax.ShapeDtypeStruct((8, cfg.FW), F32),
        ),
        in_specs=[one, const(w.shape), const(vec.shape), const(mine.shape), const(lens.shape), spec, const(grad_in.shape)],
        out_specs=[
            one,
            const((cfg.M, cfg.FW)),
            const((cfg.M, 3 * cfg.FW)),
            pl.BlockSpec((1, cfg.M, cfg.FW), lambda i: (jnp.maximum(i - cfg.S, 0), 0, 0)),
            const((cfg.M, cfg.FW)),
            const((cfg.M, 128)),
            spec,
            const((8, cfg.FW)),
        ],
        scratch_shapes=[pltpu.VMEM((3 * cfg.L, cfg.S * cfg.TP, 128), F32)] + [big] * 5 + [pltpu.VMEM((3 * cfg.L, cfg.S * cfg.TP, 128), F32)],
        compiler_params=pltpu.CompilerParams(vmem_limit_bytes=VMEM_CAP),
    )(x, w, vec, mine, lens, inp, grad_in)


def third_kernel(cfg, w, mine, lens, inp, cand, states, tf, tr, grad, grads_low, part, direct_low, sums, grads, direct):
    s = pl.program_id(0)

    @pl.when(s == 0)
    def _():
        scan_backward(cfg, cand, inp, mine, 0, lens, states, tf, tr, grad, grads, direct, sums)
        narrow(cfg, grads, grads_low, 3 * cfg.L)
        narrow(cfg, direct, direct_low, cfg.L)

    at = pl.ds(pl.multiple_of(s * cfg.T, 8), cfg.T)
    part[0] = lax.dot_general(grads_low[at, :], w[...], (((1,), (1,)), ((), ())), preferred_element_type=F32).astype(BF)


def third(cfg, w, mine, lens, inp, cand, states, tf, tr, grad):
    state = keep(cfg, cfg.L)
    spec = const(state.shape)
    return pl.pallas_call(
        functools.partial(third_kernel, cfg),
        name="third",
        grid=(cfg.S,),
        out_shape=(
            jax.ShapeDtypeStruct((cfg.M, 3 * cfg.FW), BF),
            jax.ShapeDtypeStruct((cfg.S, cfg.T, cfg.D), BF),
            jax.ShapeDtypeStruct((cfg.M, cfg.FW), BF),
            jax.ShapeDtypeStruct((8, cfg.FW), F32),
        ),
        in_specs=[const(w.shape), const(mine.shape), const(lens.shape)] + [spec] * 6,
        out_specs=[const((cfg.M, 3 * cfg.FW)), pl.BlockSpec((1, cfg.T, cfg.D), lambda i: (i, 0, 0)), const((cfg.M, cfg.FW)), const((8, cfg.FW))],
        scratch_shapes=[pltpu.VMEM((3 * cfg.L, cfg.S * cfg.TP, 128), F32), pltpu.VMEM(state.shape, F32)],
        compiler_params=pltpu.CompilerParams(vmem_limit_bytes=VMEM_CAP),
    )(w, mine, lens, inp, cand, states, tf, tr, grad)


def gather_kernel(cfg, x, out, own, gs, gr, gms, gmr):
    co = coords(cfg)
    a, zl, b, f = co
    s = zl * cfg.FS + f
    cell, core = s // 2, s % 2
    greet([member(cfg, a, b, ((cell + k) % cfg.C) * 2 + core) for k in range(1, cfg.C)] + [member(cfg, a, b, cell * 2 + 1 - core)])
    slot = lambda i: out.at[:, pl.ds(pl.multiple_of(i * cfg.FW, 128), cfg.FW)]
    gather = Gather(cfg, co, x, slot, gs, gr, gms, gmr)
    gather.start()
    copy = pltpu.make_async_copy(x, slot(s), own)
    copy.start()
    gather.finish()
    copy.wait()


def gather_hidden(cfg, x):
    return pl.pallas_call(
        functools.partial(gather_kernel, cfg),
        name="gather_hidden",
        out_shape=jax.ShapeDtypeStruct((cfg.M, cfg.D), BF),
        in_specs=[HBM],
        out_specs=HBM,
        scratch_shapes=[DMA(())] + [DMA((cfg.C,))] * 4,
        compiler_params=pltpu.CompilerParams(collective_id=1, has_side_effects=True),
    )(x)


class Reduce:
    def __init__(self, cfg, co, part, own, mate, out, got, load, ms, mr, fs, fr):
        self.cfg, self.co, self.part, self.own, self.mate, self.out, self.got = cfg, co, part, own, mate, out, got
        self.load, self.ms, self.mr, self.fs, self.fr = load, ms, mr, fs, fr
        self.s = co[1] * cfg.FS + co[3]
        self.cell, self.core = self.s // 2, self.s % 2

    def target(self, k):
        return (self.cell + k) % self.cfg.C

    def to_mate(self, k):
        a, _, b, _ = self.co
        return remote(
            self.part.at[self.target(k) * 2 + 1 - self.core], self.mate.at[k], self.ms.at[k], self.mr.at[k],
            member(self.cfg, a, b, self.cell * 2 + 1 - self.core),
        )

    def fetch(self, k):
        return pltpu.make_async_copy(self.part.at[self.target(k) * 2 + self.core], self.own.at[k], self.load.at[k])

    def far(self, k):
        a, _, b, _ = self.co
        return remote(self.out.at[k - 1], self.got.at[k - 1], self.fs.at[k], self.fr.at[k], member(self.cfg, a, b, self.target(k) * 2 + self.core))

    def order(self):
        return list(range(1, self.cfg.C)) + [0]

    def start(self):
        for k in self.order():
            self.to_mate(k).start()
            self.fetch(k).start()

    def middle(self):
        rows_, _ = self.own.shape[1:]
        step = 256 if rows_ % 256 == 0 else rows_
        for k in self.order():
            self.to_mate(k).wait_recv()
            self.fetch(k).wait()
            if k:

                def add(i, _):
                    at = pl.ds(pl.multiple_of(i * step, 8), step)
                    self.out[k - 1, at, :] = (self.own[k, at, :].astype(F32) + self.mate[k, at, :].astype(F32)).astype(BF)
                    return 0

                lax.fori_loop(0, rows_ // step, add, 0)
                self.far(k).start()

    def finish(self):
        for k in range(1, self.cfg.C):
            self.far(k).wait()
        for k in range(self.cfg.C):
            self.to_mate(k).wait_send()

    def total(self, at):
        value = self.own[0, at, :].astype(F32) + self.mate[0, at, :].astype(F32)
        for k in range(1, self.cfg.C):
            value = value + self.got[k - 1, at, :].astype(F32)
        return value


def reduce_scratch(cfg, rows_, cols):
    return [pltpu.VMEM((cfg.C, rows_, cols), BF)] * 2 + [pltpu.VMEM((cfg.C - 1, rows_, cols), BF)] * 2 + [DMA((cfg.C,))] * 5


def middle_kernel(cfg, part, z_own, inv, direct, mine, grad, sums, ng, stats, mean, *sc):
    red_sc, (ss, sr) = sc[:9], sc[9:]
    co = coords(cfg)
    a, zl, b, f = co
    s = zl * cfg.FS + f
    greet(group_targets(cfg, a, b, s))
    red = Reduce(cfg, co, part, *red_sc)
    red.start()
    red.middle()
    red.finish()
    gain = mine[10:11, :]
    eye = (lax.broadcasted_iota(jnp.int32, (128, 128), 0) == lax.broadcasted_iota(jnp.int32, (128, 128), 1)).astype(F32)

    def first_pass(i, carry):
        s0, s1 = carry
        at = pl.ds(pl.multiple_of(i * 128, 8), 128)
        value = red.total(at)
        z = z_own[at, :]
        h = value * gain
        ng[at, :] = h
        for n, x in ((0, h), (1, h * z)):
            col = jnp.sum(x, axis=-1, keepdims=True)
            stats[s, n, pl.ds(i, 1), :] = jnp.sum(col * eye, axis=0, keepdims=True)
        return s0 + jnp.sum(value * z, axis=0, keepdims=True), s1 + jnp.sum(value, axis=0, keepdims=True)

    zero = jnp.zeros((1, cfg.FW), F32)
    s0, s1 = lax.fori_loop(0, cfg.M // 128, first_pass, (zero, zero))
    sums[0:1, :] = s0
    sums[1:2, :] = s1
    exchange = Exchange(cfg, co, lambda i: stats.at[s], lambda i: stats.at[i], ss, sr)
    exchange.start()
    exchange.finish()
    total = stats[0]
    for i in range(1, cfg.F):
        total = total + stats[i]
    mean[...] = total * (1.0 / cfg.D)

    def second_pass(i, _):
        at = pl.ds(pl.multiple_of(i * 128, 8), 128)
        m0 = jnp.sum(mean[0, pl.ds(i, 1), :] * eye, axis=-1, keepdims=True)
        m1 = jnp.sum(mean[1, pl.ds(i, 1), :] * eye, axis=-1, keepdims=True)
        value = (ng[at, :] - m0 - z_own[at, :] * m1) * inv[at, 0:1]
        per = cfg.T // 128
        to = pl.ds(pl.multiple_of((i // per) * cfg.TP + (i % per) * 128, 8), 128)
        for l in range(cfg.L):
            grad[l, to, :] = value[:, 128 * l : 128 * l + 128] + direct[l, to, :]
        return 0

    lax.fori_loop(0, cfg.M // 128, second_pass, 0)


def middle(cfg, part, z_own, inv, direct, mine):
    return pl.pallas_call(
        functools.partial(middle_kernel, cfg),
        name="middle",
        out_shape=(keep(cfg, cfg.L), jax.ShapeDtypeStruct((8, cfg.FW), F32)),
        in_specs=[HBM] + [VM] * 4,
        out_specs=[VM] * 2,
        scratch_shapes=[
            pltpu.VMEM((cfg.M, cfg.FW), F32),
            pltpu.VMEM((cfg.F, 2, cfg.M // 128, 128), F32),
            pltpu.VMEM((2, cfg.M // 128, 128), F32),
        ]
        + reduce_scratch(cfg, cfg.M, cfg.FW)
        + [DMA((cfg.F,))] * 2,
        compiler_params=pltpu.CompilerParams(collective_id=2, has_side_effects=True, vmem_limit_bytes=VMEM_CAP),
    )(part, z_own, inv, direct, mine)


def last_kernel(cfg, part, dir_low, hid_low, g1, g2, x, vec, grad, hid, b1, b2, sums, dgot, *sc):
    red_sc, sc = sc[:9], sc[9:]
    own, ds, dr, hs, hr = sc[:5]
    ts = sc[5:]
    co = coords(cfg)
    a, zl, b, f = co
    s = zl * cfg.FS + f
    barrier_to = group_targets(cfg, a, b, s)
    others = [(ka, kb) for ka in range(cfg.A) for kb in range(cfg.X) if ka or kb]
    far = lambda ka, kb: ((a + ka) % cfg.A, (b + kb) % cfg.X)
    for ka, kb in others:
        ta, tb = far(ka, kb)
        barrier_to.append(device(cfg, ta, zl, tb, f))
    greet(barrier_to)
    red = Reduce(cfg, co, part, *red_sc)
    red.start()

    def across(layer, o, z):
        src, dst = ((g1, b1), (g2, b2))[layer]
        ta, tb = far(*others[o])
        rows_ = src.at[pl.ds(flat(cfg, ta, z, tb, 0), cfg.FS)]
        return remote(rows_, dst.at[o, pl.ds(z * cfg.FS, cfg.FS)], ts[2 * layer].at[o, z], ts[2 * layer + 1].at[o, z], device(cfg, ta, zl, tb, f))

    for layer in (1, 0):
        for o in range(len(others)):
            for z in range(cfg.ZL):
                across(layer, o, z).start()
    ex_d = Exchange(cfg, co, lambda i: dir_low.at[pl.ds(i * cfg.T, cfg.T)], lambda i: dgot.at[:, pl.ds(pl.multiple_of(i * cfg.FW, 128), cfg.FW)], ds, dr)
    ex_h = Exchange(cfg, co, lambda i: hid_low.at[pl.ds(i * cfg.T, cfg.T)], lambda i: hid.at[:, pl.ds(pl.multiple_of(i * cfg.FW, 128), cfg.FW)], hs, hr)
    ex_d.start()
    ex_h.start()
    copies = [pltpu.make_async_copy(e.src(s), e.dst(s), own.at[i]) for i, e in enumerate((ex_d, ex_h))]
    for copy in copies:
        copy.start()
    red.middle()
    red.finish()
    ex_d.finish()
    for copy in copies:
        copy.wait()
    step = 64

    def body(i, carry):
        s0, s1 = carry
        at = pl.ds(pl.multiple_of(i * step, 8), step)
        value = red.total(at)
        z, inverse = normalize(x[at, :].astype(F32))
        h = value * vec[4:5, :]
        m0 = jnp.mean(h, axis=-1, keepdims=True)
        m1 = jnp.mean(h * z, axis=-1, keepdims=True)
        grad[at, :] = (h - m0 - z * m1) * inverse + dgot[at, :].astype(F32)
        return s0 + jnp.sum(value * z, axis=0, keepdims=True), s1 + jnp.sum(value, axis=0, keepdims=True)

    zero = jnp.zeros((1, cfg.D), F32)
    s0, s1 = lax.fori_loop(0, cfg.T // step, body, (zero, zero))
    sums[0:1, :] = s0
    sums[1:2, :] = s1
    ex_h.finish()
    for layer in (1, 0):
        for o in range(len(others)):
            for z in range(cfg.ZL):
                across(layer, o, z).wait()


def last(cfg, part, dir_low, hid_low, g1, g2, x, vec):
    n = cfg.A * cfg.X - 1
    got = jax.ShapeDtypeStruct((n, cfg.F, cfg.R, 3 * cfg.FW), BF)
    return pl.pallas_call(
        functools.partial(last_kernel, cfg),
        name="last",
        out_shape=(
            jax.ShapeDtypeStruct((cfg.T, cfg.D), F32),
            jax.ShapeDtypeStruct((cfg.T, cfg.D), BF),
            got,
            got,
            jax.ShapeDtypeStruct((8, cfg.D), F32),
        ),
        in_specs=[HBM] * 5 + [VM] * 2,
        out_specs=[VM, HBM, HBM, HBM, VM],
        scratch_shapes=[pltpu.VMEM((cfg.T, cfg.D), BF)]
        + reduce_scratch(cfg, cfg.T, cfg.D)
        + [DMA((2,))]
        + [DMA((cfg.F,))] * 4
        + [DMA((n, cfg.ZL))] * 4,
        compiler_params=pltpu.CompilerParams(collective_id=3, has_side_effects=True, vmem_limit_bytes=VMEM_CAP),
    )(part, dir_low, hid_low, g1, g2, x, vec)


def end_kernel(cfg, w1, w2, small, o1, o2, sg, own, small_send, small_recv, *sc):
    co = coords(cfg)
    a, zl, b, f = co
    s, me = zl * cfg.FS + f, flat(cfg, *co)
    greet_all(cfg, me)

    def pieces(layer, k):
        src, dst = ((w1, o1), (w2, o2))[layer]
        to = (s + k) % cfg.F
        for c in range(3):
            piece = src.at[to, :, pl.ds(c * cfg.FW, cfg.FW)]
            place = dst.at[:, pl.ds(pl.multiple_of(c * cfg.D + s * cfg.FW, 128), cfg.FW)]
            if k == 0:
                yield pltpu.make_async_copy(piece, place, own.at[layer, c])
            else:
                yield remote(piece, place, sc[2 * layer].at[k, c], sc[2 * layer + 1].at[k, c], member(cfg, a, b, to))

    every = [(layer, k) for layer in range(2) for k in range(cfg.F)]
    for layer, k in every:
        for copy in pieces(layer, k):
            copy.start()

    def each(k, _):
        m = (me + k) % cfg.N
        remote(small.at[m // cfg.PER], sg.at[me], small_send, small_recv, (m // cfg.FS, m % cfg.FS)).start()
        return 0

    lax.fori_loop(1, cfg.N, each, 0)
    mine = pltpu.make_async_copy(small.at[me // cfg.PER], sg.at[me], own.at[2, 0])
    mine.start()
    for layer, k in every:
        for copy in pieces(layer, k):
            copy.wait()
    mine.wait()
    everyone = sg.at[pl.ds(0, cfg.N - 1)]
    pltpu.make_async_copy(everyone, everyone, small_recv).wait()
    pltpu.make_async_copy(everyone, everyone, small_send).wait()


def end(cfg, w1, w2, small):
    out = jax.ShapeDtypeStruct((cfg.R, 3 * cfg.D), BF)
    return pl.pallas_call(
        functools.partial(end_kernel, cfg),
        name="end",
        out_shape=(out, out, jax.ShapeDtypeStruct((cfg.N,) + small.shape[1:], F32)),
        in_specs=[HBM] * 3,
        out_specs=[HBM] * 3,
        scratch_shapes=[DMA((3, 3)), DMA(()), DMA(())] + [DMA((cfg.F, 3))] * 4,
        compiler_params=pltpu.CompilerParams(collective_id=4, has_side_effects=True),
    )(w1, w2, small)


def wgrad(cfg, low, grads):
    out = lax.dot_general(low.reshape(cfg.M, cfg.D), grads, (((0,), (0,)), ((), ())), preferred_element_type=F32)
    return out.astype(BF).reshape(cfg.N, cfg.R, 3 * cfg.FW)


def own_sum(cfg, g, got, a, b):
    mine = lax.dynamic_index_in_dim(lax.dynamic_index_in_dim(g.reshape(cfg.A, cfg.ZL, cfg.X, cfg.FS, cfg.R, 3 * cfg.FW), a, 0, False), b, 1, False)
    mine = mine.reshape(cfg.F, cfg.R, 3 * cfg.FW)
    return (mine.astype(F32) + jnp.sum(got.astype(F32), axis=0)).astype(BF)


CHUNKS = 4


class Square:
    def __init__(self, cfg, co):
        self.cfg, self.co = cfg, co
        a, zl, b, f = co
        y, self.core = f // 2, f % 2
        self.cells = [(zl, y), (zl, 1 - y), (1 - zl, y), (1 - zl, 1 - y)]
        self.s = zl * cfg.FS + f

    def index(self, k, mate=False):
        zl, y = self.cells[k]
        return zl * self.cfg.FS + y * 2 + ((1 - self.core) if mate else self.core)

    def place(self, k, mate=False):
        a, _, b, _ = self.co
        zl, y = self.cells[k]
        return device(self.cfg, a, zl, b, y * 2 + ((1 - self.core) if mate else self.core))


class SquareGather:
    def __init__(self, sq, slot, by_y, sems, src=None):
        self.sq, self.slot, self.by_y = sq, slot, by_y
        self.src = src or (lambda c: slot(sq.s, c))
        self.ns, self.nr, self.fs, self.fr, self.ms, self.mr = sems

    def side(self, k, c):
        sq = self.sq
        return remote(self.src(c), self.slot(sq.s, c), self.ns.at[k, c], self.nr.at[k, c], sq.place(k))

    def across(self, c):
        sq = self.sq
        cfg, (a, zl, b, f) = sq.cfg, sq.co
        y, v = f // 2, self.by_y(c)
        via = (zl + (1 - v) * (1 - 2 * zl)) * cfg.FS + (y + v * (1 - 2 * y)) * 2 + sq.core
        to = device(cfg, a, zl + v * (1 - 2 * zl), b, (y + (1 - v) * (1 - 2 * y)) * 2 + sq.core)
        block = self.slot(via, c)
        return remote(block, block, self.fs.at[c], self.fr.at[c], to)

    def near(self, k, c):
        sq = self.sq
        block = self.slot(sq.index(k), c)
        return remote(self.src(c) if k == 0 else block, block, self.ms.at[k, c], self.mr.at[k, c], sq.place(0, True))

    def push(self, c):
        self.side(1, c).start()
        self.side(2, c).start()
        self.near(0, c).start()

    def arrive(self, c):
        self.side(1, c).wait_recv()
        self.side(2, c).wait_recv()
        self.across(c).start()
        self.near(1, c).start()
        self.near(2, c).start()

    def complete(self, c):
        self.across(c).wait_recv()
        self.near(3, c).start()
        for k in range(4):
            self.near(k, c).wait_recv()

    def drain(self):
        def one(c, _):
            self.side(1, c).wait_send()
            self.side(2, c).wait_send()
            self.across(c).wait_send()
            for k in range(4):
                self.near(k, c).wait_send()
            return 0

        lax.fori_loop(0, CHUNKS, one, 0)


def gather_sems():
    return [DMA((3, CHUNKS))] * 2 + [DMA((CHUNKS,))] * 2 + [DMA((4, CHUNKS))] * 2


class SquareReduce:
    def __init__(self, sq, to_mate, own, mate, landed, gy, gz, sems):
        self.sq, self.to_mate, self.own, self.mate = sq, to_mate, own, mate
        self.landed, self.got = landed, (None, gy, gz)
        self.ms, self.mr, self.ds, self.dr, self.gs, self.gr = sems
        self.rows = own.shape[1] // CHUNKS

    def at(self, c):
        return pl.ds(c * self.rows, self.rows)

    def near(self, k, c):
        return remote(self.to_mate.at[k, self.at(c)], self.mate.at[k, self.at(c)], self.ms.at[k, c], self.mr.at[k, c], self.sq.place(0, True))

    def far(self, c):
        return remote(self.own.at[3, self.at(c)], self.landed.at[self.at(c)], self.ds.at[c], self.dr.at[c], self.sq.place(1 + c % 2))

    def side(self, k, c):
        return remote(self.own.at[k, self.at(c)], self.got[k].at[self.at(c)], self.gs.at[k, c], self.gr.at[k, c], self.sq.place(k))

    def add(self, k, c, other):
        step = 64 if self.own.shape[2] > 512 else 256

        def body(i, _):
            at = pl.ds(pl.multiple_of(c * self.rows + i * step, 8), step)
            value = other[k, at, :] if len(other.shape) == 3 else other[at, :]
            self.own[k, at, :] = (self.own[k, at, :].astype(F32) + value.astype(F32)).astype(BF)
            return 0

        lax.fori_loop(0, self.rows // step, body, 0)

    def run(self, product, between=lambda n: None):
        order = (3, 1, 2, 0)

        def settle(k):
            for c in range(CHUNKS):
                self.near(k, c).wait_recv()
                if k:
                    self.add(k, c, self.mate)
                if k == 3:
                    self.far(c).start()
                elif k and c % 2 == k - 1:
                    self.side(k, c).start()

        for n, k in enumerate(order):
            product(self.sq.index(k, True), self.to_mate.at[k])
            for c in range(CHUNKS):
                self.near(k, c).start()
            product(self.sq.index(k), self.own.at[k])
            settle(k)
            between(n)

    def pass_on(self):
        for c in range(CHUNKS):
            k = 2 - c % 2
            self.far(c).wait_recv()
            self.add(k, c, self.landed)
            self.side(k, c).start()

    def receive(self, c):
        self.side(1, c).wait_recv()
        self.side(2, c).wait_recv()

    def total(self, at):
        value = self.own[0, at, :].astype(F32) + self.mate[0, at, :].astype(F32)
        return value + self.got[1][at, :].astype(F32) + self.got[2][at, :].astype(F32)

    def drain(self):
        for c in range(CHUNKS):
            for k in range(4):
                self.near(k, c).wait_send()
            self.far(c).wait_send()
            self.side(1, c).wait_send()
            self.side(2, c).wait_send()


def reduce_parts(rows_, cols):
    return [pltpu.VMEM((4, rows_, cols), BF)] * 3 + [pltpu.VMEM((rows_, cols), BF)] * 3


def reduce_sems():
    return [DMA((4, CHUNKS))] * 2 + [DMA((CHUNKS,))] * 2 + [DMA((3, CHUNKS))] * 2


PIECES = 4


class LineGather(WeightGather):
    def __init__(self, cfg, co, w, full, own, send, recv, rs, rr, ls, lr):
        super().__init__(cfg, co, w, full, own, send, recv, None, None, None, None)
        self.rs, self.rr, self.ls, self.lr = rs, rr, ls, lr
        self.a = co[0]

    def unit(self, a, p):
        count = self.cfg.F // PIECES
        return self.full.at[pl.ds(a * self.cfg.F + p * count, count)]

    def move(self, way, i, p):
        cfg, (a, zl, b, f) = self.cfg, self.co
        block = self.unit((a - way * i + cfg.A) % cfg.A, p)
        send, recv = (self.rs, self.rr) if way == 1 else (self.ls, self.lr)
        return remote(block, block, send.at[i, p], recv.at[i, p], device(cfg, (a + way + cfg.A) % cfg.A, zl, b, f))

    def landing(self, way, i, p):
        cfg, (a, zl, b, f) = self.cfg, self.co
        block = self.unit((a - way * (i + 1) + cfg.A) % cfg.A, p)
        send, recv = (self.rs, self.rr) if way == 1 else (self.ls, self.lr)
        return remote(block, block, send.at[i, p], recv.at[i, p], device(cfg, (a + way + cfg.A) % cfg.A, zl, b, f))

    def behind(self, way):
        return self.a if way == 1 else self.cfg.A - 1 - self.a

    def start_line(self):
        for p in range(PIECES):
            for way in (1, -1):
                pl.when(self.behind(-way) > 0)(lambda way=way, p=p: self.move(way, 0, p).start())

    def forward(self, i, p):
        for way in (1, -1):

            @pl.when(self.behind(way) >= i)
            def _():
                self.landing(way, i - 1, p).wait_recv()
                if i < self.cfg.A - 1:
                    pl.when(self.behind(-way) > 0)(lambda: self.move(way, i, p).start())

    def finish(self):
        for i in range(self.cfg.A - 1):
            for p in range(PIECES):
                for way in (1, -1):
                    there = (self.behind(way) >= i) & (self.behind(-way) > 0)
                    pl.when(there)(lambda way=way, i=i, p=p: self.move(way, i, p).wait_send())


def line_sems(cfg):
    return [DMA((3,)), DMA((cfg.F, 3)), DMA((cfg.F, 3))] + [DMA((cfg.A - 1, PIECES))] * 4


class LineSum:
    def __init__(self, cfg, co, gw, land, rs, rr, ls, lr):
        self.cfg, self.co, self.gw, self.land = cfg, co, gw, land
        self.rs, self.rr, self.ls, self.lr = rs, rr, ls, lr
        self.a = co[0]
        self.count = cfg.F // PIECES

    def behind(self, way):
        return self.a if way == 1 else self.cfg.A - 1 - self.a

    def slots(self, t, p):
        return pl.ds(t * self.cfg.F + p * self.count, self.count)

    def move(self, way, t, p):
        cfg, (a, zl, b, f) = self.cfg, self.co
        send, recv, at = (self.rs, self.rr, t + 1) if way == 1 else (self.ls, self.lr, t)
        to = device(cfg, (a + way + cfg.A) % cfg.A, zl, b, f)
        return remote(self.gw.at[self.slots(t, p)], self.land.at[at, pl.ds(p * self.count, self.count)], send.at[t, p], recv.at[t, p], to)

    def landed(self, way, t, p):
        return self.land[t + 1 if way == 1 else t, pl.ds(p * self.count, self.count)]

    def each(self, todo, distances):
        for d in distances:
            for way in (1, -1):
                pl.when(self.behind(-way) >= d)(lambda d=d, way=way: todo(way, self.a + way * d))

    def target(self, n):
        way = 1 - 2 * (n % 2)
        t = self.a + way * (self.cfg.A - 1 - n // 2)
        return t, way, (t >= 0) & (t < self.cfg.A)

    def fetch(self, src, dst, sem, n):
        t, _, _ = self.target(n)
        width = self.cfg.F * self.cfg.R
        at = pl.ds(pl.multiple_of((t + self.cfg.A) % self.cfg.A * width, 128), width)
        return pltpu.make_async_copy(src.at[:, :, at], dst.at[:, :, at], sem.at[n])

    def fetch_all(self, src, dst, sem):
        for n in range(2 * self.cfg.A - 1):
            pl.when(self.target(n)[2])(lambda n=n: self.fetch(src, dst, sem, n).start())

    def produce(self, block, begin, end, ready):
        cfg = self.cfg

        def one(n, _):
            t, way, there = self.target(n)

            @pl.when(there)
            def _():
                ready(n)

                def body(h, _):
                    block(t * cfg.F + h * cfg.FS)
                    return 0

                lax.fori_loop(0, cfg.ZL, body, 0)
                for w in (1, -1):

                    @pl.when((self.behind(w) == 0) & (way == w) & (t != self.a))
                    def _():
                        for p in range(PIECES):
                            self.move(w, t, p).start()

            return 0

        lax.fori_loop(begin, end, one, 0)

    def pump(self, distance, begin=0, end=PIECES):
        def body(p, _):
            for way in (1, -1):

                @pl.when((self.behind(-way) >= distance) & (self.behind(way) > 0))
                def _():
                    t = self.a + way * distance
                    self.move(way, t, p).wait_recv()
                    at = self.slots(t, p)
                    self.gw[at] = (self.gw[at].astype(F32) + self.landed(way, t, p).astype(F32)).astype(BF)
                    self.move(way, t, p).start()

            return 0

        lax.fori_loop(begin, end, body, 0)

    def settle(self, out, then=lambda p: None):
        def body(p, _):
            mine = self.gw[self.slots(self.a, p)].astype(F32)
            to = pl.ds(p * self.count, self.count)
            for way in (1, -1):
                pl.when(self.behind(way) > 0)(lambda way=way: self.move(way, self.a, p).wait_recv())
            for low, high in ((0, 1), (1, 0), (1, 1)):

                @pl.when(((self.behind(1) > 0) == (low == 1)) & ((self.behind(-1) > 0) == (high == 1)))
                def _():
                    value = mine
                    if low:
                        value = value + self.landed(1, self.a, p).astype(F32)
                    if high:
                        value = value + self.landed(-1, self.a, p).astype(F32)
                    out[to] = value.astype(BF)

            then(p)
            return 0

        lax.fori_loop(0, PIECES, body, 0)

    def drain(self):
        def todo(way, t):
            for p in range(PIECES):
                self.move(way, t, p).wait_send()

        self.each(todo, range(1, self.cfg.A))


def line_parts(cfg):
    cols = 3 * cfg.FW
    return [pltpu.VMEM((cfg.N, cfg.R, cols), BF), pltpu.VMEM((cfg.A + 1, cfg.F, cfg.R, cols), BF)]


def line_sum_sems(cfg):
    return [DMA((cfg.A, PIECES))] * 4


def weight_rows(cfg, w, first, count):
    return w[pl.ds(first, count)].reshape(count * cfg.R, 3 * cfg.FW)


def grad_block(cfg, low, grads, gw):
    def block(first):
        slots = pl.ds(first, cfg.FS)
        columns = pl.ds(pl.multiple_of(first * cfg.R, 128), cfg.FS * cfg.R)
        data = low[:, :, columns].reshape(cfg.M, cfg.FS * cfg.R)
        out = lax.dot_general(data, grads[...], (((0,), (0,)), ((), ())), preferred_element_type=F32)
        gw[slots] = out.astype(BF).reshape(cfg.FS, cfg.R, 3 * cfg.FW)

    return block


def multiply_chunk(cfg, low, w, proj, c):
    n = cfg.T // CHUNKS
    data = low[:, pl.ds(pl.multiple_of(c * n, 16), n), :].reshape(cfg.S * n, cfg.D)
    out = jnp.dot(data, w[...].reshape(cfg.D, 3 * cfg.FW), preferred_element_type=F32)
    for i in range(cfg.S):
        to = pl.ds(pl.multiple_of(i * cfg.TP + c * n, 8), n)
        for l in range(3 * cfg.L):
            proj[l, to, :] = out[i * n : (i + 1) * n, 128 * l : 128 * l + 128]


def multiply_units(cfg, low, w, proj, c, first, count, more):
    n, k = cfg.T // CHUNKS, cfg.F * cfg.R
    depth = pl.ds(pl.multiple_of(first * k, 128), count * k)
    data = low[:, pl.ds(pl.multiple_of(c * n, 16), n), depth].reshape(cfg.S * n, count * k)
    out = jnp.dot(data, weight_rows(cfg, w, first * cfg.F, count * cfg.F), preferred_element_type=F32)
    for i in range(cfg.S):
        to = pl.ds(pl.multiple_of(i * cfg.TP + c * n, 8), n)
        for l in range(3 * cfg.L):
            value = out[i * n : (i + 1) * n, 128 * l : 128 * l + 128]
            proj[l, to, :] = proj[l, to, :] + value if more else value


def scan_chunk(cfg, proj, inp, vec, base, lens, hid, states, tf_ref, tr_ref, carry, c):
    half_pf, half_pr = 0.5 * wide(cfg, vec, base), 0.5 * wide(cfg, vec, base + 1)
    half_bf, half_br = 0.5 * wide(cfg, vec, base + 2), 0.5 * wide(cfg, vec, base + 3)
    live = jnp.broadcast_to(lens[:, 0:1], (cfg.S, cfg.FW))
    n = cfg.T // CHUNKS

    def step(i, state):
        t = c * n + i
        u, p, q = (rows(cfg, proj, t, j * cfg.L, cfg.L) for j in range(3))
        here = rows(cfg, inp, t, 0, cfg.L)
        p, q, hu, hc = 0.5 * p + half_bf, 0.5 * q + half_br, 0.5 * u, 0.5 * state
        tf = jnp.tanh(p + half_pf * state)
        tr = jnp.tanh(q + half_pr * state)
        new = (hc + hu) + tf * (hc - hu)
        out = jnp.where(t < live, 0.5 * (here + new) + 0.5 * tr * (new - here), 0.0)
        put(cfg, hid, t, out)
        put(cfg, states, t, new)
        put(cfg, tf_ref, t, tf)
        put(cfg, tr_ref, t, tr)
        return new

    carry[...] = lax.fori_loop(0, n, step, carry[...], unroll=4)


def forward_kernel(cfg, *refs):
    refs = list(refs)

    def take(n):
        out = refs[:n]
        del refs[:n]
        return out

    x, cot, w1, w2, small = take(5)
    low1_out, low2_out, f1_out, f2_out, saved, vec, mine, lens, zo_out, inv_out, hid_out, p_out, dir_out, sums = take(14)
    xg, hg, low, f1, f2, sg, cg, proj, inp, states, tf, tr, hid, direct, hid_low, p_low, z_own, inv, carry = take(19)
    own_sem, small_send, small_recv, cs, cr, flush = take(6)
    xsems, hsems, w1sems, w2sems = take(6), take(6), take(7), take(7)
    co = coords(cfg)
    a, zl, b, f = co
    sq = Square(cfg, co)
    s, me = sq.s, flat(cfg, *co)
    rows_c = cfg.T // CHUNKS
    cols = lambda i: pl.ds(pl.multiple_of(i * cfg.FW, 128), cfg.FW)
    greet_all(cfg, me)
    one = LineGather(cfg, co, w1, f1, *w1sems)
    two = LineGather(cfg, co, w2, f2, *w2sems)
    one.start()

    def each(k, _):
        m = (me + k) % cfg.N
        remote(small, sg.at[me], small_send, small_recv, (m // cfg.FS, m % cfg.FS)).start()
        return 0

    lax.fori_loop(1, cfg.N, each, 0)
    part = lambda c: pl.ds(pl.multiple_of(c * rows_c, 16), rows_c)
    xgather = SquareGather(sq, lambda i, c: xg.at[i, part(c)], lambda c: 1 - c % 2, xsems, lambda c: x.at[part(c)])
    hgather = SquareGather(sq, lambda i, c: hg.at[:, part(c), cols(i)], lambda c: 1 - c % 2, hsems)
    two.start()
    for c in range(CHUNKS):
        xgather.push(c)
    exchange = Exchange(cfg, co, lambda i: cot.at[:, cols(i)], lambda i: cg.at[i], cs, cr)
    local = [
        pltpu.make_async_copy(x, xg.at[s], own_sem.at[0]),
        pltpu.make_async_copy(cot.at[:, cols(s)], cg.at[s], own_sem.at[1]),
        pltpu.make_async_copy(small, sg.at[me], own_sem.at[2]),
    ]
    for copy in local:
        copy.start()

    everyone = sg.at[pl.ds(0, cfg.N - 1)]
    def norm_one(c):
        def body(i, _):
            two_of = pl.ds(2 * i, 2)
            z, _ = normalize(xg[two_of, part(c), :].reshape(2 * rows_c, cfg.D).astype(F32))
            low[two_of, part(c), :] = (z * vec[4:5, :] + vec[5:6, :]).astype(BF).reshape(2, rows_c, cfg.D)
            for h in range(2):
                own = xg[2 * i + h, part(c), cols(s)].astype(F32)
                to = pl.ds(pl.multiple_of((2 * i + h) * cfg.TP + c * rows_c, 8), rows_c)
                for l in range(cfg.L):
                    inp[l, to, :] = own[:, 128 * l : 128 * l + 128]
            return 0

        lax.fori_loop(0, cfg.S // 2, body, 0)

    def norm_two(c):
        def body(i, _):
            two_of = pl.ds(2 * i, 2)
            data = hg[two_of, part(c), :].reshape(2 * rows_c, cfg.D).astype(F32)
            mean = jnp.mean(data, axis=-1, keepdims=True)
            center = data - mean
            inverse = lax.rsqrt(jnp.mean(center * center, axis=-1, keepdims=True) + EPSILON)
            low[two_of, part(c), :] = (center * inverse * vec[10:11, :] + vec[11:12, :]).astype(BF).reshape(2, rows_c, cfg.D)
            own = (hg[two_of, part(c), cols(s)].reshape(2 * rows_c, cfg.FW).astype(F32) - mean) * inverse
            for h in range(2):
                at = pl.ds(pl.multiple_of((2 * i + h) * cfg.T + c * rows_c, 8), rows_c)
                inv[at, :] = jnp.broadcast_to(inverse[h * rows_c : (h + 1) * rows_c], (rows_c, 128))
                z_own[at, :] = own[h * rows_c : (h + 1) * rows_c]
            return 0

        lax.fori_loop(0, cfg.S // 2, body, 0)

    def hidden_chunk(c):
        for i in range(cfg.S):
            to = pl.ds(pl.multiple_of(i * cfg.TP + c * rows_c, 8), rows_c)
            for l in range(cfg.L):
                hg[i, part(c), pl.ds(pl.multiple_of(s * cfg.FW + 128 * l, 128), 128)] = hid[l, to, :].astype(BF)

    keep_low1 = pltpu.make_async_copy(low, low1_out, flush.at[0])
    keep_f1 = pltpu.make_async_copy(f1, f1_out, flush.at[1])
    keeps = [
        pltpu.make_async_copy(ref if n != 1 else proj.at[pl.ds(0, cfg.L)], saved.at[pl.ds(n * cfg.L, cfg.L)], flush.at[2 + n])
        for n, ref in enumerate((inp, None, states, tf, tr))
    ]
    carry[...] = jnp.zeros_like(carry)
    one.middle()
    one.start_line()
    pltpu.make_async_copy(everyone, everyone, small_recv).wait()
    for copy in local:
        copy.wait()
    for i in range(cfg.N // cfg.PER):
        total = sg[i * cfg.PER].astype(F32)
        for p in range(1, cfg.PER):
            total = total + sg[i * cfg.PER + p].astype(F32)
        vec[:, 128 * i : 128 * i + 128] = total
    mine[...] = vec[:, cols(s)]
    for i in range(cfg.S):
        n = flat(cfg, a, i // cfg.FS, b, i % cfg.FS)
        length = jnp.max(sg[n].astype(F32)[12:13, :], axis=-1, keepdims=True)
        lens[i : i + 1, :] = jnp.broadcast_to(length, (1, 128)).astype(jnp.int32)

    xgather.arrive(0)
    one.forward(1, 0)
    one.forward(1, 1)
    xgather.arrive(1)
    one.forward(1, 2)
    one.forward(1, 3)
    xgather.arrive(2)
    one.forward(2, 0)
    xgather.arrive(3)
    one.forward(2, 1)
    one.forward(2, 2)
    one.forward(2, 3)
    two.middle()
    two.start_line()
    exchange.start()

    def layer_one(k, _):
        @pl.when(k < CHUNKS)
        def _():
            xgather.complete(k)
            norm_one(k)

            @pl.when(k == 3)
            def _():
                keep_low1.start()
                for p in range(PIECES):
                    one.forward(3, p)
                keep_f1.start()

        @pl.when(k >= CHUNKS - 1)
        def _():
            c = k - (CHUNKS - 1)
            multiply_chunk(cfg, low, f1, proj, c)
            scan_chunk(cfg, proj, inp, mine, 0, lens, hid, states, tf, tr, carry, c)
            hidden_chunk(c)
            hgather.push(c)
            pl.when(c > 0)(lambda: hgather.arrive(c - 1))
            two.forward(1, c)

        return 0

    lax.fori_loop(0, 2 * CHUNKS - 1, layer_one, 0)
    for copy in keeps:
        copy.start()
    carry[...] = jnp.zeros_like(carry)
    hgather.arrive(CHUNKS - 1)
    two.forward(2, 0)
    two.forward(2, 1)
    keep_low1.wait()

    for copy in keeps:
        copy.wait()
    end_unit = a // (cfg.A - 1)
    at_end = (a == 0) | (a == cfg.A - 1)

    def layer_two(k, _):
        hgather.complete(k)
        norm_two(k)

        @pl.when(k == 0)
        def _():
            two.forward(2, 2)
            two.forward(2, 3)

        @pl.when(at_end)
        def _():
            multiply_units(cfg, low, f2, proj, k, end_unit, cfg.A - 1, False)

        @pl.when(jnp.logical_not(at_end))
        def _():
            multiply_units(cfg, low, f2, proj, k, 0, cfg.A, False)

        return 0

    lax.fori_loop(0, CHUNKS, layer_two, 0)
    for p in range(PIECES):
        two.forward(3, p)

    def layer_two_scan(k, _):
        @pl.when(at_end)
        def _():
            multiply_units(cfg, low, f2, proj, k, (cfg.A - 1) * (1 - end_unit), 1, True)

        scan_chunk(cfg, proj, hid, mine, 6, lens, inp, states, tf, tr, carry, k)
        return 0

    lax.fori_loop(0, CHUNKS, layer_two_scan, 0)
    outs = [
        pltpu.make_async_copy(low, low2_out, flush.at[0]),
        pltpu.make_async_copy(z_own, zo_out, flush.at[7]),
        pltpu.make_async_copy(inv, inv_out, flush.at[8]),
        pltpu.make_async_copy(f2, f2_out, flush.at[9]),
    ]
    for copy in outs:
        copy.start()
    hgather.drain()
    one.finish()
    two.finish()
    narrow(cfg, inp, hid_low, cfg.L)
    outs.append(pltpu.make_async_copy(hid_low, hid_out, flush.at[10]))
    outs[-1].start()
    exchange.finish()
    for i in range(cfg.S):
        g = cg[i].astype(F32)
        for l in range(cfg.L):
            inp[l, i * cfg.TP : i * cfg.TP + cfg.T, :] = g[:, 128 * l : 128 * l + 128]
    scan_backward(cfg, proj, hid, mine, 6, lens, states, tf, tr, inp, proj, direct, sums)
    narrow(cfg, proj, p_low, 3 * cfg.L)
    outs.append(pltpu.make_async_copy(p_low, p_out, flush.at[11]))
    outs.append(pltpu.make_async_copy(direct, dir_out, flush.at[12]))
    for copy in outs[-2:]:
        copy.start()
    xgather.drain()
    pltpu.make_async_copy(everyone, everyone, small_send).wait()
    keep_f1.wait()
    for copy in outs:
        copy.wait()


def forward(cfg, x, cot, w1, w2, small):
    low = jax.ShapeDtypeStruct((cfg.S, cfg.T, cfg.D), BF)
    full = jax.ShapeDtypeStruct((cfg.N, cfg.R, 3 * cfg.FW), BF)
    state = keep(cfg, cfg.L)
    vm = lambda t: pltpu.VMEM(t.shape, t.dtype)
    shape = jax.ShapeDtypeStruct
    outs = [
        (low, HBM), (low, HBM), (full, HBM), (full, HBM), (keep(cfg, 5 * cfg.L), HBM),
        (shape((16, cfg.D), F32), VM), (shape((16, cfg.FW), F32), VM), (shape((cfg.S, 128), jnp.int32), VM),
        (shape((cfg.M, cfg.FW), F32), HBM), (shape((cfg.M, 128), F32), HBM), (shape((cfg.M, cfg.FW), BF), HBM),
        (shape((cfg.M, 3 * cfg.FW), BF), HBM), (state, HBM), (shape((8, cfg.FW), F32), VM),
    ]
    return pl.pallas_call(
        functools.partial(forward_kernel, cfg),
        name="forward",
        out_shape=[o for o, _ in outs],
        in_specs=[HBM] * 5,
        out_specs=[p for _, p in outs],
        scratch_shapes=[
            vm(low), vm(low), vm(low), vm(full), vm(full), pltpu.VMEM((cfg.N, 16, 128), BF), pltpu.VMEM((cfg.S, cfg.T, cfg.FW), BF),
            vm(keep(cfg, 3 * cfg.L)),
        ]
        + [vm(state)] * 6
        + [pltpu.VMEM((cfg.M, cfg.FW), BF), pltpu.VMEM((cfg.M, 3 * cfg.FW), BF), pltpu.VMEM((cfg.M, cfg.FW), F32), pltpu.VMEM((cfg.M, 128), F32), pltpu.VMEM((cfg.S, cfg.FW), F32)]
        + [DMA((4,)), DMA(()), DMA(()), DMA((cfg.F,)), DMA((cfg.F,)), DMA((13,))]
        + gather_sems() * 2
        + line_sems(cfg) * 2,
        compiler_params=pltpu.CompilerParams(collective_id=5, has_side_effects=True, vmem_limit_bytes=VMEM_CAP),
    )(x, cot, w1, w2, small)


def inner_kernel(cfg, *refs):
    refs = list(refs)

    def take(n):
        out = refs[:n]
        del refs[:n]
        return out

    p_in, f2_in, low_in, zo_in, inv_in, dir_in, saved, hid_low, mine, lens = take(10)
    p_out, dlow_out, land, hid, norms, sums = take(6)
    p, w, low, z_own, inv, direct, inp, states, tf, tr, proj, grad, ng, stats, mean, group_sum = take(16)
    red_parts, t_parts = take(6), take(2)
    load, low_sem, ss, sr, hs, hr, s2, r2 = take(8)
    red_sems, t_sems = take(6), take(4)
    co = coords(cfg)
    a, zl, b, f = co
    sq = Square(cfg, co)
    s = sq.s
    cols = lambda i: pl.ds(pl.multiple_of(i * cfg.FW, 128), cfg.FW)
    loads = [pltpu.make_async_copy(src, dst, load.at[n]) for n, (src, dst) in enumerate((
        (p_in, p), (f2_in, w), (zo_in, z_own), (inv_in, inv), (dir_in, direct),
        (saved.at[pl.ds(0, cfg.L)], inp), (saved.at[pl.ds(cfg.L, cfg.L)], proj.at[pl.ds(0, cfg.L)]),
        (saved.at[pl.ds(2 * cfg.L, cfg.L)], states), (saved.at[pl.ds(3 * cfg.L, cfg.L)], tf), (saved.at[pl.ds(4 * cfg.L, cfg.L)], tr),
    ))]
    tsum = LineSum(cfg, co, *t_parts, *t_sems)
    loads[0].start()
    tsum.fetch_all(low_in, low, low_sem)
    loads[1].start()
    ready = lambda n: tsum.fetch(low_in, low, low_sem, n).wait()
    greet(group_targets(cfg, a, b, s) + t_targets(cfg, co))
    ex_h = Exchange(cfg, co, lambda i: hid_low.at[pl.ds(i * cfg.T, cfg.T)], lambda i: hid.at[:, cols(i)], hs, hr)
    ex_h.start(1, 5)
    own_hid = pltpu.make_async_copy(ex_h.src(s), ex_h.dst(s), load.at[11])
    own_hid.start()
    red = SquareReduce(sq, *red_parts, red_sems)
    loads[0].wait()

    def product(i, out):
        block = weight_rows(cfg, w, i * (cfg.FW // cfg.R), cfg.FW // cfg.R)

        def body(n, _):
            at = pl.ds(pl.multiple_of(n * 512, 8), 512)
            out[at, :] = lax.dot_general(p[at, :], block, (((1,), (1,)), ((), ())), preferred_element_type=F32).astype(BF)
            return 0

        lax.fori_loop(0, cfg.M // 512, body, 0)

    block_of = grad_block(cfg, low, p, t_parts[0])
    tsum.produce(block_of, 0, 4, ready)
    loads[1].wait()
    for copy in loads[2:]:
        copy.start()
    red.run(product, lambda n: tsum.pump(2, n, n + 1))
    red.pass_on()
    tsum.produce(block_of, 4, 7, ready)
    tsum.pump(1)
    for copy in loads[2:]:
        copy.wait()
    gain = mine[10:11, :]
    eye = (lax.broadcasted_iota(jnp.int32, (128, 128), 0) == lax.broadcasted_iota(jnp.int32, (128, 128), 1)).astype(F32)

    def first_pass(i, carry):
        s0, s1 = carry
        at = pl.ds(pl.multiple_of(i * 128, 8), 128)
        value = red.total(at)
        z = z_own[at, :]
        h = value * gain
        ng[at, :] = h
        for n, x in ((0, h), (1, h * z)):
            col = jnp.sum(x, axis=-1, keepdims=True)
            stats[s, n, pl.ds(i, 1), :] = jnp.sum(col * eye, axis=0, keepdims=True)
        return s0 + jnp.sum(value * z, axis=0, keepdims=True), s1 + jnp.sum(value, axis=0, keepdims=True)

    zero = jnp.zeros((1, cfg.FW), F32)
    carry = (zero, zero)
    per = cfg.M // 128 // CHUNKS
    for c in range(CHUNKS):
        red.receive(c)
        carry = lax.fori_loop(c * per, (c + 1) * per, first_pass, carry)
    norms[0:1, :] = carry[0]
    norms[1:2, :] = carry[1]
    exchange = Exchange(cfg, co, lambda i: stats.at[s], lambda i: stats.at[i], ss, sr)
    exchange.start()
    ex_h.start(5)
    exchange.finish()
    total = stats[0]
    for i in range(1, cfg.F):
        total = total + stats[i]
    mean[...] = total * (1.0 / cfg.D)

    def second_pass(i, _):
        at = pl.ds(pl.multiple_of(i * 128, 8), 128)
        m0 = jnp.sum(mean[0, pl.ds(i, 1), :] * eye, axis=-1, keepdims=True)
        m1 = jnp.sum(mean[1, pl.ds(i, 1), :] * eye, axis=-1, keepdims=True)
        value = (ng[at, :] - m0 - z_own[at, :] * m1) * inv[at, 0:1]
        each = cfg.T // 128
        to = pl.ds(pl.multiple_of((i // each) * cfg.TP + (i % each) * 128, 8), 128)
        for l in range(cfg.L):
            grad[l, to, :] = value[:, 128 * l : 128 * l + 128] + direct[l, to, :]
        return 0

    lax.fori_loop(0, cfg.M // 128, second_pass, 0)
    ex_2 = Exchange(cfg, co, lambda i: group_sum.at[i], lambda i: land.at[i], s2, r2)
    tsum.settle(group_sum, ex_2.piece_sender(PIECES))
    own_sum = pltpu.make_async_copy(group_sum.at[s], land.at[s], load.at[2])
    own_sum.start()
    scan_backward(cfg, proj, inp, mine, 0, lens, states, tf, tr, grad, proj, direct, sums)
    narrow(cfg, proj, p, 3 * cfg.L)
    outs = [pltpu.make_async_copy(p, p_out, load.at[0])]
    outs[0].start()
    red.drain()
    dlow = red_parts[0].at[0]
    narrow(cfg, direct, dlow, cfg.L)
    outs.append(pltpu.make_async_copy(dlow, dlow_out, load.at[1]))
    outs[1].start()
    ex_2.finish()
    own_sum.wait()
    ex_h.finish()
    own_hid.wait()
    tsum.drain()
    for copy in outs:
        copy.wait()


def inner(cfg, p, f2, low, zo, inv, direct, saved, hid_low, mine, lens):
    shape = jax.ShapeDtypeStruct
    state = keep(cfg, cfg.L)
    vm = lambda t: pltpu.VMEM(t.shape, t.dtype)
    part = shape((cfg.F, cfg.R, 3 * cfg.FW), BF)
    return pl.pallas_call(
        functools.partial(inner_kernel, cfg),
        name="inner",
        out_shape=[shape((cfg.M, 3 * cfg.FW), BF), shape((cfg.M, cfg.FW), BF), part, shape((cfg.T, cfg.D), BF), shape((8, cfg.FW), F32), shape((8, cfg.FW), F32)],
        in_specs=[HBM] * 8 + [VM] * 2,
        out_specs=[HBM] * 4 + [VM] * 2,
        scratch_shapes=[vm(p), vm(f2), vm(low), vm(zo), vm(inv)]
        + [vm(state)] * 5
        + [vm(keep(cfg, 3 * cfg.L)), vm(state), pltpu.VMEM((cfg.M, cfg.FW), F32)]
        + [pltpu.VMEM((cfg.F, 2, cfg.M // 128, 128), F32), pltpu.VMEM((2, cfg.M // 128, 128), F32), vm(part)]
        + reduce_parts(cfg.M, cfg.FW)
        + line_parts(cfg)
        + [DMA((12,)), DMA((2 * cfg.A - 1,))] + [DMA((cfg.F,))] * 6
        + reduce_sems()
        + line_sum_sems(cfg),
        compiler_params=pltpu.CompilerParams(collective_id=6, has_side_effects=True, vmem_limit_bytes=VMEM_CAP),
    )(p, f2, low, zo, inv, direct, saved, hid_low, mine, lens)


def final_kernel(cfg, *refs):
    refs = list(refs)

    def take(n):
        out = refs[:n]
        del refs[:n]
        return out

    p_in, f1_in, low_in, dlow, sum2, x, vec, sums1, sums2, norm2 = take(10)
    grad, o1, o2, total = take(4)
    p, w, low, dgot, land1, land2, group_sum, small, sg = take(9)
    red_parts, t_parts = take(6), take(2)
    load, low_sem, small_send, small_recv, ds, dr, s1, r1 = take(8)
    red_sems, t_sems = take(6), take(4)
    co = coords(cfg)
    a, zl, b, f = co
    sq = Square(cfg, co)
    s, me = sq.s, flat(cfg, *co)
    cols = lambda i: pl.ds(pl.multiple_of(i * cfg.FW, 128), cfg.FW)
    loads = [pltpu.make_async_copy(src, dst, load.at[n]) for n, (src, dst) in enumerate(((p_in, p), (f1_in, w)))]
    tsum = LineSum(cfg, co, *t_parts, *t_sems)
    loads[0].start()
    tsum.fetch_all(low_in, low, low_sem)
    loads[1].start()
    ready = lambda n: tsum.fetch(low_in, low, low_sem, n).wait()
    greet_all(cfg, me)
    red = SquareReduce(sq, *red_parts, red_sems)
    ex_d = Exchange(cfg, co, lambda i: dlow.at[pl.ds(i * cfg.T, cfg.T)], lambda i: dgot.at[:, cols(i)], ds, dr)
    ex_d.start()
    copies = [pltpu.make_async_copy(ex_d.src(s), ex_d.dst(s), load.at[3]), pltpu.make_async_copy(sum2, land2, load.at[4])]
    for copy in copies:
        copy.start()
    loads[0].wait()

    def product(i, out):
        data = p[pl.ds(pl.multiple_of(i * cfg.T, 8), cfg.T), :]

        def body(n, _):
            wide_ = cfg.D // 4
            block_ = weight_rows(cfg, w, n * (wide_ // cfg.R), wide_ // cfg.R)
            value = lax.dot_general(data, block_, (((1,), (1,)), ((), ())), preferred_element_type=F32)
            out[:, pl.ds(pl.multiple_of(n * wide_, 128), wide_)] = value.astype(BF)
            return 0

        lax.fori_loop(0, 4, body, 0)

    block_of = grad_block(cfg, low, p, t_parts[0])
    tsum.produce(block_of, 0, 4, ready)
    loads[1].wait()
    red.run(product, lambda n: tsum.pump(2, n, n + 1))
    tsum.produce(block_of, 4, 7, ready)
    ex_1 = Exchange(cfg, co, lambda i: group_sum.at[i], lambda i: land1.at[i], s1, r1)
    red.pass_on()
    tsum.pump(1)
    ex_d.finish()
    for copy in copies:
        copy.wait()
    step = 64

    def body(i, carry):
        s0, s1_ = carry
        at = pl.ds(pl.multiple_of(i * step, 8), step)
        value = red.total(at)
        z, inverse = normalize(x[at, :].astype(F32))
        h = value * vec[4:5, :]
        m0 = jnp.mean(h, axis=-1, keepdims=True)
        m1 = jnp.mean(h * z, axis=-1, keepdims=True)
        grad[at, :] = (h - m0 - z * m1) * inverse + dgot[at, :].astype(F32)
        return s0 + jnp.sum(value * z, axis=0, keepdims=True), s1_ + jnp.sum(value, axis=0, keepdims=True)

    zero = jnp.zeros((1, cfg.D), F32)
    carry = (zero, zero)
    per = cfg.T // step // CHUNKS
    for c in range(CHUNKS):
        red.receive(c)
        carry = lax.fori_loop(c * per, (c + 1) * per, body, carry)
    many = cfg.N // cfg.PER
    small[...] = jnp.zeros_like(small)
    for i in range(cfg.L):
        lanes = slice(128 * i, 128 * i + 128)
        small[s * cfg.L + i, 0:4, :] = sums1[0:4, lanes]
        small[s * cfg.L + i, 6:10, :] = sums2[0:4, lanes]
        small[s * cfg.L + i, 10:12, :] = norm2[0:2, lanes]
    for i in range(many):
        small[i, 4:5, :] = carry[0][:, 128 * i : 128 * i + 128]
        small[i, 5:6, :] = carry[1][:, 128 * i : 128 * i + 128]

    def each(k, _):
        m = (me + k) % cfg.N
        remote(small.at[m // cfg.PER], sg.at[me], small_send, small_recv, (m // cfg.FS, m % cfg.FS)).start()
        return 0

    lax.fori_loop(1, cfg.N, each, 0)
    sg[me] = small[me // cfg.PER]
    tsum.settle(group_sum, ex_1.piece_sender(PIECES))
    land1[s] = group_sum[s]

    def spread(land, out):
        for i in range(cfg.F):
            for c in range(3):
                at = c * cfg.D + i * cfg.FW
                out[:, at : at + cfg.FW] = land[i, :, c * cfg.FW : (c + 1) * cfg.FW].astype(F32)

    spread(land2, o2)
    everyone = sg.at[pl.ds(0, cfg.N - 1)]
    pltpu.make_async_copy(everyone, everyone, small_recv).wait()
    value = sg[0]
    for i in range(1, cfg.N):
        value = value + sg[i]
    total[...] = value
    ex_1.finish()
    spread(land1, o1)
    red.drain()
    tsum.drain()
    pltpu.make_async_copy(everyone, everyone, small_send).wait()


def final(cfg, p, f1, low, dlow, sum2, x, vec, sums1, sums2, norm2):
    shape = jax.ShapeDtypeStruct
    vm = lambda t: pltpu.VMEM(t.shape, t.dtype)
    part = pltpu.VMEM((cfg.F, cfg.R, 3 * cfg.FW), BF)
    out = shape((cfg.R, 3 * cfg.D), F32)
    return pl.pallas_call(
        functools.partial(final_kernel, cfg),
        name="final",
        out_shape=[shape((cfg.T, cfg.D), F32), out, out, shape((16, 128), F32)],
        in_specs=[HBM] * 5 + [VM] * 5,
        out_specs=[VM] * 4,
        scratch_shapes=[vm(p), vm(f1), vm(low), pltpu.VMEM((cfg.T, cfg.D), BF), part, part, part]
        + [pltpu.VMEM((cfg.N // cfg.PER, 16, 128), F32), pltpu.VMEM((cfg.N, 16, 128), F32)]
        + reduce_parts(cfg.T, cfg.D)
        + line_parts(cfg)
        + [DMA((5,)), DMA((2 * cfg.A - 1,)), DMA(()), DMA(())]
        + [DMA((cfg.F,))] * 4
        + reduce_sems()
        + line_sum_sems(cfg),
        compiler_params=pltpu.CompilerParams(collective_id=7, has_side_effects=True, vmem_limit_bytes=VMEM_CAP),
    )(p, f1, low, dlow, sum2, x, vec, sums1, sums2, norm2)


def shards_square(cfg, inputs, cotangent, w1, w2, packed, me):
    low1, low2, full1, full2, saved, vec, mine, lens, z_own, inv, hid2, p2, direct2, sums2 = forward(cfg, inputs[0], cotangent[0], w1, w2, packed)
    p1, direct1, part2, hidden, norm2, sums1 = inner(cfg, p2, full2, low2, z_own, inv, direct2, saved, hid2, mine, lens)
    grad, gw1, gw2, total = final(cfg, p1, full1, low1, direct1, part2, inputs[0], vec, sums1, sums2, norm2)
    total = lax.dynamic_slice(total, (0, (me % cfg.PER) * cfg.R), (16, cfg.R))
    out = [hidden[None], grad[None], gw1] + [total[i] for i in range(6)] + [gw2] + [total[i] for i in range(6, 12)]
    return tuple(out)


def shards(mesh, inputs, lengths, w1, pf1, pr1, bf1, br1, ng1, nb1, w2, pf2, pr2, bf2, br2, ng2, nb2, cotangent):
    _, steps, width = inputs.shape
    cfg = make_cfg(mesh, steps, width)
    a, zl, b, f = coords(cfg)
    j, me = zl * cfg.FS + f, flat(cfg, a, zl, b, f)
    vectors = [pf1, pr1, bf1, br1, ng1, nb1, pf2, pr2, bf2, br2, ng2, nb2, jnp.broadcast_to(lengths.astype(BF), (cfg.R,))]
    packed = jnp.tile(jnp.concatenate([jnp.stack(vectors), jnp.zeros((3, cfg.R), BF)]), (1, cfg.PER))
    lane = lax.broadcasted_iota(jnp.int32, (16, 128), 1)
    packed = jnp.where(lane // cfg.R == me % cfg.PER, packed, jnp.zeros_like(packed))

    square = cfg.ZL == 2 and cfg.FS == 4 and cfg.A == 4 and cfg.X == 1 and cfg.R % 16 == 0 and cfg.FW % 128 == 0
    if square:
        return shards_square(cfg, inputs, cotangent, w1, w2, packed, me)
    xg, cg, full1, full2, smalls = start(cfg, inputs[0], cotangent[0], w1, w2, packed)
    full1, full2 = full1.reshape(cfg.D, 3 * cfg.FW), full2.reshape(cfg.D, 3 * cfg.FW)
    vec = jnp.sum(smalls.astype(F32).reshape(cfg.N // cfg.PER, cfg.PER, 16, 128), axis=1)
    vec = jnp.transpose(vec, (1, 0, 2)).reshape(16, cfg.D)
    mine = lax.dynamic_slice(vec, (0, j * cfg.FW), (16, cfg.FW))
    lens = vec[12].reshape(cfg.A, cfg.ZL, cfg.X, cfg.FS, cfg.R)[..., 0]
    lens = lax.dynamic_index_in_dim(lax.dynamic_index_in_dim(lens, a, 0, False), b, 1, False).reshape(cfg.S)
    lens = jnp.broadcast_to(lens.astype(jnp.int32)[:, None], (cfg.S, 128))

    low1, hid1, hid1_low, inp, cand, states, tf, tr = first(cfg, xg, full1, vec, mine, lens)
    hg = gather_hidden(cfg, hid1_low).reshape(cfg.S, cfg.T, cfg.D)
    low2, hid2_low, grads2, part2, z_own, inv, direct2, sums2 = second(cfg, hg, full2, vec, mine, lens, hid1, cg)
    grad1, norm2 = middle(cfg, part2, z_own, inv, direct2, mine)
    gw2 = wgrad(cfg, low2, grads2)
    grads1, part1, direct1, sums1 = third(cfg, full1, mine, lens, inp, cand, states, tf, tr, grad1)
    gw1 = wgrad(cfg, low1, grads1)
    input_grad, hidden, got1, got2, norm1 = last(cfg, part1, direct1, hid2_low, gw1, gw2, inputs[0], vec)
    s1, s2 = own_sum(cfg, gw1, got1, a, b), own_sum(cfg, gw2, got2, a, b)

    block = jnp.concatenate([sums1[:4], jnp.zeros((2, cfg.FW), F32), sums2[:4], norm2[:2], jnp.zeros((4, cfg.FW), F32)])
    small = lax.dynamic_update_slice(jnp.zeros((16, cfg.D), F32), block, (0, j * cfg.FW))
    small = lax.dynamic_update_slice(small, norm1[:2], (4, 0))
    small = jnp.transpose(small.reshape(16, cfg.N // cfg.PER, 128), (1, 0, 2))
    gw1, gw2, smalls = end(cfg, s1, s2, small)
    total = jnp.sum(smalls, axis=0)
    total = lax.dynamic_slice(total, (0, (me % cfg.PER) * cfg.R), (16, cfg.R))
    out = [hidden[None], input_grad[None], gw1.astype(F32)] + [total[i] for i in range(6)] + [gw2.astype(F32)] + [total[i] for i in range(6, 12)]
    return tuple(out)


def solution(mesh):
    both = ("dp", "fsdp")
    seq, mat, vec = P(both, None, None), P(both, None), P(both)
    return jax.shard_map(
        functools.partial(shards, mesh),
        mesh=mesh,
        in_specs=(seq, vec) + ((mat,) + (vec,) * 6) * 2 + (seq,),
        out_specs=(seq, seq) + ((mat,) + (vec,) * 6) * 2,
        check_vma=False,
    )
```

```python
import functools
from collections import namedtuple

import jax
import jax.numpy as jnp
from jax import lax
from jax.experimental import pallas as pl
from jax.experimental.pallas import tpu as pltpu
from jax.sharding import PartitionSpec as P

MESH = pl.DeviceIdType.MESH
HBM = pl.BlockSpec(memory_space=pltpu.HBM)
VM = pl.BlockSpec(memory_space=pltpu.VMEM)
DMA = pltpu.SemaphoreType.DMA
BF = jnp.bfloat16
F32 = jnp.float32
EPSILON = 1e-05
PAD = 8
VMEM_CAP = 62 << 20

Cfg = namedtuple("Cfg", ("DP", "FS", "N", "A", "ZL", "X", "F", "C", "S", "T", "TP", "D", "FW", "L", "R", "M", "PER"))


def make_cfg(mesh, steps, width):
    dp, fs = mesh.shape["dp"], mesh.shape["fsdp"]
    zl = 2 if fs < 8 and dp % 4 == 0 else 1
    x = 2 if zl == 1 and dp % 2 == 0 else 1
    a = dp // (zl * x)
    f = zl * fs
    fw = width // f
    rows = width // (dp * fs)
    return Cfg(dp, fs, dp * fs, a, zl, x, f, f // 2, f, steps, steps + PAD, width, fw, fw // 128, rows, f * steps, 128 // rows)


def coords(cfg):
    dp, f = lax.axis_index("dp"), lax.axis_index("fsdp")
    b, zl, a = dp % cfg.X, (dp // cfg.X) % cfg.ZL, dp // (cfg.X * cfg.ZL)
    return a, zl, b, f


def device(cfg, a, zl, b, f):
    return ((a * cfg.ZL + zl) * cfg.X + b, f)


def flat(cfg, a, zl, b, f):
    return ((a * cfg.ZL + zl) * cfg.X + b) * cfg.FS + f


def member(cfg, a, b, s):
    return device(cfg, a, s // cfg.FS, b, s % cfg.FS)


def remote(src, dst, send, recv, where):
    return pltpu.make_async_remote_copy(src_ref=src, dst_ref=dst, send_sem=send, recv_sem=recv, device_id=where, device_id_type=MESH)


def greet(targets):
    barrier = pltpu.get_barrier_semaphore()
    for where in targets:
        pl.semaphore_signal(barrier, inc=1, device_id=where, device_id_type=MESH)
    pl.semaphore_wait(barrier, len(targets))


def greet_all(cfg, me):
    barrier = pltpu.get_barrier_semaphore()

    def one(k, _):
        m = (me + k) % cfg.N
        pl.semaphore_signal(barrier, inc=1, device_id=(m // cfg.FS, m % cfg.FS), device_id_type=MESH)
        return 0

    lax.fori_loop(1, cfg.N, one, 0)
    pl.semaphore_wait(barrier, cfg.N - 1)


def group_targets(cfg, a, b, s):
    return [member(cfg, a, b, (s + k) % cfg.F) for k in range(1, cfg.F)]


class Gather:
    def __init__(self, cfg, co, src, slot, send, recv, mate_send, mate_recv):
        self.cfg, self.co, self.src, self.slot = cfg, co, src, slot
        self.sems = send, recv, mate_send, mate_recv
        a, zl, b, f = co
        self.s = zl * cfg.FS + f
        self.cell, self.core = self.s // 2, self.s % 2

    def far(self, k):
        cfg, (a, zl, b, f) = self.cfg, self.co
        send, recv, _, _ = self.sems
        to = member(cfg, a, b, ((self.cell + k) % cfg.C) * 2 + self.core)
        return remote(self.src, self.slot(self.s), send.at[k], recv.at[k], to)

    def near(self, k):
        cfg, (a, zl, b, f) = self.cfg, self.co
        _, _, send, recv = self.sems
        origin = ((self.cell - k + cfg.C) % cfg.C) * 2 + self.core
        src = self.src if k == 0 else self.slot(origin)
        return remote(src, self.slot(origin), send.at[k], recv.at[k], member(cfg, a, b, self.cell * 2 + 1 - self.core))

    def start(self):
        for k in range(1, self.cfg.C):
            self.far(k).start()
        self.near(0).start()

    def finish(self):
        for k in range(1, self.cfg.C):
            self.far(k).wait_recv()
            self.near(k).start()
        for k in range(1, self.cfg.C):
            self.far(k).wait_send()
        for k in range(self.cfg.C):
            self.near(k).wait()


class Exchange:
    def __init__(self, cfg, co, src, dst, send, recv):
        self.cfg, self.co, self.src, self.dst, self.send, self.recv = cfg, co, src, dst, send, recv
        self.s = co[1] * cfg.FS + co[3]

    def copy(self, k):
        a, zl, b, f = self.co
        to = (self.s + k) % self.cfg.F
        return remote(self.src(to), self.dst(self.s), self.send.at[k], self.recv.at[k], member(self.cfg, a, b, to))

    def start(self, begin=1, end=None):
        for k in range(begin, end or self.cfg.F):
            self.copy(k).start()

    def piece_sender(self, pieces):
        count = self.cfg.F // pieces

        def send(p):
            for h in range(count):
                to = p * count + h
                pl.when(to != self.s)(lambda to=to: self.copy((to - self.s + self.cfg.F) % self.cfg.F).start())

        return send

    def finish(self):
        for k in range(1, self.cfg.F):
            self.copy(k).wait()


class WeightGather:
    def __init__(self, cfg, co, w, full, own, send, recv, asend, arecv, bsend, brecv):
        self.cfg, self.co, self.w, self.full = cfg, co, w, full
        self.own, self.send, self.recv = own, send, recv
        self.asend, self.arecv, self.bsend, self.brecv = asend, arecv, bsend, brecv
        self.s = co[1] * cfg.FS + co[3]

    def pieces(self, k):
        cfg, (a, zl, b, f) = self.cfg, self.co
        to = (self.s + k) % cfg.F
        me = flat(cfg, a, zl, b, f)
        for c in range(3):
            src = self.w.at[:, pl.ds(pl.multiple_of(c * cfg.D + to * cfg.FW, 128), cfg.FW)]
            dst = self.full.at[me, :, pl.ds(c * cfg.FW, cfg.FW)]
            if k == 0:
                yield pltpu.make_async_copy(src, dst, self.own.at[c])
            else:
                yield remote(src, dst, self.send.at[k, c], self.recv.at[k, c], member(cfg, a, b, to))

    def start(self):
        for k in range(self.cfg.F):
            for copy in self.pieces(k):
                copy.start()

    def middle(self):
        for k in range(self.cfg.F):
            for copy in self.pieces(k):
                copy.wait()

    def rows_of(self, a, p, b):
        cfg = self.cfg
        count = cfg.FS // 2
        return self.full.at[pl.ds(flat(cfg, a, p // 2, b, 0) + (p % 2) * count, count)]

    def to_a(self, k, p):
        cfg, (a, zl, b, f) = self.cfg, self.co
        rows = self.rows_of(a, p, b)
        return remote(rows, rows, self.asend.at[k, p], self.arecv.at[k, p], device(cfg, (a + k) % cfg.A, zl, b, f))

    def to_b(self, k, ka, p):
        cfg, (a, zl, b, f) = self.cfg, self.co
        rows = self.rows_of((a - ka + cfg.A) % cfg.A, p, b)
        return remote(rows, rows, self.bsend.at[k, ka, p], self.brecv.at[k, ka, p], device(cfg, a, zl, (b + k) % cfg.X, f))

    def start_a(self):
        for p in range(2 * self.cfg.ZL):
            for k in range(1, self.cfg.A):
                self.to_a(k, p).start()

    def start_b(self):
        for p in range(2 * self.cfg.ZL):
            for k in range(1, self.cfg.X):
                self.to_b(k, 0, p).start()

    def start_out(self):
        self.start_a()
        self.start_b()

    def forward(self, p):
        for ka in range(1, self.cfg.A):
            self.to_a(ka, p).wait_recv()
            for k in range(1, self.cfg.X):
                self.to_b(k, ka, p).start()

    def finish(self):
        cfg = self.cfg
        for p in range(2 * cfg.ZL):
            for ka in range(cfg.A):
                for k in range(1, cfg.X):
                    self.to_b(k, ka, p).wait()
            for ka in range(1, cfg.A):
                self.to_a(ka, p).wait_send()

    def finish_out(self):
        for p in range(2 * self.cfg.ZL):
            self.forward(p)
        self.finish()


def t_targets(cfg, co):
    a, zl, b, f = co
    return [device(cfg, (a + way + cfg.A) % cfg.A, zl, b, f) for way in (1, -1)]


def weight_sems(cfg):
    return [DMA((3,)), DMA((cfg.F, 3)), DMA((cfg.F, 3))] + [DMA((cfg.A, 2 * cfg.ZL))] * 2 + [DMA((cfg.X, cfg.A, 2 * cfg.ZL))] * 2


def start_kernel(cfg, x, cot, w1, w2, small, xg, cg, f1, f2, sg, own_sem, small_send, small_recv, gs, gr, gms, gmr, cs, cr, *wsems):
    co = coords(cfg)
    a, zl, b, f = co
    s, me = zl * cfg.FS + f, flat(cfg, *co)
    greet_all(cfg, me)
    weights = [WeightGather(cfg, co, w1, f1, *wsems[:7]), WeightGather(cfg, co, w2, f2, *wsems[7:])]
    weights[0].start()
    gather = Gather(cfg, co, x, lambda i: xg.at[i], gs, gr, gms, gmr)
    gather.start()

    def each(k, _):
        m = (me + k) % cfg.N
        remote(small, sg.at[me], small_send, small_recv, (m // cfg.FS, m % cfg.FS)).start()
        return 0

    lax.fori_loop(1, cfg.N, each, 0)
    weights[1].start()
    exchange = Exchange(cfg, co, lambda i: cot.at[:, pl.ds(pl.multiple_of(i * cfg.FW, 128), cfg.FW)], lambda i: cg.at[i], cs, cr)
    exchange.start()
    locals_ = [
        pltpu.make_async_copy(x, xg.at[s], own_sem.at[0]),
        pltpu.make_async_copy(cot.at[:, pl.ds(pl.multiple_of(s * cfg.FW, 128), cfg.FW)], cg.at[s], own_sem.at[1]),
        pltpu.make_async_copy(small, sg.at[me], own_sem.at[2]),
    ]
    for copy in locals_:
        copy.start()
    weights[0].middle()
    weights[0].start_out()
    weights[1].middle()
    gather.finish()
    weights[0].finish_out()
    weights[1].start_out()
    exchange.finish()
    weights[1].finish_out()
    everyone = sg.at[pl.ds(0, cfg.N - 1)]
    pltpu.make_async_copy(everyone, everyone, small_recv).wait()
    pltpu.make_async_copy(everyone, everyone, small_send).wait()
    for copy in locals_:
        copy.wait()


def start(cfg, x, cot, w1, w2, small):
    full = jax.ShapeDtypeStruct((cfg.N, cfg.R, 3 * cfg.FW), BF)
    return pl.pallas_call(
        functools.partial(start_kernel, cfg),
        name="start",
        out_shape=(
            jax.ShapeDtypeStruct((cfg.S, cfg.T, cfg.D), BF),
            jax.ShapeDtypeStruct((cfg.S, cfg.T, cfg.FW), BF),
            full,
            full,
            jax.ShapeDtypeStruct((cfg.N, 16, 128), BF),
        ),
        in_specs=[HBM] * 5,
        out_specs=[HBM] * 5,
        scratch_shapes=[DMA((3,)), DMA(()), DMA(())] + [DMA((cfg.C,))] * 4 + [DMA((cfg.F,))] * 2 + weight_sems(cfg) * 2,
        compiler_params=pltpu.CompilerParams(collective_id=0, has_side_effects=True),
    )(x, cot, w1, w2, small)


def rows(cfg, ref, t, first, count):
    return jnp.concatenate([ref[first + i, pl.ds(t, cfg.S, stride=cfg.TP), :] for i in range(count)], axis=1)


def put(cfg, ref, t, value, first=0):
    for i in range(value.shape[1] // 128):
        ref[first + i, pl.ds(t, cfg.S, stride=cfg.TP), :] = value[:, 128 * i : 128 * i + 128]


def wide(cfg, ref, row):
    return jnp.broadcast_to(ref[row : row + 1, :], (cfg.S, cfg.FW))


def scan_forward(cfg, proj, inp, vec, base, lens, hid, states, tf_ref, tr_ref):
    half_pf, half_pr = 0.5 * wide(cfg, vec, base), 0.5 * wide(cfg, vec, base + 1)
    half_bf, half_br = 0.5 * wide(cfg, vec, base + 2), 0.5 * wide(cfg, vec, base + 3)
    live = jnp.broadcast_to(lens[:, 0:1], (cfg.S, cfg.FW))

    def step(t, c):
        u, p, q = (rows(cfg, proj, t, i * cfg.L, cfg.L) for i in range(3))
        here = rows(cfg, inp, t, 0, cfg.L)
        p, q, hu, hc = 0.5 * p + half_bf, 0.5 * q + half_br, 0.5 * u, 0.5 * c
        tf = jnp.tanh(p + half_pf * c)
        tr = jnp.tanh(q + half_pr * c)
        new = (hc + hu) + tf * (hc - hu)
        out = jnp.where(t < live, 0.5 * (here + new) + 0.5 * tr * (new - here), 0.0)
        put(cfg, hid, t, out)
        put(cfg, states, t, new)
        put(cfg, tf_ref, t, tf)
        put(cfg, tr_ref, t, tr)
        return new

    lax.fori_loop(0, cfg.T, step, jnp.zeros((cfg.S, cfg.FW), F32), unroll=4)


def scan_backward(cfg, cand, inp, vec, base, lens, states, tf_ref, tr_ref, grad, grads, direct, sums):
    pf, pr = wide(cfg, vec, base), wide(cfg, vec, base + 1)
    live = jnp.broadcast_to(lens[:, 0:1], (cfg.S, cfg.FW))

    def step(i, carry):
        e, new, s0, s1, s2, s3 = carry
        t = cfg.T - 1 - i
        u, here, g = rows(cfg, cand, t, 0, cfg.L), rows(cfg, inp, t, 0, cfg.L), rows(cfg, grad, t, 0, cfg.L)
        f = 0.5 * rows(cfg, tf_ref, t, 0, cfg.L) + 0.5
        r = 0.5 * rows(cfg, tr_ref, t, 0, cfg.L) + 0.5
        c = jnp.where(t > 0, rows(cfg, states, jnp.maximum(t - 1, 0), 0, cfg.L), 0.0)
        k = jnp.where(t < live, g, 0.0)
        kr = k * r
        rest = 1.0 - f
        w = (c - u) * (f * rest)
        dq = (k - kr) * (new - here) * r
        s = e + kr
        dp = s * w
        put(cfg, grads, t, s * rest, 0)
        put(cfg, grads, t, dp, cfg.L)
        put(cfg, grads, t, dq, 2 * cfg.L)
        put(cfg, direct, t, k - kr)
        e = s * (f + w * pf) + dq * pr
        return e, c, s0 + dp * c, s1 + dq * c, s2 + dp, s3 + dq

    zero = jnp.zeros((cfg.S, cfg.FW), F32)
    out = lax.fori_loop(0, cfg.T, step, (zero, rows(cfg, states, cfg.T - 1, 0, cfg.L)) + (zero,) * 4, unroll=4)
    for i in range(4):
        sums[i : i + 1, :] = jnp.sum(out[2 + i], axis=0, keepdims=True)


def normalize(x):
    center = x - jnp.mean(x, axis=-1, keepdims=True)
    inverse = lax.rsqrt(jnp.mean(center * center, axis=-1, keepdims=True) + EPSILON)
    return center * inverse, inverse


def project(cfg, z, gain, shift, w, low, proj, s):
    lowered = (z * gain + shift).astype(BF)
    low[0] = lowered
    out = jnp.dot(lowered, w[...], preferred_element_type=F32)
    base = pl.multiple_of(s * cfg.TP, 8)
    for i in range(3 * cfg.L):
        proj[i, pl.ds(base, cfg.T), :] = out[:, 128 * i : 128 * i + 128]


def seq_block(cfg, ref, i, s):
    return ref[i, pl.ds(pl.multiple_of(s * cfg.TP, 8), cfg.T), :]


def narrow(cfg, src, dst, count):
    for i in range(count):
        for s in range(cfg.S):
            dst[s * cfg.T : (s + 1) * cfg.T, 128 * i : 128 * i + 128] = src[i, s * cfg.TP : s * cfg.TP + cfg.T, :].astype(dst.dtype)


def first_kernel(cfg, x, w, vec, mine, lens, low, hid, hid_low, inp, cand, states, tf, tr, proj):
    s = pl.program_id(0)
    _, zl, _, f = coords(cfg)
    j = zl * cfg.FS + f
    data = x[0].astype(F32)
    z, _ = normalize(data)
    project(cfg, z, vec[4:5, :], vec[5:6, :], w, low, proj, s)
    own = x[0, :, pl.ds(pl.multiple_of(j * cfg.FW, 128), cfg.FW)].astype(F32)
    for i in range(cfg.L):
        inp[i, pl.ds(pl.multiple_of(s * cfg.TP, 8), cfg.T), :] = own[:, 128 * i : 128 * i + 128]

    @pl.when(s == cfg.S - 1)
    def _():
        scan_forward(cfg, proj, inp, mine, 0, lens, hid, states, tf, tr)
        narrow(cfg, hid, hid_low, cfg.L)
        for i in range(cfg.L):
            cand[i] = proj[i]


def keep(cfg, count):
    return jax.ShapeDtypeStruct((count, cfg.S * cfg.TP, 128), F32)


def const(shape):
    return pl.BlockSpec(shape, lambda i: (0,) * len(shape))


def first(cfg, x, w, vec, mine, lens):
    state = keep(cfg, cfg.L)
    spec = const(state.shape)
    return pl.pallas_call(
        functools.partial(first_kernel, cfg),
        name="first",
        grid=(cfg.S,),
        out_shape=(jax.ShapeDtypeStruct((cfg.S, cfg.T, cfg.D), BF), state, jax.ShapeDtypeStruct((cfg.M, cfg.FW), BF)) + (state,) * 5,
        in_specs=[pl.BlockSpec((1, cfg.T, cfg.D), lambda i: (i, 0, 0)), const(w.shape), const(vec.shape), const(mine.shape), const(lens.shape)],
        out_specs=[pl.BlockSpec((1, cfg.T, cfg.D), lambda i: (i, 0, 0)), spec, const((cfg.M, cfg.FW))] + [spec] * 5,
        scratch_shapes=[pltpu.VMEM((3 * cfg.L, cfg.S * cfg.TP, 128), F32)],
        compiler_params=pltpu.CompilerParams(vmem_limit_bytes=VMEM_CAP),
    )(x, w, vec, mine, lens)


def second_kernel(cfg, x, w, vec, mine, lens, inp, grad_in, low, hid_low, grads_low, part, z_own, inv, direct, sums, proj, hid, states, tf, tr, grad, grads):
    i = pl.program_id(0)
    _, zl, _, f = coords(cfg)
    j = zl * cfg.FS + f

    @pl.when(i < cfg.S)
    def _():
        z, inverse = normalize(x[0].astype(F32))
        project(cfg, z, vec[10:11, :], vec[11:12, :], w, low, proj, i)
        at = pl.ds(pl.multiple_of(i * cfg.T, 8), cfg.T)
        inv[at, :] = jnp.broadcast_to(inverse, (cfg.T, 128))
        raw = x[0, :, pl.ds(pl.multiple_of(j * cfg.FW, 128), cfg.FW)].astype(F32)
        mean = jnp.mean(x[0].astype(F32), axis=-1, keepdims=True)
        z_own[at, :] = (raw - mean) * inverse

    @pl.when(i == cfg.S - 1)
    def _():
        for s in range(cfg.S):
            g = grad_in[s].astype(F32)
            for l in range(cfg.L):
                grad[l, s * cfg.TP : s * cfg.TP + cfg.T, :] = g[:, 128 * l : 128 * l + 128]
        scan_forward(cfg, proj, inp, mine, 6, lens, hid, states, tf, tr)
        narrow(cfg, hid, hid_low, cfg.L)
        scan_backward(cfg, proj, inp, mine, 6, lens, states, tf, tr, grad, grads, direct, sums)
        narrow(cfg, grads, grads_low, 3 * cfg.L)

    @pl.when(i >= cfg.S)
    def _():
        k = i - cfg.S
        block = w[pl.ds(pl.multiple_of(k * cfg.FW, 8), cfg.FW), :]
        part[0] = lax.dot_general(grads_low[...], block, (((1,), (1,)), ((), ())), preferred_element_type=F32).astype(BF)


def second(cfg, x, w, vec, mine, lens, inp, grad_in):
    state = keep(cfg, cfg.L)
    spec = const(state.shape)
    big = pltpu.VMEM(state.shape, F32)
    last = cfg.S - 1
    one = pl.BlockSpec((1, cfg.T, cfg.D), lambda i: (jnp.minimum(i, last), 0, 0))
    return pl.pallas_call(
        functools.partial(second_kernel, cfg),
        name="second",
        grid=(cfg.S + cfg.F,),
        out_shape=(
            jax.ShapeDtypeStruct((cfg.S, cfg.T, cfg.D), BF),
            jax.ShapeDtypeStruct((cfg.M, cfg.FW), BF),
            jax.ShapeDtypeStruct((cfg.M, 3 * cfg.FW), BF),
            jax.ShapeDtypeStruct((cfg.F, cfg.M, cfg.FW), BF),
            jax.ShapeDtypeStruct((cfg.M, cfg.FW), F32),
            jax.ShapeDtypeStruct((cfg.M, 128), F32),
            state,
            jax.ShapeDtypeStruct((8, cfg.FW), F32),
        ),
        in_specs=[one, const(w.shape), const(vec.shape), const(mine.shape), const(lens.shape), spec, const(grad_in.shape)],
        out_specs=[
            one,
            const((cfg.M, cfg.FW)),
            const((cfg.M, 3 * cfg.FW)),
            pl.BlockSpec((1, cfg.M, cfg.FW), lambda i: (jnp.maximum(i - cfg.S, 0), 0, 0)),
            const((cfg.M, cfg.FW)),
            const((cfg.M, 128)),
            spec,
            const((8, cfg.FW)),
        ],
        scratch_shapes=[pltpu.VMEM((3 * cfg.L, cfg.S * cfg.TP, 128), F32)] + [big] * 5 + [pltpu.VMEM((3 * cfg.L, cfg.S * cfg.TP, 128), F32)],
        compiler_params=pltpu.CompilerParams(vmem_limit_bytes=VMEM_CAP),
    )(x, w, vec, mine, lens, inp, grad_in)


def third_kernel(cfg, w, mine, lens, inp, cand, states, tf, tr, grad, grads_low, part, direct_low, sums, grads, direct):
    s = pl.program_id(0)

    @pl.when(s == 0)
    def _():
        scan_backward(cfg, cand, inp, mine, 0, lens, states, tf, tr, grad, grads, direct, sums)
        narrow(cfg, grads, grads_low, 3 * cfg.L)
        narrow(cfg, direct, direct_low, cfg.L)

    at = pl.ds(pl.multiple_of(s * cfg.T, 8), cfg.T)
    part[0] = lax.dot_general(grads_low[at, :], w[...], (((1,), (1,)), ((), ())), preferred_element_type=F32).astype(BF)


def third(cfg, w, mine, lens, inp, cand, states, tf, tr, grad):
    state = keep(cfg, cfg.L)
    spec = const(state.shape)
    return pl.pallas_call(
        functools.partial(third_kernel, cfg),
        name="third",
        grid=(cfg.S,),
        out_shape=(
            jax.ShapeDtypeStruct((cfg.M, 3 * cfg.FW), BF),
            jax.ShapeDtypeStruct((cfg.S, cfg.T, cfg.D), BF),
            jax.ShapeDtypeStruct((cfg.M, cfg.FW), BF),
            jax.ShapeDtypeStruct((8, cfg.FW), F32),
        ),
        in_specs=[const(w.shape), const(mine.shape), const(lens.shape)] + [spec] * 6,
        out_specs=[const((cfg.M, 3 * cfg.FW)), pl.BlockSpec((1, cfg.T, cfg.D), lambda i: (i, 0, 0)), const((cfg.M, cfg.FW)), const((8, cfg.FW))],
        scratch_shapes=[pltpu.VMEM((3 * cfg.L, cfg.S * cfg.TP, 128), F32), pltpu.VMEM(state.shape, F32)],
        compiler_params=pltpu.CompilerParams(vmem_limit_bytes=VMEM_CAP),
    )(w, mine, lens, inp, cand, states, tf, tr, grad)


def gather_kernel(cfg, x, out, own, gs, gr, gms, gmr):
    co = coords(cfg)
    a, zl, b, f = co
    s = zl * cfg.FS + f
    cell, core = s // 2, s % 2
    greet([member(cfg, a, b, ((cell + k) % cfg.C) * 2 + core) for k in range(1, cfg.C)] + [member(cfg, a, b, cell * 2 + 1 - core)])
    slot = lambda i: out.at[:, pl.ds(pl.multiple_of(i * cfg.FW, 128), cfg.FW)]
    gather = Gather(cfg, co, x, slot, gs, gr, gms, gmr)
    gather.start()
    copy = pltpu.make_async_copy(x, slot(s), own)
    copy.start()
    gather.finish()
    copy.wait()


def gather_hidden(cfg, x):
    return pl.pallas_call(
        functools.partial(gather_kernel, cfg),
        name="gather_hidden",
        out_shape=jax.ShapeDtypeStruct((cfg.M, cfg.D), BF),
        in_specs=[HBM],
        out_specs=HBM,
        scratch_shapes=[DMA(())] + [DMA((cfg.C,))] * 4,
        compiler_params=pltpu.CompilerParams(collective_id=1, has_side_effects=True),
    )(x)


class Reduce:
    def __init__(self, cfg, co, part, own, mate, out, got, load, ms, mr, fs, fr):
        self.cfg, self.co, self.part, self.own, self.mate, self.out, self.got = cfg, co, part, own, mate, out, got
        self.load, self.ms, self.mr, self.fs, self.fr = load, ms, mr, fs, fr
        self.s = co[1] * cfg.FS + co[3]
        self.cell, self.core = self.s // 2, self.s % 2

    def target(self, k):
        return (self.cell + k) % self.cfg.C

    def to_mate(self, k):
        a, _, b, _ = self.co
        return remote(
            self.part.at[self.target(k) * 2 + 1 - self.core], self.mate.at[k], self.ms.at[k], self.mr.at[k],
            member(self.cfg, a, b, self.cell * 2 + 1 - self.core),
        )

    def fetch(self, k):
        return pltpu.make_async_copy(self.part.at[self.target(k) * 2 + self.core], self.own.at[k], self.load.at[k])

    def far(self, k):
        a, _, b, _ = self.co
        return remote(self.out.at[k - 1], self.got.at[k - 1], self.fs.at[k], self.fr.at[k], member(self.cfg, a, b, self.target(k) * 2 + self.core))

    def order(self):
        return list(range(1, self.cfg.C)) + [0]

    def start(self):
        for k in self.order():
            self.to_mate(k).start()
            self.fetch(k).start()

    def middle(self):
        rows_, _ = self.own.shape[1:]
        step = 256 if rows_ % 256 == 0 else rows_
        for k in self.order():
            self.to_mate(k).wait_recv()
            self.fetch(k).wait()
            if k:

                def add(i, _):
                    at = pl.ds(pl.multiple_of(i * step, 8), step)
                    self.out[k - 1, at, :] = (self.own[k, at, :].astype(F32) + self.mate[k, at, :].astype(F32)).astype(BF)
                    return 0

                lax.fori_loop(0, rows_ // step, add, 0)
                self.far(k).start()

    def finish(self):
        for k in range(1, self.cfg.C):
            self.far(k).wait()
        for k in range(self.cfg.C):
            self.to_mate(k).wait_send()

    def total(self, at):
        value = self.own[0, at, :].astype(F32) + self.mate[0, at, :].astype(F32)
        for k in range(1, self.cfg.C):
            value = value + self.got[k - 1, at, :].astype(F32)
        return value


def reduce_scratch(cfg, rows_, cols):
    return [pltpu.VMEM((cfg.C, rows_, cols), BF)] * 2 + [pltpu.VMEM((cfg.C - 1, rows_, cols), BF)] * 2 + [DMA((cfg.C,))] * 5


def middle_kernel(cfg, part, z_own, inv, direct, mine, grad, sums, ng, stats, mean, *sc):
    red_sc, (ss, sr) = sc[:9], sc[9:]
    co = coords(cfg)
    a, zl, b, f = co
    s = zl * cfg.FS + f
    greet(group_targets(cfg, a, b, s))
    red = Reduce(cfg, co, part, *red_sc)
    red.start()
    red.middle()
    red.finish()
    gain = mine[10:11, :]
    eye = (lax.broadcasted_iota(jnp.int32, (128, 128), 0) == lax.broadcasted_iota(jnp.int32, (128, 128), 1)).astype(F32)

    def first_pass(i, carry):
        s0, s1 = carry
        at = pl.ds(pl.multiple_of(i * 128, 8), 128)
        value = red.total(at)
        z = z_own[at, :]
        h = value * gain
        ng[at, :] = h
        for n, x in ((0, h), (1, h * z)):
            col = jnp.sum(x, axis=-1, keepdims=True)
            stats[s, n, pl.ds(i, 1), :] = jnp.sum(col * eye, axis=0, keepdims=True)
        return s0 + jnp.sum(value * z, axis=0, keepdims=True), s1 + jnp.sum(value, axis=0, keepdims=True)

    zero = jnp.zeros((1, cfg.FW), F32)
    s0, s1 = lax.fori_loop(0, cfg.M // 128, first_pass, (zero, zero))
    sums[0:1, :] = s0
    sums[1:2, :] = s1
    exchange = Exchange(cfg, co, lambda i: stats.at[s], lambda i: stats.at[i], ss, sr)
    exchange.start()
    exchange.finish()
    total = stats[0]
    for i in range(1, cfg.F):
        total = total + stats[i]
    mean[...] = total * (1.0 / cfg.D)

    def second_pass(i, _):
        at = pl.ds(pl.multiple_of(i * 128, 8), 128)
        m0 = jnp.sum(mean[0, pl.ds(i, 1), :] * eye, axis=-1, keepdims=True)
        m1 = jnp.sum(mean[1, pl.ds(i, 1), :] * eye, axis=-1, keepdims=True)
        value = (ng[at, :] - m0 - z_own[at, :] * m1) * inv[at, 0:1]
        per = cfg.T // 128
        to = pl.ds(pl.multiple_of((i // per) * cfg.TP + (i % per) * 128, 8), 128)
        for l in range(cfg.L):
            grad[l, to, :] = value[:, 128 * l : 128 * l + 128] + direct[l, to, :]
        return 0

    lax.fori_loop(0, cfg.M // 128, second_pass, 0)


def middle(cfg, part, z_own, inv, direct, mine):
    return pl.pallas_call(
        functools.partial(middle_kernel, cfg),
        name="middle",
        out_shape=(keep(cfg, cfg.L), jax.ShapeDtypeStruct((8, cfg.FW), F32)),
        in_specs=[HBM] + [VM] * 4,
        out_specs=[VM] * 2,
        scratch_shapes=[
            pltpu.VMEM((cfg.M, cfg.FW), F32),
            pltpu.VMEM((cfg.F, 2, cfg.M // 128, 128), F32),
            pltpu.VMEM((2, cfg.M // 128, 128), F32),
        ]
        + reduce_scratch(cfg, cfg.M, cfg.FW)
        + [DMA((cfg.F,))] * 2,
        compiler_params=pltpu.CompilerParams(collective_id=2, has_side_effects=True, vmem_limit_bytes=VMEM_CAP),
    )(part, z_own, inv, direct, mine)


def last_kernel(cfg, part, dir_low, hid_low, g1, g2, x, vec, grad, hid, b1, b2, sums, dgot, *sc):
    red_sc, sc = sc[:9], sc[9:]
    own, ds, dr, hs, hr = sc[:5]
    ts = sc[5:]
    co = coords(cfg)
    a, zl, b, f = co
    s = zl * cfg.FS + f
    barrier_to = group_targets(cfg, a, b, s)
    others = [(ka, kb) for ka in range(cfg.A) for kb in range(cfg.X) if ka or kb]
    far = lambda ka, kb: ((a + ka) % cfg.A, (b + kb) % cfg.X)
    for ka, kb in others:
        ta, tb = far(ka, kb)
        barrier_to.append(device(cfg, ta, zl, tb, f))
    greet(barrier_to)
    red = Reduce(cfg, co, part, *red_sc)
    red.start()

    def across(layer, o, z):
        src, dst = ((g1, b1), (g2, b2))[layer]
        ta, tb = far(*others[o])
        rows_ = src.at[pl.ds(flat(cfg, ta, z, tb, 0), cfg.FS)]
        return remote(rows_, dst.at[o, pl.ds(z * cfg.FS, cfg.FS)], ts[2 * layer].at[o, z], ts[2 * layer + 1].at[o, z], device(cfg, ta, zl, tb, f))

    for layer in (1, 0):
        for o in range(len(others)):
            for z in range(cfg.ZL):
                across(layer, o, z).start()
    ex_d = Exchange(cfg, co, lambda i: dir_low.at[pl.ds(i * cfg.T, cfg.T)], lambda i: dgot.at[:, pl.ds(pl.multiple_of(i * cfg.FW, 128), cfg.FW)], ds, dr)
    ex_h = Exchange(cfg, co, lambda i: hid_low.at[pl.ds(i * cfg.T, cfg.T)], lambda i: hid.at[:, pl.ds(pl.multiple_of(i * cfg.FW, 128), cfg.FW)], hs, hr)
    ex_d.start()
    ex_h.start()
    copies = [pltpu.make_async_copy(e.src(s), e.dst(s), own.at[i]) for i, e in enumerate((ex_d, ex_h))]
    for copy in copies:
        copy.start()
    red.middle()
    red.finish()
    ex_d.finish()
    for copy in copies:
        copy.wait()
    step = 64

    def body(i, carry):
        s0, s1 = carry
        at = pl.ds(pl.multiple_of(i * step, 8), step)
        value = red.total(at)
        z, inverse = normalize(x[at, :].astype(F32))
        h = value * vec[4:5, :]
        m0 = jnp.mean(h, axis=-1, keepdims=True)
        m1 = jnp.mean(h * z, axis=-1, keepdims=True)
        grad[at, :] = (h - m0 - z * m1) * inverse + dgot[at, :].astype(F32)
        return s0 + jnp.sum(value * z, axis=0, keepdims=True), s1 + jnp.sum(value, axis=0, keepdims=True)

    zero = jnp.zeros((1, cfg.D), F32)
    s0, s1 = lax.fori_loop(0, cfg.T // step, body, (zero, zero))
    sums[0:1, :] = s0
    sums[1:2, :] = s1
    ex_h.finish()
    for layer in (1, 0):
        for o in range(len(others)):
            for z in range(cfg.ZL):
                across(layer, o, z).wait()


def last(cfg, part, dir_low, hid_low, g1, g2, x, vec):
    n = cfg.A * cfg.X - 1
    got = jax.ShapeDtypeStruct((n, cfg.F, cfg.R, 3 * cfg.FW), BF)
    return pl.pallas_call(
        functools.partial(last_kernel, cfg),
        name="last",
        out_shape=(
            jax.ShapeDtypeStruct((cfg.T, cfg.D), F32),
            jax.ShapeDtypeStruct((cfg.T, cfg.D), BF),
            got,
            got,
            jax.ShapeDtypeStruct((8, cfg.D), F32),
        ),
        in_specs=[HBM] * 5 + [VM] * 2,
        out_specs=[VM, HBM, HBM, HBM, VM],
        scratch_shapes=[pltpu.VMEM((cfg.T, cfg.D), BF)]
        + reduce_scratch(cfg, cfg.T, cfg.D)
        + [DMA((2,))]
        + [DMA((cfg.F,))] * 4
        + [DMA((n, cfg.ZL))] * 4,
        compiler_params=pltpu.CompilerParams(collective_id=3, has_side_effects=True, vmem_limit_bytes=VMEM_CAP),
    )(part, dir_low, hid_low, g1, g2, x, vec)


def end_kernel(cfg, w1, w2, small, o1, o2, sg, own, small_send, small_recv, *sc):
    co = coords(cfg)
    a, zl, b, f = co
    s, me = zl * cfg.FS + f, flat(cfg, *co)
    greet_all(cfg, me)

    def pieces(layer, k):
        src, dst = ((w1, o1), (w2, o2))[layer]
        to = (s + k) % cfg.F
        for c in range(3):
            piece = src.at[to, :, pl.ds(c * cfg.FW, cfg.FW)]
            place = dst.at[:, pl.ds(pl.multiple_of(c * cfg.D + s * cfg.FW, 128), cfg.FW)]
            if k == 0:
                yield pltpu.make_async_copy(piece, place, own.at[layer, c])
            else:
                yield remote(piece, place, sc[2 * layer].at[k, c], sc[2 * layer + 1].at[k, c], member(cfg, a, b, to))

    every = [(layer, k) for layer in range(2) for k in range(cfg.F)]
    for layer, k in every:
        for copy in pieces(layer, k):
            copy.start()

    def each(k, _):
        m = (me + k) % cfg.N
        remote(small.at[m // cfg.PER], sg.at[me], small_send, small_recv, (m // cfg.FS, m % cfg.FS)).start()
        return 0

    lax.fori_loop(1, cfg.N, each, 0)
    mine = pltpu.make_async_copy(small.at[me // cfg.PER], sg.at[me], own.at[2, 0])
    mine.start()
    for layer, k in every:
        for copy in pieces(layer, k):
            copy.wait()
    mine.wait()
    everyone = sg.at[pl.ds(0, cfg.N - 1)]
    pltpu.make_async_copy(everyone, everyone, small_recv).wait()
    pltpu.make_async_copy(everyone, everyone, small_send).wait()


def end(cfg, w1, w2, small):
    out = jax.ShapeDtypeStruct((cfg.R, 3 * cfg.D), BF)
    return pl.pallas_call(
        functools.partial(end_kernel, cfg),
        name="end",
        out_shape=(out, out, jax.ShapeDtypeStruct((cfg.N,) + small.shape[1:], F32)),
        in_specs=[HBM] * 3,
        out_specs=[HBM] * 3,
        scratch_shapes=[DMA((3, 3)), DMA(()), DMA(())] + [DMA((cfg.F, 3))] * 4,
        compiler_params=pltpu.CompilerParams(collective_id=4, has_side_effects=True),
    )(w1, w2, small)


def wgrad(cfg, low, grads):
    out = lax.dot_general(low.reshape(cfg.M, cfg.D), grads, (((0,), (0,)), ((), ())), preferred_element_type=F32)
    return out.astype(BF).reshape(cfg.N, cfg.R, 3 * cfg.FW)


def own_sum(cfg, g, got, a, b):
    mine = lax.dynamic_index_in_dim(lax.dynamic_index_in_dim(g.reshape(cfg.A, cfg.ZL, cfg.X, cfg.FS, cfg.R, 3 * cfg.FW), a, 0, False), b, 1, False)
    mine = mine.reshape(cfg.F, cfg.R, 3 * cfg.FW)
    return (mine.astype(F32) + jnp.sum(got.astype(F32), axis=0)).astype(BF)


CHUNKS = 4


class Square:
    def __init__(self, cfg, co):
        self.cfg, self.co = cfg, co
        a, zl, b, f = co
        y, self.core = f // 2, f % 2
        self.cells = [(zl, y), (zl, 1 - y), (1 - zl, y), (1 - zl, 1 - y)]
        self.s = zl * cfg.FS + f

    def index(self, k, mate=False):
        zl, y = self.cells[k]
        return zl * self.cfg.FS + y * 2 + ((1 - self.core) if mate else self.core)

    def place(self, k, mate=False):
        a, _, b, _ = self.co
        zl, y = self.cells[k]
        return device(self.cfg, a, zl, b, y * 2 + ((1 - self.core) if mate else self.core))


class SquareGather:
    def __init__(self, sq, slot, by_y, sems, src=None):
        self.sq, self.slot, self.by_y = sq, slot, by_y
        self.src = src or (lambda c: slot(sq.s, c))
        self.ns, self.nr, self.fs, self.fr, self.ms, self.mr = sems

    def side(self, k, c):
        sq = self.sq
        return remote(self.src(c), self.slot(sq.s, c), self.ns.at[k, c], self.nr.at[k, c], sq.place(k))

    def across(self, c):
        sq = self.sq
        cfg, (a, zl, b, f) = sq.cfg, sq.co
        y, v = f // 2, self.by_y(c)
        via = (zl + (1 - v) * (1 - 2 * zl)) * cfg.FS + (y + v * (1 - 2 * y)) * 2 + sq.core
        to = device(cfg, a, zl + v * (1 - 2 * zl), b, (y + (1 - v) * (1 - 2 * y)) * 2 + sq.core)
        block = self.slot(via, c)
        return remote(block, block, self.fs.at[c], self.fr.at[c], to)

    def near(self, k, c):
        sq = self.sq
        block = self.slot(sq.index(k), c)
        return remote(self.src(c) if k == 0 else block, block, self.ms.at[k, c], self.mr.at[k, c], sq.place(0, True))

    def push(self, c):
        self.side(1, c).start()
        self.side(2, c).start()
        self.near(0, c).start()

    def arrive(self, c):
        self.side(1, c).wait_recv()
        self.side(2, c).wait_recv()
        self.across(c).start()
        self.near(1, c).start()
        self.near(2, c).start()

    def complete(self, c):
        self.across(c).wait_recv()
        self.near(3, c).start()
        for k in range(4):
            self.near(k, c).wait_recv()

    def drain(self):
        def one(c, _):
            self.side(1, c).wait_send()
            self.side(2, c).wait_send()
            self.across(c).wait_send()
            for k in range(4):
                self.near(k, c).wait_send()
            return 0

        lax.fori_loop(0, CHUNKS, one, 0)


def gather_sems():
    return [DMA((3, CHUNKS))] * 2 + [DMA((CHUNKS,))] * 2 + [DMA((4, CHUNKS))] * 2


class SquareReduce:
    def __init__(self, sq, to_mate, own, mate, landed, gy, gz, sems):
        self.sq, self.to_mate, self.own, self.mate = sq, to_mate, own, mate
        self.landed, self.got = landed, (None, gy, gz)
        self.ms, self.mr, self.ds, self.dr, self.gs, self.gr = sems
        self.rows = own.shape[1] // CHUNKS

    def at(self, c):
        return pl.ds(c * self.rows, self.rows)

    def near(self, k, c):
        return remote(self.to_mate.at[k, self.at(c)], self.mate.at[k, self.at(c)], self.ms.at[k, c], self.mr.at[k, c], self.sq.place(0, True))

    def far(self, c):
        return remote(self.own.at[3, self.at(c)], self.landed.at[self.at(c)], self.ds.at[c], self.dr.at[c], self.sq.place(1 + c % 2))

    def side(self, k, c):
        return remote(self.own.at[k, self.at(c)], self.got[k].at[self.at(c)], self.gs.at[k, c], self.gr.at[k, c], self.sq.place(k))

    def add(self, k, c, other):
        step = 64 if self.own.shape[2] > 512 else 256

        def body(i, _):
            at = pl.ds(pl.multiple_of(c * self.rows + i * step, 8), step)
            value = other[k, at, :] if len(other.shape) == 3 else other[at, :]
            self.own[k, at, :] = (self.own[k, at, :].astype(F32) + value.astype(F32)).astype(BF)
            return 0

        lax.fori_loop(0, self.rows // step, body, 0)

    def run(self, product, between=lambda n: None):
        order = (3, 1, 2, 0)

        def settle(k):
            for c in range(CHUNKS):
                self.near(k, c).wait_recv()
                if k:
                    self.add(k, c, self.mate)
                if k == 3:
                    self.far(c).start()
                elif k and c % 2 == k - 1:
                    self.side(k, c).start()

        for n, k in enumerate(order):
            product(self.sq.index(k, True), self.to_mate.at[k])
            for c in range(CHUNKS):
                self.near(k, c).start()
            product(self.sq.index(k), self.own.at[k])
            settle(k)
            between(n)

    def pass_on(self):
        for c in range(CHUNKS):
            k = 2 - c % 2
            self.far(c).wait_recv()
            self.add(k, c, self.landed)
            self.side(k, c).start()

    def receive(self, c):
        self.side(1, c).wait_recv()
        self.side(2, c).wait_recv()

    def total(self, at):
        value = self.own[0, at, :].astype(F32) + self.mate[0, at, :].astype(F32)
        return value + self.got[1][at, :].astype(F32) + self.got[2][at, :].astype(F32)

    def drain(self):
        for c in range(CHUNKS):
            for k in range(4):
                self.near(k, c).wait_send()
            self.far(c).wait_send()
            self.side(1, c).wait_send()
            self.side(2, c).wait_send()


def reduce_parts(rows_, cols):
    return [pltpu.VMEM((4, rows_, cols), BF)] * 3 + [pltpu.VMEM((rows_, cols), BF)] * 3


def reduce_sems():
    return [DMA((4, CHUNKS))] * 2 + [DMA((CHUNKS,))] * 2 + [DMA((3, CHUNKS))] * 2


PIECES = 4


class LineGather(WeightGather):
    def __init__(self, cfg, co, w, full, own, send, recv, rs, rr, ls, lr):
        super().__init__(cfg, co, w, full, own, send, recv, None, None, None, None)
        self.rs, self.rr, self.ls, self.lr = rs, rr, ls, lr
        self.a = co[0]

    def unit(self, a, p):
        count = self.cfg.F // PIECES
        return self.full.at[pl.ds(a * self.cfg.F + p * count, count)]

    def move(self, way, i, p):
        cfg, (a, zl, b, f) = self.cfg, self.co
        block = self.unit((a - way * i + cfg.A) % cfg.A, p)
        send, recv = (self.rs, self.rr) if way == 1 else (self.ls, self.lr)
        return remote(block, block, send.at[i, p], recv.at[i, p], device(cfg, (a + way + cfg.A) % cfg.A, zl, b, f))

    def landing(self, way, i, p):
        cfg, (a, zl, b, f) = self.cfg, self.co
        block = self.unit((a - way * (i + 1) + cfg.A) % cfg.A, p)
        send, recv = (self.rs, self.rr) if way == 1 else (self.ls, self.lr)
        return remote(block, block, send.at[i, p], recv.at[i, p], device(cfg, (a + way + cfg.A) % cfg.A, zl, b, f))

    def behind(self, way):
        return self.a if way == 1 else self.cfg.A - 1 - self.a

    def start_line(self):
        for p in range(PIECES):
            for way in (1, -1):
                pl.when(self.behind(-way) > 0)(lambda way=way, p=p: self.move(way, 0, p).start())

    def forward(self, i, p):
        for way in (1, -1):

            @pl.when(self.behind(way) >= i)
            def _():
                self.landing(way, i - 1, p).wait_recv()
                if i < self.cfg.A - 1:
                    pl.when(self.behind(-way) > 0)(lambda: self.move(way, i, p).start())

    def finish(self):
        for i in range(self.cfg.A - 1):
            for p in range(PIECES):
                for way in (1, -1):
                    there = (self.behind(way) >= i) & (self.behind(-way) > 0)
                    pl.when(there)(lambda way=way, i=i, p=p: self.move(way, i, p).wait_send())


def line_sems(cfg):
    return [DMA((3,)), DMA((cfg.F, 3)), DMA((cfg.F, 3))] + [DMA((cfg.A - 1, PIECES))] * 4


class LineSum:
    def __init__(self, cfg, co, gw, land, rs, rr, ls, lr):
        self.cfg, self.co, self.gw, self.land = cfg, co, gw, land
        self.rs, self.rr, self.ls, self.lr = rs, rr, ls, lr
        self.a = co[0]
        self.count = cfg.F // PIECES

    def behind(self, way):
        return self.a if way == 1 else self.cfg.A - 1 - self.a

    def slots(self, t, p):
        return pl.ds(t * self.cfg.F + p * self.count, self.count)

    def move(self, way, t, p):
        cfg, (a, zl, b, f) = self.cfg, self.co
        send, recv, at = (self.rs, self.rr, t + 1) if way == 1 else (self.ls, self.lr, t)
        to = device(cfg, (a + way + cfg.A) % cfg.A, zl, b, f)
        return remote(self.gw.at[self.slots(t, p)], self.land.at[at, pl.ds(p * self.count, self.count)], send.at[t, p], recv.at[t, p], to)

    def landed(self, way, t, p):
        return self.land[t + 1 if way == 1 else t, pl.ds(p * self.count, self.count)]

    def each(self, todo, distances):
        for d in distances:
            for way in (1, -1):
                pl.when(self.behind(-way) >= d)(lambda d=d, way=way: todo(way, self.a + way * d))

    def target(self, n):
        way = 1 - 2 * (n % 2)
        t = self.a + way * (self.cfg.A - 1 - n // 2)
        return t, way, (t >= 0) & (t < self.cfg.A)

    def fetch(self, src, dst, sem, n):
        t, _, _ = self.target(n)
        width = self.cfg.F * self.cfg.R
        at = pl.ds(pl.multiple_of((t + self.cfg.A) % self.cfg.A * width, 128), width)
        return pltpu.make_async_copy(src.at[:, :, at], dst.at[:, :, at], sem.at[n])

    def fetch_all(self, src, dst, sem):
        for n in range(2 * self.cfg.A - 1):
            pl.when(self.target(n)[2])(lambda n=n: self.fetch(src, dst, sem, n).start())

    def produce(self, block, begin, end, ready):
        cfg = self.cfg

        def one(n, _):
            t, way, there = self.target(n)

            @pl.when(there)
            def _():
                ready(n)

                def body(h, _):
                    block(t * cfg.F + h * cfg.FS)
                    return 0

                lax.fori_loop(0, cfg.ZL, body, 0)
                for w in (1, -1):

                    @pl.when((self.behind(w) == 0) & (way == w) & (t != self.a))
                    def _():
                        for p in range(PIECES):
                            self.move(w, t, p).start()

            return 0

        lax.fori_loop(begin, end, one, 0)

    def pump(self, distance, begin=0, end=PIECES):
        def body(p, _):
            for way in (1, -1):

                @pl.when((self.behind(-way) >= distance) & (self.behind(way) > 0))
                def _():
                    t = self.a + way * distance
                    self.move(way, t, p).wait_recv()
                    at = self.slots(t, p)
                    self.gw[at] = (self.gw[at].astype(F32) + self.landed(way, t, p).astype(F32)).astype(BF)
                    self.move(way, t, p).start()

            return 0

        lax.fori_loop(begin, end, body, 0)

    def settle(self, out, then=lambda p: None):
        def body(p, _):
            mine = self.gw[self.slots(self.a, p)].astype(F32)
            to = pl.ds(p * self.count, self.count)
            for way in (1, -1):
                pl.when(self.behind(way) > 0)(lambda way=way: self.move(way, self.a, p).wait_recv())
            for low, high in ((0, 1), (1, 0), (1, 1)):

                @pl.when(((self.behind(1) > 0) == (low == 1)) & ((self.behind(-1) > 0) == (high == 1)))
                def _():
                    value = mine
                    if low:
                        value = value + self.landed(1, self.a, p).astype(F32)
                    if high:
                        value = value + self.landed(-1, self.a, p).astype(F32)
                    out[to] = value.astype(BF)

            then(p)
            return 0

        lax.fori_loop(0, PIECES, body, 0)

    def drain(self):
        def todo(way, t):
            for p in range(PIECES):
                self.move(way, t, p).wait_send()

        self.each(todo, range(1, self.cfg.A))


def line_parts(cfg):
    cols = 3 * cfg.FW
    return [pltpu.VMEM((cfg.N, cfg.R, cols), BF), pltpu.VMEM((cfg.A + 1, cfg.F, cfg.R, cols), BF)]


def line_sum_sems(cfg):
    return [DMA((cfg.A, PIECES))] * 4


def weight_rows(cfg, w, first, count):
    return w[pl.ds(first, count)].reshape(count * cfg.R, 3 * cfg.FW)


def grad_block(cfg, low, grads, gw):
    def block(first):
        slots = pl.ds(first, cfg.FS)
        columns = pl.ds(pl.multiple_of(first * cfg.R, 128), cfg.FS * cfg.R)
        data = low[:, :, columns].reshape(cfg.M, cfg.FS * cfg.R)
        out = lax.dot_general(data, grads[...], (((0,), (0,)), ((), ())), preferred_element_type=F32)
        gw[slots] = out.astype(BF).reshape(cfg.FS, cfg.R, 3 * cfg.FW)

    return block


def multiply_chunk(cfg, low, w, proj, c):
    n = cfg.T // CHUNKS
    data = low[:, pl.ds(pl.multiple_of(c * n, 16), n), :].reshape(cfg.S * n, cfg.D)
    out = jnp.dot(data, w[...].reshape(cfg.D, 3 * cfg.FW), preferred_element_type=F32)
    for i in range(cfg.S):
        to = pl.ds(pl.multiple_of(i * cfg.TP + c * n, 8), n)
        for l in range(3 * cfg.L):
            proj[l, to, :] = out[i * n : (i + 1) * n, 128 * l : 128 * l + 128]


def multiply_units(cfg, low, w, proj, c, first, count, more):
    n, k = cfg.T // CHUNKS, cfg.F * cfg.R
    depth = pl.ds(pl.multiple_of(first * k, 128), count * k)
    data = low[:, pl.ds(pl.multiple_of(c * n, 16), n), depth].reshape(cfg.S * n, count * k)
    out = jnp.dot(data, weight_rows(cfg, w, first * cfg.F, count * cfg.F), preferred_element_type=F32)
    for i in range(cfg.S):
        to = pl.ds(pl.multiple_of(i * cfg.TP + c * n, 8), n)
        for l in range(3 * cfg.L):
            value = out[i * n : (i + 1) * n, 128 * l : 128 * l + 128]
            proj[l, to, :] = proj[l, to, :] + value if more else value


def scan_chunk(cfg, proj, inp, vec, base, lens, hid, states, tf_ref, tr_ref, carry, c):
    half_pf, half_pr = 0.5 * wide(cfg, vec, base), 0.5 * wide(cfg, vec, base + 1)
    half_bf, half_br = 0.5 * wide(cfg, vec, base + 2), 0.5 * wide(cfg, vec, base + 3)
    live = jnp.broadcast_to(lens[:, 0:1], (cfg.S, cfg.FW))
    n = cfg.T // CHUNKS

    def step(i, state):
        t = c * n + i
        u, p, q = (rows(cfg, proj, t, j * cfg.L, cfg.L) for j in range(3))
        here = rows(cfg, inp, t, 0, cfg.L)
        p, q, hu, hc = 0.5 * p + half_bf, 0.5 * q + half_br, 0.5 * u, 0.5 * state
        tf = jnp.tanh(p + half_pf * state)
        tr = jnp.tanh(q + half_pr * state)
        new = (hc + hu) + tf * (hc - hu)
        out = jnp.where(t < live, 0.5 * (here + new) + 0.5 * tr * (new - here), 0.0)
        put(cfg, hid, t, out)
        put(cfg, states, t, new)
        put(cfg, tf_ref, t, tf)
        put(cfg, tr_ref, t, tr)
        return new

    carry[...] = lax.fori_loop(0, n, step, carry[...], unroll=8)


def forward_kernel(cfg, *refs):
    refs = list(refs)

    def take(n):
        out = refs[:n]
        del refs[:n]
        return out

    x, cot, w1, w2, small = take(5)
    low1_out, low2_out, f1_out, f2_out, saved, vec, mine, lens, zo_out, inv_out, hid_out, p_out, dir_out, sums = take(14)
    xg, hg, low, f1, f2, sg, cg, proj, inp, states, tf, tr, hid, direct, hid_low, p_low, z_own, inv, carry = take(19)
    own_sem, small_send, small_recv, cs, cr, flush = take(6)
    xsems, hsems, w1sems, w2sems = take(6), take(6), take(7), take(7)
    co = coords(cfg)
    a, zl, b, f = co
    sq = Square(cfg, co)
    s, me = sq.s, flat(cfg, *co)
    rows_c = cfg.T // CHUNKS
    cols = lambda i: pl.ds(pl.multiple_of(i * cfg.FW, 128), cfg.FW)
    greet_all(cfg, me)
    one = LineGather(cfg, co, w1, f1, *w1sems)
    two = LineGather(cfg, co, w2, f2, *w2sems)
    one.start()

    def each(k, _):
        m = (me + k) % cfg.N
        remote(small, sg.at[me], small_send, small_recv, (m // cfg.FS, m % cfg.FS)).start()
        return 0

    lax.fori_loop(1, cfg.N, each, 0)
    part = lambda c: pl.ds(pl.multiple_of(c * rows_c, 16), rows_c)
    xgather = SquareGather(sq, lambda i, c: xg.at[i, part(c)], lambda c: 1 - c % 2, xsems, lambda c: x.at[part(c)])
    hgather = SquareGather(sq, lambda i, c: hg.at[:, part(c), cols(i)], lambda c: 1 - c % 2, hsems)
    two.start()
    for c in range(CHUNKS):
        xgather.push(c)
    exchange = Exchange(cfg, co, lambda i: cot.at[:, cols(i)], lambda i: cg.at[i], cs, cr)
    local = [
        pltpu.make_async_copy(x, xg.at[s], own_sem.at[0]),
        pltpu.make_async_copy(cot.at[:, cols(s)], cg.at[s], own_sem.at[1]),
        pltpu.make_async_copy(small, sg.at[me], own_sem.at[2]),
    ]
    for copy in local:
        copy.start()

    everyone = sg.at[pl.ds(0, cfg.N - 1)]
    def norm_one(c):
        def body(i, _):
            two_of = pl.ds(2 * i, 2)
            z, _ = normalize(xg[two_of, part(c), :].reshape(2 * rows_c, cfg.D).astype(F32))
            low[two_of, part(c), :] = (z * vec[4:5, :] + vec[5:6, :]).astype(BF).reshape(2, rows_c, cfg.D)
            for h in range(2):
                own = xg[2 * i + h, part(c), cols(s)].astype(F32)
                to = pl.ds(pl.multiple_of((2 * i + h) * cfg.TP + c * rows_c, 8), rows_c)
                for l in range(cfg.L):
                    inp[l, to, :] = own[:, 128 * l : 128 * l + 128]
            return 0

        lax.fori_loop(0, cfg.S // 2, body, 0)

    def norm_two(c):
        def body(i, _):
            two_of = pl.ds(2 * i, 2)
            data = hg[two_of, part(c), :].reshape(2 * rows_c, cfg.D).astype(F32)
            mean = jnp.mean(data, axis=-1, keepdims=True)
            center = data - mean
            inverse = lax.rsqrt(jnp.mean(center * center, axis=-1, keepdims=True) + EPSILON)
            low[two_of, part(c), :] = (center * inverse * vec[10:11, :] + vec[11:12, :]).astype(BF).reshape(2, rows_c, cfg.D)
            own = (hg[two_of, part(c), cols(s)].reshape(2 * rows_c, cfg.FW).astype(F32) - mean) * inverse
            for h in range(2):
                at = pl.ds(pl.multiple_of((2 * i + h) * cfg.T + c * rows_c, 8), rows_c)
                inv[at, :] = jnp.broadcast_to(inverse[h * rows_c : (h + 1) * rows_c], (rows_c, 128))
                z_own[at, :] = own[h * rows_c : (h + 1) * rows_c]
            return 0

        lax.fori_loop(0, cfg.S // 2, body, 0)

    def hidden_chunk(c):
        for i in range(cfg.S):
            to = pl.ds(pl.multiple_of(i * cfg.TP + c * rows_c, 8), rows_c)
            for l in range(cfg.L):
                hg[i, part(c), pl.ds(pl.multiple_of(s * cfg.FW + 128 * l, 128), 128)] = hid[l, to, :].astype(BF)

    keep_low1 = pltpu.make_async_copy(low, low1_out, flush.at[0])
    keep_f1 = pltpu.make_async_copy(f1, f1_out, flush.at[1])
    keeps = [
        pltpu.make_async_copy(ref if n != 1 else proj.at[pl.ds(0, cfg.L)], saved.at[pl.ds(n * cfg.L, cfg.L)], flush.at[2 + n])
        for n, ref in enumerate((inp, None, states, tf, tr))
    ]
    carry[...] = jnp.zeros_like(carry)
    one.middle()
    one.start_line()
    pltpu.make_async_copy(everyone, everyone, small_recv).wait()
    for copy in local:
        copy.wait()
    for i in range(cfg.N // cfg.PER):
        total = sg[i * cfg.PER].astype(F32)
        for p in range(1, cfg.PER):
            total = total + sg[i * cfg.PER + p].astype(F32)
        vec[:, 128 * i : 128 * i + 128] = total
    mine[...] = vec[:, cols(s)]
    for i in range(cfg.S):
        n = flat(cfg, a, i // cfg.FS, b, i % cfg.FS)
        length = jnp.max(sg[n].astype(F32)[12:13, :], axis=-1, keepdims=True)
        lens[i : i + 1, :] = jnp.broadcast_to(length, (1, 128)).astype(jnp.int32)

    xgather.arrive(0)
    one.forward(1, 0)
    one.forward(1, 1)
    xgather.arrive(1)
    one.forward(1, 2)
    one.forward(1, 3)
    xgather.arrive(2)
    one.forward(2, 0)
    xgather.arrive(3)
    one.forward(2, 1)
    one.forward(2, 2)
    one.forward(2, 3)
    two.middle()
    two.start_line()
    exchange.start()

    def layer_one(k, _):
        @pl.when(k < CHUNKS)
        def _():
            xgather.complete(k)
            norm_one(k)

            @pl.when(k == 3)
            def _():
                keep_low1.start()
                for p in range(PIECES):
                    one.forward(3, p)
                keep_f1.start()

        @pl.when(k >= CHUNKS - 1)
        def _():
            c = k - (CHUNKS - 1)
            multiply_chunk(cfg, low, f1, proj, c)
            scan_chunk(cfg, proj, inp, mine, 0, lens, hid, states, tf, tr, carry, c)
            hidden_chunk(c)
            hgather.push(c)
            pl.when(c > 0)(lambda: hgather.arrive(c - 1))
            two.forward(1, c)

        return 0

    lax.fori_loop(0, 2 * CHUNKS - 1, layer_one, 0)
    for copy in keeps:
        copy.start()
    carry[...] = jnp.zeros_like(carry)
    hgather.arrive(CHUNKS - 1)
    two.forward(2, 0)
    two.forward(2, 1)
    keep_low1.wait()

    for copy in keeps:
        copy.wait()
    end_unit = a // (cfg.A - 1)
    at_end = (a == 0) | (a == cfg.A - 1)

    def layer_two(k, _):
        hgather.complete(k)
        norm_two(k)

        @pl.when(k == 0)
        def _():
            two.forward(2, 2)
            two.forward(2, 3)

        @pl.when(at_end)
        def _():
            multiply_units(cfg, low, f2, proj, k, end_unit, cfg.A - 1, False)

        @pl.when(jnp.logical_not(at_end))
        def _():
            multiply_units(cfg, low, f2, proj, k, 0, cfg.A, False)

        return 0

    lax.fori_loop(0, CHUNKS, layer_two, 0)
    for p in range(PIECES):
        two.forward(3, p)

    def layer_two_scan(k, _):
        @pl.when(at_end)
        def _():
            multiply_units(cfg, low, f2, proj, k, (cfg.A - 1) * (1 - end_unit), 1, True)

        scan_chunk(cfg, proj, hid, mine, 6, lens, inp, states, tf, tr, carry, k)
        return 0

    lax.fori_loop(0, CHUNKS, layer_two_scan, 0)
    outs = [
        pltpu.make_async_copy(low, low2_out, flush.at[0]),
        pltpu.make_async_copy(z_own, zo_out, flush.at[7]),
        pltpu.make_async_copy(inv, inv_out, flush.at[8]),
        pltpu.make_async_copy(f2, f2_out, flush.at[9]),
    ]
    for copy in outs:
        copy.start()
    hgather.drain()
    one.finish()
    two.finish()
    narrow(cfg, inp, hid_low, cfg.L)
    outs.append(pltpu.make_async_copy(hid_low, hid_out, flush.at[10]))
    outs[-1].start()
    exchange.finish()
    for i in range(cfg.S):
        g = cg[i].astype(F32)
        for l in range(cfg.L):
            inp[l, i * cfg.TP : i * cfg.TP + cfg.T, :] = g[:, 128 * l : 128 * l + 128]
    scan_backward(cfg, proj, hid, mine, 6, lens, states, tf, tr, inp, proj, direct, sums)
    narrow(cfg, proj, p_low, 3 * cfg.L)
    outs.append(pltpu.make_async_copy(p_low, p_out, flush.at[11]))
    outs.append(pltpu.make_async_copy(direct, dir_out, flush.at[12]))
    for copy in outs[-2:]:
        copy.start()
    xgather.drain()
    pltpu.make_async_copy(everyone, everyone, small_send).wait()
    keep_f1.wait()
    for copy in outs:
        copy.wait()


def forward(cfg, x, cot, w1, w2, small):
    low = jax.ShapeDtypeStruct((cfg.S, cfg.T, cfg.D), BF)
    full = jax.ShapeDtypeStruct((cfg.N, cfg.R, 3 * cfg.FW), BF)
    state = keep(cfg, cfg.L)
    vm = lambda t: pltpu.VMEM(t.shape, t.dtype)
    shape = jax.ShapeDtypeStruct
    outs = [
        (low, HBM), (low, HBM), (full, HBM), (full, HBM), (keep(cfg, 5 * cfg.L), HBM),
        (shape((16, cfg.D), F32), VM), (shape((16, cfg.FW), F32), VM), (shape((cfg.S, 128), jnp.int32), VM),
        (shape((cfg.M, cfg.FW), F32), HBM), (shape((cfg.M, 128), F32), HBM), (shape((cfg.M, cfg.FW), BF), HBM),
        (shape((cfg.M, 3 * cfg.FW), BF), HBM), (state, HBM), (shape((8, cfg.FW), F32), VM),
    ]
    return pl.pallas_call(
        functools.partial(forward_kernel, cfg),
        name="forward",
        out_shape=[o for o, _ in outs],
        in_specs=[HBM] * 5,
        out_specs=[p for _, p in outs],
        scratch_shapes=[
            vm(low), vm(low), vm(low), vm(full), vm(full), pltpu.VMEM((cfg.N, 16, 128), BF), pltpu.VMEM((cfg.S, cfg.T, cfg.FW), BF),
            vm(keep(cfg, 3 * cfg.L)),
        ]
        + [vm(state)] * 6
        + [pltpu.VMEM((cfg.M, cfg.FW), BF), pltpu.VMEM((cfg.M, 3 * cfg.FW), BF), pltpu.VMEM((cfg.M, cfg.FW), F32), pltpu.VMEM((cfg.M, 128), F32), pltpu.VMEM((cfg.S, cfg.FW), F32)]
        + [DMA((4,)), DMA(()), DMA(()), DMA((cfg.F,)), DMA((cfg.F,)), DMA((13,))]
        + gather_sems() * 2
        + line_sems(cfg) * 2,
        compiler_params=pltpu.CompilerParams(collective_id=5, has_side_effects=True, vmem_limit_bytes=VMEM_CAP),
    )(x, cot, w1, w2, small)


def inner_kernel(cfg, *refs):
    refs = list(refs)

    def take(n):
        out = refs[:n]
        del refs[:n]
        return out

    p_in, f2_in, low_in, zo_in, inv_in, dir_in, saved, hid_low, mine, lens = take(10)
    p_out, dlow_out, land, hid, norms, sums = take(6)
    p, w, low, z_own, inv, direct, inp, states, tf, tr, proj, grad, ng, stats, mean, group_sum = take(16)
    red_parts, t_parts = take(6), take(2)
    load, low_sem, ss, sr, hs, hr, s2, r2 = take(8)
    red_sems, t_sems = take(6), take(4)
    co = coords(cfg)
    a, zl, b, f = co
    sq = Square(cfg, co)
    s = sq.s
    cols = lambda i: pl.ds(pl.multiple_of(i * cfg.FW, 128), cfg.FW)
    loads = [pltpu.make_async_copy(src, dst, load.at[n]) for n, (src, dst) in enumerate((
        (p_in, p), (f2_in, w), (zo_in, z_own), (inv_in, inv), (dir_in, direct),
        (saved.at[pl.ds(0, cfg.L)], inp), (saved.at[pl.ds(cfg.L, cfg.L)], proj.at[pl.ds(0, cfg.L)]),
        (saved.at[pl.ds(2 * cfg.L, cfg.L)], states), (saved.at[pl.ds(3 * cfg.L, cfg.L)], tf), (saved.at[pl.ds(4 * cfg.L, cfg.L)], tr),
    ))]
    tsum = LineSum(cfg, co, *t_parts, *t_sems)
    loads[0].start()
    tsum.fetch_all(low_in, low, low_sem)
    loads[1].start()
    ready = lambda n: tsum.fetch(low_in, low, low_sem, n).wait()
    greet(group_targets(cfg, a, b, s) + t_targets(cfg, co))
    ex_h = Exchange(cfg, co, lambda i: hid_low.at[pl.ds(i * cfg.T, cfg.T)], lambda i: hid.at[:, cols(i)], hs, hr)
    ex_h.start(1, 5)
    own_hid = pltpu.make_async_copy(ex_h.src(s), ex_h.dst(s), load.at[11])
    own_hid.start()
    red = SquareReduce(sq, *red_parts, red_sems)
    loads[0].wait()

    def product(i, out):
        block = weight_rows(cfg, w, i * (cfg.FW // cfg.R), cfg.FW // cfg.R)

        def body(n, _):
            at = pl.ds(pl.multiple_of(n * 512, 8), 512)
            out[at, :] = lax.dot_general(p[at, :], block, (((1,), (1,)), ((), ())), preferred_element_type=F32).astype(BF)
            return 0

        lax.fori_loop(0, cfg.M // 512, body, 0)

    block_of = grad_block(cfg, low, p, t_parts[0])
    tsum.produce(block_of, 0, 4, ready)
    loads[1].wait()
    for copy in loads[2:]:
        copy.start()
    red.run(product, lambda n: tsum.pump(2, n, n + 1))
    red.pass_on()
    tsum.produce(block_of, 4, 7, ready)
    tsum.pump(1)
    for copy in loads[2:]:
        copy.wait()
    gain = mine[10:11, :]
    eye = (lax.broadcasted_iota(jnp.int32, (128, 128), 0) == lax.broadcasted_iota(jnp.int32, (128, 128), 1)).astype(F32)

    def first_pass(i, carry):
        s0, s1 = carry
        at = pl.ds(pl.multiple_of(i * 128, 8), 128)
        value = red.total(at)
        z = z_own[at, :]
        h = value * gain
        ng[at, :] = h
        for n, x in ((0, h), (1, h * z)):
            col = jnp.sum(x, axis=-1, keepdims=True)
            stats[s, n, pl.ds(i, 1), :] = jnp.sum(col * eye, axis=0, keepdims=True)
        return s0 + jnp.sum(value * z, axis=0, keepdims=True), s1 + jnp.sum(value, axis=0, keepdims=True)

    zero = jnp.zeros((1, cfg.FW), F32)
    carry = (zero, zero)
    per = cfg.M // 128 // CHUNKS
    for c in range(CHUNKS):
        red.receive(c)
        carry = lax.fori_loop(c * per, (c + 1) * per, first_pass, carry)
    norms[0:1, :] = carry[0]
    norms[1:2, :] = carry[1]
    exchange = Exchange(cfg, co, lambda i: stats.at[s], lambda i: stats.at[i], ss, sr)
    exchange.start()
    ex_h.start(5)
    exchange.finish()
    total = stats[0]
    for i in range(1, cfg.F):
        total = total + stats[i]
    mean[...] = total * (1.0 / cfg.D)

    def second_pass(i, _):
        at = pl.ds(pl.multiple_of(i * 128, 8), 128)
        m0 = jnp.sum(mean[0, pl.ds(i, 1), :] * eye, axis=-1, keepdims=True)
        m1 = jnp.sum(mean[1, pl.ds(i, 1), :] * eye, axis=-1, keepdims=True)
        value = (ng[at, :] - m0 - z_own[at, :] * m1) * inv[at, 0:1]
        each = cfg.T // 128
        to = pl.ds(pl.multiple_of((i // each) * cfg.TP + (i % each) * 128, 8), 128)
        for l in range(cfg.L):
            grad[l, to, :] = value[:, 128 * l : 128 * l + 128] + direct[l, to, :]
        return 0

    lax.fori_loop(0, cfg.M // 128, second_pass, 0)
    ex_2 = Exchange(cfg, co, lambda i: group_sum.at[i], lambda i: land.at[i], s2, r2)
    tsum.settle(group_sum, ex_2.piece_sender(PIECES))
    own_sum = pltpu.make_async_copy(group_sum.at[s], land.at[s], load.at[2])
    own_sum.start()
    scan_backward(cfg, proj, inp, mine, 0, lens, states, tf, tr, grad, proj, direct, sums)
    narrow(cfg, proj, p, 3 * cfg.L)
    outs = [pltpu.make_async_copy(p, p_out, load.at[0])]
    outs[0].start()
    red.drain()
    dlow = red_parts[0].at[0]
    narrow(cfg, direct, dlow, cfg.L)
    outs.append(pltpu.make_async_copy(dlow, dlow_out, load.at[1]))
    outs[1].start()
    ex_2.finish()
    own_sum.wait()
    ex_h.finish()
    own_hid.wait()
    tsum.drain()
    for copy in outs:
        copy.wait()


def inner(cfg, p, f2, low, zo, inv, direct, saved, hid_low, mine, lens):
    shape = jax.ShapeDtypeStruct
    state = keep(cfg, cfg.L)
    vm = lambda t: pltpu.VMEM(t.shape, t.dtype)
    part = shape((cfg.F, cfg.R, 3 * cfg.FW), BF)
    return pl.pallas_call(
        functools.partial(inner_kernel, cfg),
        name="inner",
        out_shape=[shape((cfg.M, 3 * cfg.FW), BF), shape((cfg.M, cfg.FW), BF), part, shape((cfg.T, cfg.D), BF), shape((8, cfg.FW), F32), shape((8, cfg.FW), F32)],
        in_specs=[HBM] * 8 + [VM] * 2,
        out_specs=[HBM] * 4 + [VM] * 2,
        scratch_shapes=[vm(p), vm(f2), vm(low), vm(zo), vm(inv)]
        + [vm(state)] * 5
        + [vm(keep(cfg, 3 * cfg.L)), vm(state), pltpu.VMEM((cfg.M, cfg.FW), F32)]
        + [pltpu.VMEM((cfg.F, 2, cfg.M // 128, 128), F32), pltpu.VMEM((2, cfg.M // 128, 128), F32), vm(part)]
        + reduce_parts(cfg.M, cfg.FW)
        + line_parts(cfg)
        + [DMA((12,)), DMA((2 * cfg.A - 1,))] + [DMA((cfg.F,))] * 6
        + reduce_sems()
        + line_sum_sems(cfg),
        compiler_params=pltpu.CompilerParams(collective_id=6, has_side_effects=True, vmem_limit_bytes=VMEM_CAP),
    )(p, f2, low, zo, inv, direct, saved, hid_low, mine, lens)


def final_kernel(cfg, *refs):
    refs = list(refs)

    def take(n):
        out = refs[:n]
        del refs[:n]
        return out

    p_in, f1_in, low_in, dlow, sum2, x, vec, sums1, sums2, norm2 = take(10)
    grad, o1, o2, total = take(4)
    p, w, low, dgot, land1, land2, group_sum, small, sg = take(9)
    red_parts, t_parts = take(6), take(2)
    load, low_sem, small_send, small_recv, ds, dr, s1, r1 = take(8)
    red_sems, t_sems = take(6), take(4)
    co = coords(cfg)
    a, zl, b, f = co
    sq = Square(cfg, co)
    s, me = sq.s, flat(cfg, *co)
    cols = lambda i: pl.ds(pl.multiple_of(i * cfg.FW, 128), cfg.FW)
    loads = [pltpu.make_async_copy(src, dst, load.at[n]) for n, (src, dst) in enumerate(((p_in, p), (f1_in, w)))]
    tsum = LineSum(cfg, co, *t_parts, *t_sems)
    loads[0].start()
    tsum.fetch_all(low_in, low, low_sem)
    loads[1].start()
    ready = lambda n: tsum.fetch(low_in, low, low_sem, n).wait()
    greet_all(cfg, me)
    red = SquareReduce(sq, *red_parts, red_sems)
    ex_d = Exchange(cfg, co, lambda i: dlow.at[pl.ds(i * cfg.T, cfg.T)], lambda i: dgot.at[:, cols(i)], ds, dr)
    ex_d.start()
    copies = [pltpu.make_async_copy(ex_d.src(s), ex_d.dst(s), load.at[3]), pltpu.make_async_copy(sum2, land2, load.at[4])]
    for copy in copies:
        copy.start()
    loads[0].wait()

    def product(i, out):
        data = p[pl.ds(pl.multiple_of(i * cfg.T, 8), cfg.T), :]

        def body(n, _):
            wide_ = cfg.D // 4
            block_ = weight_rows(cfg, w, n * (wide_ // cfg.R), wide_ // cfg.R)
            value = lax.dot_general(data, block_, (((1,), (1,)), ((), ())), preferred_element_type=F32)
            out[:, pl.ds(pl.multiple_of(n * wide_, 128), wide_)] = value.astype(BF)
            return 0

        lax.fori_loop(0, 4, body, 0)

    block_of = grad_block(cfg, low, p, t_parts[0])
    tsum.produce(block_of, 0, 4, ready)
    loads[1].wait()
    red.run(product, lambda n: tsum.pump(2, n, n + 1))
    tsum.produce(block_of, 4, 7, ready)
    ex_1 = Exchange(cfg, co, lambda i: group_sum.at[i], lambda i: land1.at[i], s1, r1)
    red.pass_on()
    tsum.pump(1)
    ex_d.finish()
    for copy in copies:
        copy.wait()
    step = 64

    def body(i, carry):
        s0, s1_ = carry
        at = pl.ds(pl.multiple_of(i * step, 8), step)
        value = red.total(at)
        z, inverse = normalize(x[at, :].astype(F32))
        h = value * vec[4:5, :]
        m0 = jnp.mean(h, axis=-1, keepdims=True)
        m1 = jnp.mean(h * z, axis=-1, keepdims=True)
        grad[at, :] = (h - m0 - z * m1) * inverse + dgot[at, :].astype(F32)
        return s0 + jnp.sum(value * z, axis=0, keepdims=True), s1_ + jnp.sum(value, axis=0, keepdims=True)

    zero = jnp.zeros((1, cfg.D), F32)
    carry = (zero, zero)
    per = cfg.T // step // CHUNKS
    for c in range(CHUNKS):
        red.receive(c)
        carry = lax.fori_loop(c * per, (c + 1) * per, body, carry)
    many = cfg.N // cfg.PER
    small[...] = jnp.zeros_like(small)
    for i in range(cfg.L):
        lanes = slice(128 * i, 128 * i + 128)
        small[s * cfg.L + i, 0:4, :] = sums1[0:4, lanes]
        small[s * cfg.L + i, 6:10, :] = sums2[0:4, lanes]
        small[s * cfg.L + i, 10:12, :] = norm2[0:2, lanes]
    for i in range(many):
        small[i, 4:5, :] = carry[0][:, 128 * i : 128 * i + 128]
        small[i, 5:6, :] = carry[1][:, 128 * i : 128 * i + 128]

    def each(k, _):
        m = (me + k) % cfg.N
        remote(small.at[m // cfg.PER], sg.at[me], small_send, small_recv, (m // cfg.FS, m % cfg.FS)).start()
        return 0

    lax.fori_loop(1, cfg.N, each, 0)
    sg[me] = small[me // cfg.PER]
    tsum.settle(group_sum, ex_1.piece_sender(PIECES))
    land1[s] = group_sum[s]

    def spread(land, out):
        for i in range(cfg.F):
            for c in range(3):
                at = c * cfg.D + i * cfg.FW
                out[:, at : at + cfg.FW] = land[i, :, c * cfg.FW : (c + 1) * cfg.FW].astype(F32)

    spread(land2, o2)
    everyone = sg.at[pl.ds(0, cfg.N - 1)]
    pltpu.make_async_copy(everyone, everyone, small_recv).wait()
    value = sg[0]
    for i in range(1, cfg.N):
        value = value + sg[i]
    total[...] = value
    ex_1.finish()
    spread(land1, o1)
    red.drain()
    tsum.drain()
    pltpu.make_async_copy(everyone, everyone, small_send).wait()


def final(cfg, p, f1, low, dlow, sum2, x, vec, sums1, sums2, norm2):
    shape = jax.ShapeDtypeStruct
    vm = lambda t: pltpu.VMEM(t.shape, t.dtype)
    part = pltpu.VMEM((cfg.F, cfg.R, 3 * cfg.FW), BF)
    out = shape((cfg.R, 3 * cfg.D), F32)
    return pl.pallas_call(
        functools.partial(final_kernel, cfg),
        name="final",
        out_shape=[shape((cfg.T, cfg.D), F32), out, out, shape((16, 128), F32)],
        in_specs=[HBM] * 5 + [VM] * 5,
        out_specs=[VM] * 4,
        scratch_shapes=[vm(p), vm(f1), vm(low), pltpu.VMEM((cfg.T, cfg.D), BF), part, part, part]
        + [pltpu.VMEM((cfg.N // cfg.PER, 16, 128), F32), pltpu.VMEM((cfg.N, 16, 128), F32)]
        + reduce_parts(cfg.T, cfg.D)
        + line_parts(cfg)
        + [DMA((5,)), DMA((2 * cfg.A - 1,)), DMA(()), DMA(())]
        + [DMA((cfg.F,))] * 4
        + reduce_sems()
        + line_sum_sems(cfg),
        compiler_params=pltpu.CompilerParams(collective_id=7, has_side_effects=True, vmem_limit_bytes=VMEM_CAP),
    )(p, f1, low, dlow, sum2, x, vec, sums1, sums2, norm2)


def shards_square(cfg, inputs, cotangent, w1, w2, packed, me):
    low1, low2, full1, full2, saved, vec, mine, lens, z_own, inv, hid2, p2, direct2, sums2 = forward(cfg, inputs[0], cotangent[0], w1, w2, packed)
    p1, direct1, part2, hidden, norm2, sums1 = inner(cfg, p2, full2, low2, z_own, inv, direct2, saved, hid2, mine, lens)
    grad, gw1, gw2, total = final(cfg, p1, full1, low1, direct1, part2, inputs[0], vec, sums1, sums2, norm2)
    total = lax.dynamic_slice(total, (0, (me % cfg.PER) * cfg.R), (16, cfg.R))
    out = [hidden[None], grad[None], gw1] + [total[i] for i in range(6)] + [gw2] + [total[i] for i in range(6, 12)]
    return tuple(out)


def shards(mesh, inputs, lengths, w1, pf1, pr1, bf1, br1, ng1, nb1, w2, pf2, pr2, bf2, br2, ng2, nb2, cotangent):
    _, steps, width = inputs.shape
    cfg = make_cfg(mesh, steps, width)
    a, zl, b, f = coords(cfg)
    j, me = zl * cfg.FS + f, flat(cfg, a, zl, b, f)
    vectors = [pf1, pr1, bf1, br1, ng1, nb1, pf2, pr2, bf2, br2, ng2, nb2, jnp.broadcast_to(lengths.astype(BF), (cfg.R,))]
    packed = jnp.tile(jnp.concatenate([jnp.stack(vectors), jnp.zeros((3, cfg.R), BF)]), (1, cfg.PER))
    lane = lax.broadcasted_iota(jnp.int32, (16, 128), 1)
    packed = jnp.where(lane // cfg.R == me % cfg.PER, packed, jnp.zeros_like(packed))

    square = cfg.ZL == 2 and cfg.FS == 4 and cfg.A == 4 and cfg.X == 1 and cfg.R % 16 == 0 and cfg.FW % 128 == 0
    if square:
        return shards_square(cfg, inputs, cotangent, w1, w2, packed, me)
    xg, cg, full1, full2, smalls = start(cfg, inputs[0], cotangent[0], w1, w2, packed)
    full1, full2 = full1.reshape(cfg.D, 3 * cfg.FW), full2.reshape(cfg.D, 3 * cfg.FW)
    vec = jnp.sum(smalls.astype(F32).reshape(cfg.N // cfg.PER, cfg.PER, 16, 128), axis=1)
    vec = jnp.transpose(vec, (1, 0, 2)).reshape(16, cfg.D)
    mine = lax.dynamic_slice(vec, (0, j * cfg.FW), (16, cfg.FW))
    lens = vec[12].reshape(cfg.A, cfg.ZL, cfg.X, cfg.FS, cfg.R)[..., 0]
    lens = lax.dynamic_index_in_dim(lax.dynamic_index_in_dim(lens, a, 0, False), b, 1, False).reshape(cfg.S)
    lens = jnp.broadcast_to(lens.astype(jnp.int32)[:, None], (cfg.S, 128))

    low1, hid1, hid1_low, inp, cand, states, tf, tr = first(cfg, xg, full1, vec, mine, lens)
    hg = gather_hidden(cfg, hid1_low).reshape(cfg.S, cfg.T, cfg.D)
    low2, hid2_low, grads2, part2, z_own, inv, direct2, sums2 = second(cfg, hg, full2, vec, mine, lens, hid1, cg)
    grad1, norm2 = middle(cfg, part2, z_own, inv, direct2, mine)
    gw2 = wgrad(cfg, low2, grads2)
    grads1, part1, direct1, sums1 = third(cfg, full1, mine, lens, inp, cand, states, tf, tr, grad1)
    gw1 = wgrad(cfg, low1, grads1)
    input_grad, hidden, got1, got2, norm1 = last(cfg, part1, direct1, hid2_low, gw1, gw2, inputs[0], vec)
    s1, s2 = own_sum(cfg, gw1, got1, a, b), own_sum(cfg, gw2, got2, a, b)

    block = jnp.concatenate([sums1[:4], jnp.zeros((2, cfg.FW), F32), sums2[:4], norm2[:2], jnp.zeros((4, cfg.FW), F32)])
    small = lax.dynamic_update_slice(jnp.zeros((16, cfg.D), F32), block, (0, j * cfg.FW))
    small = lax.dynamic_update_slice(small, norm1[:2], (4, 0))
    small = jnp.transpose(small.reshape(16, cfg.N // cfg.PER, 128), (1, 0, 2))
    gw1, gw2, smalls = end(cfg, s1, s2, small)
    total = jnp.sum(smalls, axis=0)
    total = lax.dynamic_slice(total, (0, (me % cfg.PER) * cfg.R), (16, cfg.R))
    out = [hidden[None], input_grad[None], gw1.astype(F32)] + [total[i] for i in range(6)] + [gw2.astype(F32)] + [total[i] for i in range(6, 12)]
    return tuple(out)


def solution(mesh):
    both = ("dp", "fsdp")
    seq, mat, vec = P(both, None, None), P(both, None), P(both)
    return jax.shard_map(
        functools.partial(shards, mesh),
        mesh=mesh,
        in_specs=(seq, vec) + ((mat,) + (vec,) * 6) * 2 + (seq,),
        out_specs=(seq, seq) + ((mat,) + (vec,) * 6) * 2,
        check_vma=False,
    )
```
